32 devices in a mesh: dp: 4 (over y, core), mp: 8 (over z, x).
Axes of the slice: x: 2, y: 2, z: 4, core: 2. Of those that a mesh axis runs over, the one named last changes fastest.
Arguments:
- pair_tokens: bfloat16 [64, 48, 8192], P('dp', None, 'mp'), may hold values from -6 to 6
- norm_gain: float32 [8192], replicated, may hold values from 0.1 to 1.9
- q_weight: bfloat16 [8192, 4096], P('dp', 'mp'), may hold values from -1.5 to 1.5
- k_weight: bfloat16 [8192, 1024], P('dp', 'mp'), may hold values from -1.5 to 1.5
- value_weight: bfloat16 [8192, 1024], P('dp', 'mp'), may hold values from -0.0625 to 0.0625
- o_weight: bfloat16 [4096, 8192], P('mp', 'dp'), may hold values from -0.375 to 0.375
- pair_row: int32 [64], replicated, may hold values from 0 to 15, as said below
- pair_span: int32 [64, 2], replicated, may hold values from 0 to 128, as said below
- block_ids: int32 [2048], P('dp'), may hold values from 0 to 11, as said below
Outputs:
- attn_out: bfloat16 [2048, 8192], P('dp', 'mp')
The draws below stay inside these ranges and needn't reach their ends.
Inputs may be any that keep to these rules, and one draw needn't show every extreme that they name: `pair_row`: every packed row is tiled exactly by the spans of the pairs that name it; the pairs listed on one index of dp that name rows of one index of dp number at most 4, and 4 is reached. `pair_span`: each span holds one pair, start before end; end - start is at least 3 and at most 48; 48 is reached in every row, and the last pair of every row ends at 128. `block_ids`: the pair's place counts the pairs of its row in order of position; roles are 0 prompt, 1 chosen, 2 rejected, in that order within each pair, each present; consistent with pair_row and pair_span.
All inputs are finite; a program needn't handle non-finite values.
Results may differ from the reference program's by a relative error of at most 0.013.
Values may be sent and summed in bfloat16 or wider, within the bound.
A program may use at most 128 MiB of HBM per device.

```python
import jax
import jax.numpy as jnp
from jax import lax

MODEL_WIDTH = 8192
QUERY_HEADS = 32
KEY_VALUE_HEADS = 8
HEAD_SIZE = 128
ROW_TOKENS = 128
PAIR_CAP = 48
PAIRS_ROW = 4
PACK_ROWS = 4
QUERY_PER_KV = 4
ROWS = 16
TOKENS = 2048
PAIRS_DEV = 16
NPAIRS = 64
N_DP = 4
N_MP = 8


def packing_layout(key):
    key_rows = jax.random.split(jax.random.fold_in(key, 7), 7)
    count = PAIRS_ROW
    rest = ROW_TOKENS - PAIR_CAP
    shortest = rest // 4
    spare = rest - (count - 1) * shortest
    cuts = jnp.sort(jax.random.randint(key_rows[0], (ROWS, count - 2), 0, spare + 1), axis=1)
    edges = jnp.concatenate([jnp.zeros((ROWS, 1), jnp.int32), cuts, jnp.full((ROWS, 1), spare, jnp.int32)], axis=1)
    others = edges[:, 1:] - edges[:, :-1] + shortest
    unordered = jnp.concatenate([jnp.full((ROWS, 1), PAIR_CAP, jnp.int32), others], axis=1)
    order_keys = jax.random.randint(key_rows[1], (ROWS, count), 0, 1 << 20) * count + jnp.arange(count)
    order = jnp.argsort(order_keys, axis=1)
    lengths = jnp.take_along_axis(unordered, order, axis=1)
    starts = jnp.cumsum(lengths, axis=1) - lengths
    prompt = 1 + jax.random.randint(key_rows[2], (ROWS, count), 0, lengths - 2)
    chosen = 1 + jax.random.randint(key_rows[3], (ROWS, count), 0, lengths - 1 - prompt)
    placing = jax.random.permutation(key_rows[4], N_DP)
    shift_all = jax.random.permutation(key_rows[5], N_DP)
    shifts = shift_all[jnp.arange(PAIRS_DEV) % N_DP]
    slot_keys = jax.random.randint(key_rows[6], (N_DP, PAIRS_DEV), 0, 1 << 20) * PAIRS_DEV + jnp.arange(PAIRS_DEV)[None, :]
    slot_of = jnp.argsort(slot_keys, axis=1)
    source = jnp.arange(NPAIRS) // PAIRS_DEV
    within_src = jnp.arange(NPAIRS) % PAIRS_DEV
    owner = (placing[source] + shifts[within_src]) % N_DP
    slot = slot_of[owner, within_src]
    row = owner * PACK_ROWS + slot // count
    place = slot % count
    return (row, starts, lengths, prompt, chosen, place)


def draw_pair_row(key, part):
    row, starts, lengths, prompt, chosen, place = packing_layout(key)
    return row.astype(jnp.int32)


def draw_pair_span(key, part):
    row, starts, lengths, prompt, chosen, place = packing_layout(key)
    first = starts[row, place]
    return jnp.stack([first, first + lengths[row, place]], axis=1).astype(jnp.int32)


def draw_block_ids(key, part):
    row, starts, lengths, prompt, chosen, place = packing_layout(key)
    steps_t = jnp.arange(ROW_TOKENS)
    which = jnp.sum((steps_t[None, :, None] >= starts[:, None, 1:]).astype(jnp.int32), axis=2)
    offset = steps_t[None, :] - jnp.take_along_axis(starts, which, axis=1)
    prompt_len = jnp.take_along_axis(prompt, which, axis=1)
    chosen_len = jnp.take_along_axis(chosen, which, axis=1)
    role = (offset >= prompt_len).astype(jnp.int32) + (offset >= prompt_len + chosen_len).astype(jnp.int32)
    return (3 * which + role).reshape(-1).astype(jnp.int32)


def projections(key):
    key_rows = jax.random.split(jax.random.fold_in(key, 11), 2)
    rotary_base = jnp.clip(jax.random.normal(key_rows[0], (MODEL_WIDTH, KEY_VALUE_HEADS * HEAD_SIZE), jnp.float32), -4.0, 4.0) * MODEL_WIDTH ** (-0.5)
    noise = jnp.clip(jax.random.normal(key_rows[1], (MODEL_WIDTH, QUERY_HEADS * HEAD_SIZE), jnp.float32), -4.0, 4.0) * MODEL_WIDTH ** (-0.5)
    return (rotary_base, noise)


def draw_k_weight(key, part):
    rotary_base, noise = projections(key)
    return rotary_base.astype(jnp.bfloat16)


def draw_q_weight(key, part):
    rotary_base, noise = projections(key)
    return noise.astype(jnp.bfloat16)


def block_scale(rng, shape, cuts, least, high):
    loudness = 1.0
    for dim, blocks in cuts:
        heights = jax.random.uniform(jax.random.fold_in(jax.random.fold_in(rng, 6), dim), (blocks,), jnp.float32, least / len(cuts), high / len(cuts))
        loudness = loudness * jnp.repeat(jnp.exp(heights), shape[dim] // blocks).reshape((-1,) + (1,) * (len(shape) - 1 - dim))
    return loudness


def normal_values(rng, extent, deviation, limit, pieces=(), kind=jnp.bfloat16):
    gain = block_scale(rng, extent, pieces, -0.22, 0.18) if pieces else 1.0
    values = jax.random.normal(rng, extent, jnp.float32) * deviation * gain
    return jnp.minimum(jnp.maximum(values, -limit), limit).astype(kind)


def setup_inputs(seed: int = 0) -> dict:
    key_of = jax.random.split(jax.random.key(seed), 10)
    return {
        "pair_tokens": normal_values(key_of[0], (NPAIRS, PAIR_CAP, MODEL_WIDTH), 1.0, 6.0, ((0, 4), (2, 8))),
        "norm_gain": jnp.clip(1.0 + 0.18 * jax.random.normal(key_of[1], (MODEL_WIDTH,), jnp.float32), 0.1, 1.9),
        "q_weight": draw_q_weight(jax.random.fold_in(key_of[9], 71), 0),
        "k_weight": draw_k_weight(jax.random.fold_in(key_of[9], 71), 0),
        "value_weight": normal_values(key_of[4], (MODEL_WIDTH, KEY_VALUE_HEADS * HEAD_SIZE), MODEL_WIDTH ** -0.5, 0.0625, ((0, 4), (1, 8))),
        "o_weight": normal_values(key_of[5], (QUERY_HEADS * HEAD_SIZE, MODEL_WIDTH), (QUERY_HEADS * HEAD_SIZE // 16) ** -0.5, 0.375, ((0, 8), (1, 4))),
        "pair_row": draw_pair_row(jax.random.fold_in(key_of[9], 71), 0),
        "pair_span": draw_pair_span(jax.random.fold_in(key_of[9], 71), 0),
        "block_ids": draw_block_ids(jax.random.fold_in(key_of[9], 71), 0),
    }


def apply_rotary(values, token_position, heads):
    half = HEAD_SIZE // 2
    freq = 500000.0 ** (-(jnp.arange(half, dtype=jnp.float32) * 2.0 / HEAD_SIZE))
    angle = token_position.astype(jnp.float32)[:, None] * freq[None, :]
    cosine = jnp.cos(angle)[:, None, :]
    sine = jnp.sin(angle)[:, None, :]
    shaped = values.reshape(values.shape[0], heads, HEAD_SIZE)
    first = shaped[..., :half]
    second = shaped[..., half:]
    turned = jnp.concatenate([first * cosine - second * sine, second * cosine + first * sine], axis=-1)
    return turned.reshape(values.shape[0], heads * HEAD_SIZE).astype(jnp.bfloat16)

def row_mask(ids):
    pair_of = ids // 3
    role_of = ids % 3
    steps_a = jnp.arange(ids.shape[0])
    causal = steps_a[None, :] <= steps_a[:, None]
    same = pair_of[:, None] == pair_of[None, :]
    hidden_pair = (role_of[:, None] == 2) & (role_of[None, :] == 1)
    return causal & same & jnp.logical_not(hidden_pair)

def reference(pair_tokens, norm_gain, q_weight, k_weight, value_weight, o_weight, pair_row, pair_span, block_ids):
    slots = jnp.arange(PAIR_CAP, dtype=jnp.int32)
    length = pair_span[:, 1] - pair_span[:, 0]
    target = pair_row[:, None] * ROW_TOKENS + pair_span[:, 0][:, None] + slots[None, :]
    target = jnp.where(slots[None, :] < length[:, None], target, TOKENS).astype(jnp.int32)
    packed = jnp.zeros((TOKENS, MODEL_WIDTH), jnp.bfloat16).at[target.reshape(-1)].set(pair_tokens.reshape(-1, MODEL_WIDTH), mode='drop')
    group_width = QUERY_HEADS * HEAD_SIZE // N_MP

    def one_row(inputs):
        row_tokens, ids = inputs
        visible = row_mask(ids)
        token_position = lax.optimization_barrier(jnp.sum(visible.astype(jnp.int32), axis=1)) - 1
        wide = row_tokens.astype(jnp.float32)
        scale = lax.rsqrt(lax.optimization_barrier(jnp.mean(wide * wide, axis=-1, keepdims=True)) + 1e-05)
        normed = (wide * scale * norm_gain[None, :]).astype(jnp.bfloat16)
        query_heads = jnp.dot(normed, q_weight, preferred_element_type=jnp.float32)
        key_rows = jnp.dot(normed, k_weight, preferred_element_type=jnp.float32)
        value_heads = jnp.dot(normed, value_weight, preferred_element_type=jnp.float32).astype(jnp.bfloat16)
        rotated_query = apply_rotary(query_heads, token_position, QUERY_HEADS).astype(jnp.float32).reshape(ROW_TOKENS, KEY_VALUE_HEADS, QUERY_PER_KV, HEAD_SIZE)
        rotated_key = apply_rotary(key_rows, token_position, KEY_VALUE_HEADS).astype(jnp.float32).reshape(ROW_TOKENS, KEY_VALUE_HEADS, HEAD_SIZE)
        value_expanded = value_heads.astype(jnp.float32).reshape(ROW_TOKENS, KEY_VALUE_HEADS, HEAD_SIZE)
        scores = jnp.einsum('ihgd,jhd->hgij', rotated_query, rotated_key) * HEAD_SIZE ** (-0.5)
        scores = jnp.where(visible[None, None], scores, -1e+30)
        top = lax.optimization_barrier(jnp.max(scores, axis=-1, keepdims=True))
        expo = jnp.exp(scores - top)
        probs = (expo / lax.optimization_barrier(jnp.sum(expo, axis=-1, keepdims=True))).astype(jnp.bfloat16)
        attn = jnp.einsum('hgij,jhd->ihgd', probs.astype(jnp.float32), value_expanded).astype(jnp.bfloat16)
        attn = attn.reshape(ROW_TOKENS, QUERY_HEADS * HEAD_SIZE)
        total = jnp.zeros((ROW_TOKENS, MODEL_WIDTH), jnp.float32)
        for group in range(N_MP):
            part = jnp.dot(attn[:, group * group_width:(group + 1) * group_width], o_weight[group * group_width:(group + 1) * group_width], preferred_element_type=jnp.float32).astype(jnp.bfloat16)
            part = lax.optimization_barrier(part)
            total = total + part.astype(jnp.float32)
        return total.astype(jnp.bfloat16)
    result = lax.map(one_row, (packed.reshape(ROWS, ROW_TOKENS, MODEL_WIDTH), block_ids.reshape(ROWS, ROW_TOKENS)))
    return result.reshape(TOKENS, MODEL_WIDTH)
```

```python
import functools

import jax
import jax.numpy as jnp
import numpy as np
from jax import lax
from jax.experimental import pallas as pl
from jax.experimental.pallas import tpu as pltpu
from jax.sharding import PartitionSpec as P

HEAD_SIZE = 128
ROW_TOKENS = 128
QUERY_PER_KV = 4
SLICES = 4
PARTS = 4
COLUMNS = 4
UNITS = 2
MESH = pl.DeviceIdType.MESH


def ring_member(place, count):
    place = lax.rem(place + 2 * count, count)
    return jnp.where(place < count // 2, 2 * place, 2 * (count - 1 - place) + 1)


def pieces_of_output(n_mp, width, chunk):
    if width != 2 * chunk:
        return 1
    order = list(range(0, n_mp, 2)) + list(range(1, n_mp, 2))[::-1]
    apart = all(order[p - 1] // 2 != order[(p + 1) % n_mp] // 2 for p in range(n_mp))
    return 2 if apart else 1


def kernel(
    n_dp, n_mp,
    row_ref, span_ref, tok_ref, gain_ref, q_ref, k_ref, v_ref, o_ref, ids_ref, freq_ref,
    out_ref,
    tokv, xout, xin, xg, wall, wo, acc, square, attn, sums, terms, cos_ref, sin_ref, vis_ref,
    put_ref, pick, first_of, length_of,
    own_sem, t_send, t_recv, w_send, w_recv, x_send, x_recv, s_send, s_recv,
):
    me_dp = lax.axis_index("dp")
    me_mp = lax.axis_index("mp")

    def place_of(g):
        return jnp.where(lax.rem(g, 2) == 0, g // 2, n_mp - 1 - g // 2)

    place = place_of(me_mp)
    sides = (ring_member(place + 1, n_mp), ring_member(place - 1, n_mp))
    groups = n_dp // 2
    core = lax.rem(me_dp, 2)
    group = me_dp // 2
    partner = me_dp + 1 - 2 * core
    others = [lax.rem(me_dp + 2 * j, n_dp) for j in range(1, groups)]
    tokens, chunk = out_ref.shape
    half = tokens // 2
    rows_dev = tokens // ROW_TOKENS
    pairs_dev, cap, _ = tok_ref.shape
    most = -(-pairs_dev // n_dp)
    slots = n_dp * most
    block = most * cap
    depth, q_width = q_ref.shape
    k_width = k_ref.shape[1]
    width = o_ref.shape[1]
    n_out = pieces_of_output(n_mp, width, chunk)
    slice_width = chunk // SLICES
    part_rows = depth // PARTS
    unit = chunk // UNITS
    column = chunk // COLUMNS
    out_column = width // n_out // COLUMNS
    base = 3 * PARTS
    kinds = base + n_out * COLUMNS
    last = n_mp - 1
    part_stage = [min(2, last), min(4, last), min(5, last), last]

    def token_slice(sub):
        return pl.ds(pl.multiple_of(sub * slice_width, 128), slice_width)

    own_tokens = pltpu.make_async_copy(tok_ref, tokv, own_sem.at[4])
    own_tokens.start()

    barrier = pltpu.get_barrier_semaphore()
    for side in sides:
        pl.semaphore_signal(barrier, inc=1, device_id={"mp": side}, device_id_type=MESH)
    for j in range(1, n_dp):
        peer = lax.rem(me_dp + j, n_dp)
        pl.semaphore_signal(barrier, inc=1, device_id={"dp": peer}, device_id_type=MESH)

    owner_list = [lax.div(row_ref[me_dp * pairs_dev + p], rows_dev) for p in range(pairs_dev)]
    slot_list = []
    for p in range(pairs_dev):
        rank = jnp.int32(0)
        for e in range(p):
            rank = rank + jnp.where(owner_list[e] == owner_list[p], 1, 0)
        slot_list.append(owner_list[p] * most + rank)
    for s in range(slots):
        index = jnp.int32(0)
        for p in range(1, pairs_dev):
            index = jnp.where(slot_list[p] == s, p, index)
        pick[s] = index

    pl.semaphore_wait(barrier, 2 + n_dp - 1)

    def token_rows(owner):
        return pl.ds(pl.multiple_of(owner * block, 16), block)

    def token_copy(j, sub, landing):
        peer = lax.rem(me_dp + j, n_dp)
        return pltpu.make_async_remote_copy(
            src_ref=xout.at[token_rows(peer), token_slice(sub)],
            dst_ref=xin.at[token_rows(landing), token_slice(sub)],
            send_sem=t_send.at[sub, j - 1],
            recv_sem=t_recv.at[sub, landing],
            device_id={"dp": peer},
            device_id_type=MESH,
        )

    def send_tokens(sub, carry):
        def arrange(s, c):
            rows = pl.ds(pl.multiple_of(s * cap, 16), cap)
            xout[rows, token_slice(sub)] = tokv[pick[s], :, token_slice(sub)]
            return c

        lax.fori_loop(0, slots, arrange, 0)
        for j in range(1, n_dp):
            token_copy(j, sub, me_dp).start()
        xin[token_rows(me_dp), token_slice(sub)] = xout[token_rows(me_dp), token_slice(sub)]
        return carry

    own_tokens.wait()
    lax.fori_loop(0, SLICES, send_tokens, 0)

    def hop_of(g):
        gap = lax.rem(place_of(g) - place + n_mp, n_mp)
        gap = jnp.where(gap == 0, n_mp, gap)
        return jnp.minimum(gap, jnp.where(gap == n_mp, n_mp, n_mp - gap))

    def out_columns(second, owner):
        if n_out == 1:
            return owner * 0
        later = (hop_of(2 * owner + 1) < hop_of(2 * owner)).astype(jnp.int32)
        return chunk * (1 - later if second else later)

    starts = (0, q_width, q_width + k_width)
    spans = (q_width, k_width, k_width)

    def part(kind, owner):
        if kind >= base:
            second, c = divmod(kind - base, COLUMNS)
            start = owner * width + out_columns(second, owner) + c * out_column
            return wo.at[:, pl.ds(pl.multiple_of(start, 128), out_column)]
        p, which = divmod(kind, 3)
        start = owner * depth + p * part_rows
        return wall.at[
            pl.ds(pl.multiple_of(start, 16), part_rows), pl.ds(starts[which], spans[which])
        ]

    def shard(kind):
        if kind >= base:
            second, c = divmod(kind - base, COLUMNS)
            start = out_columns(second, me_dp) + c * out_column
            return o_ref.at[:, pl.ds(pl.multiple_of(start, 128), out_column)]
        p, which = divmod(kind, 3)
        return (q_ref, k_ref, v_ref)[which].at[pl.ds(p * part_rows, part_rows), :]

    def weight_copy(kind, owner, source, target, slot, peer):
        return pltpu.make_async_remote_copy(
            src_ref=source,
            dst_ref=target,
            send_sem=w_send.at[kind, slot],
            recv_sem=w_recv.at[kind, owner],
            device_id={"dp": peer},
            device_id_type=MESH,
        )

    def held_copy(kind, owner, slot):
        return weight_copy(kind, owner, part(kind, owner), part(kind, owner), slot, partner)

    def send_away(kind):
        for j, peer in enumerate(others):
            weight_copy(kind, me_dp, shard(kind), part(kind, me_dp), 1 + j, peer).start()

    def send_partner(kind):
        weight_copy(kind, me_dp, shard(kind), part(kind, me_dp), 0, partner).start()

    owns = [
        pltpu.make_async_copy(
            (q_ref, k_ref, v_ref)[w],
            wall.at[
                pl.ds(pl.multiple_of(me_dp * depth, 16), depth), pl.ds(starts[w], spans[w])
            ],
            own_sem.at[w],
        )
        for w in range(3)
    ]
    owns.append(
        pltpu.make_async_copy(
            o_ref,
            wo.at[:, pl.ds(pl.multiple_of(me_dp * width, 128), width)],
            own_sem.at[3],
        )
    )

    for kind in range(base // 2):
        send_away(kind)
    for w in range(3):
        owns[w].start()
    for kind in range(base):
        send_partner(kind)

    def x_copy(step, way, sub):
        sign = -1 if way == 0 else 1
        chunk_of = ring_member(place + sign * step, n_mp)
        ref = xg.at[chunk_of, pl.ds(way * half, half), token_slice(sub)]
        return pltpu.make_async_remote_copy(
            src_ref=ref,
            dst_ref=ref,
            send_sem=x_send.at[way, sub, step],
            recv_sem=x_recv.at[way, sub, step],
            device_id={"mp": sides[way]},
            device_id_type=MESH,
        )

    def x_arrival(step, way, sub):
        sign = -1 if way == 0 else 1
        chunk_of = ring_member(place + sign * (step + 1), n_mp)
        ref = xg.at[chunk_of, pl.ds(way * half, half), token_slice(sub)]
        return pltpu.make_async_remote_copy(
            src_ref=ref,
            dst_ref=ref,
            send_sem=x_send.at[way, sub, step],
            recv_sem=x_recv.at[way, sub, step],
            device_id={"mp": sides[way]},
            device_id_type=MESH,
        )

    def find_places(j, carry):
        firsts = [jnp.int32(0)] * most
        lengths = [jnp.int32(0)] * most
        found = jnp.int32(0)
        for p in range(pairs_dev):
            i = j * pairs_dev + p
            row = row_ref[i]
            begin = span_ref[i, 0]
            end = span_ref[i, 1]
            first = lax.rem(row, rows_dev) * ROW_TOKENS + begin
            spot = jnp.where(lax.div(row, rows_dev) == me_dp, found, most)
            for k in range(most):
                firsts[k] = jnp.where(spot == k, first, firsts[k])
                lengths[k] = jnp.where(spot == k, end - begin, lengths[k])
            found = jnp.where(spot == most, found, found + 1)
        for k in range(most):
            first_of[j * most + k] = firsts[k]
            length_of[j * most + k] = lengths[k]
        return carry

    lax.fori_loop(0, n_dp, find_places, 0)
    lane = lax.broadcasted_iota(jnp.int32, (1, slots * cap), 1)
    target = jnp.full((1, slots * cap), tokens, jnp.int32)
    for s in range(slots):
        offset = lane - s * cap
        inside = (offset >= 0) & (offset < length_of[s])
        target = jnp.where(inside, offset + first_of[s], target)
    at = lax.broadcasted_iota(jnp.int32, (tokens, slots * cap), 0)
    put_ref[...] = jnp.where(at == target, 1.0, 0.0).astype(jnp.bfloat16)

    def tables(r, carry):
        rows = pl.ds(pl.multiple_of(r * ROW_TOKENS, ROW_TOKENS), ROW_TOKENS)
        ids_j = jnp.broadcast_to(ids_ref[pl.ds(r, 1), :], (ROW_TOKENS, ROW_TOKENS)).astype(
            jnp.float32
        )
        ids_i = jnp.transpose(ids_j)
        pair_i = jnp.floor((ids_i + 0.5) * (1.0 / 3.0))
        pair_j = jnp.floor((ids_j + 0.5) * (1.0 / 3.0))
        at_i = lax.broadcasted_iota(jnp.int32, (ROW_TOKENS, ROW_TOKENS), 0)
        at_j = lax.broadcasted_iota(jnp.int32, (ROW_TOKENS, ROW_TOKENS), 1)
        hidden = (ids_i - 3.0 * pair_i == 2.0) & (ids_j - 3.0 * pair_j == 1.0)
        seen = jnp.where((at_j <= at_i) & (pair_i == pair_j), 1.0, 0.0)
        seen = jnp.where(hidden, 0.0, seen)
        vis_ref[rows, :] = seen
        angle = (jnp.sum(seen, axis=1, keepdims=True) - 1.0) * freq_ref[...]
        lane_at = lax.broadcasted_iota(jnp.int32, (ROW_TOKENS, HEAD_SIZE), 1)
        sine = jnp.sin(angle)
        cos_ref[rows, :] = jnp.cos(angle)
        sin_ref[rows, :] = jnp.where(lane_at < HEAD_SIZE // 2, -sine, sine)
        return carry

    acc[...] = jnp.zeros_like(acc)
    square[...] = jnp.zeros_like(square)

    def ramp(sub, carry):
        for j in range(1, n_dp):
            token_copy(j, sub, lax.rem(me_dp + j, n_dp)).wait_recv()
        xg[me_mp, :, token_slice(sub)] = jnp.dot(
            put_ref[...], xin[:, token_slice(sub)], preferred_element_type=jnp.float32
        ).astype(jnp.bfloat16)
        for way in range(2):
            x_copy(0, way, sub).start()

        def forward(k, c):
            for way in range(2):
                x_arrival(k, way, sub - 1 - k).wait_recv()
                x_copy(k + 1, way, sub - 1 - k).start()
            return c

        lax.fori_loop(0, sub, forward, 0)
        lax.fori_loop(sub * rows_dev // SLICES, (sub + 1) * rows_dev // SLICES, tables, 0)
        return carry

    lax.fori_loop(0, SLICES, ramp, 0)

    for kind in range(base // 2, base):
        send_away(kind)
    owns[3].start()
    for w in range(3):
        owns[w].wait()
    for kind in range(base):
        held_copy(kind, partner, 0).wait_recv()

    def pass_part(p):
        for kind in range(3 * p, 3 * p + 3):
            for j in range(1, groups):
                owner = lax.rem(me_dp + n_dp - 2 * j, n_dp)
                held_copy(kind, owner, 0).wait_recv()
                held_copy(kind, owner, groups + j - 1).start()

    def rest_part(p):
        for kind in range(3 * p, 3 * p + 3):
            for i in range(1, groups):
                held_copy(kind, lax.rem(partner + 2 * i, n_dp), 0).wait_recv()

    second_own = (me_dp * width + out_columns(1, me_dp)) // chunk
    held = hop_of(second_own) == n_mp

    def send_second():
        for c in range(COLUMNS):
            send_away(base + COLUMNS + c)

    def project(way, g, u):
        halves = pl.ds(pl.multiple_of(way * half, 16), half)
        wide = xg[g, halves, pl.ds(pl.multiple_of(u * unit, 128), unit)].astype(jnp.float32)
        power = wide * wide
        total = power[:, 0:128]
        for i in range(1, unit // 128):
            total = total + power[:, i * 128:(i + 1) * 128]
        square[halves, :] += total
        start = g * chunk + u * unit
        scaled = (wide * gain_ref[:, pl.ds(pl.multiple_of(start, 128), unit)]).astype(jnp.bfloat16)
        acc[halves, :] += jnp.dot(
            scaled,
            wall[pl.ds(pl.multiple_of(start, 16), unit), :],
            preferred_element_type=jnp.float32,
        )

    def project_due(way, stage):
        def one(i, carry):
            hop = i // UNITS
            u = lax.rem(i, UNITS)
            g = ring_member(place + jnp.where(way == 0, -hop, hop), n_mp)
            start = g * chunk + u * unit
            owner = start // depth
            near = (owner // 2 == group) & ((start + unit - 1) // depth // 2 == group)
            if depth % unit == 0:
                needed = lax.rem(start + unit - 1, depth) // part_rows
            else:
                needed = PARTS - 1
            when = last
            for p in range(PARTS - 2, -1, -1):
                when = jnp.where(needed == p, part_stage[p], when)
            due = jnp.where(near, hop, jnp.maximum(hop, when))

            @pl.when(due == stage)
            def _():
                project(way, g, u)

            return carry

        lowest = jnp.where(stage >= part_stage[0], 0, stage)
        lax.fori_loop(lowest * UNITS, (stage + 1) * UNITS, one, 0)

    def stage_of(stage, carry):
        for p in range(PARTS):
            pl.when(stage == part_stage[p])(functools.partial(pass_part, p))

        def side(way, c):
            for i in range(SLICES // 2):
                sub = way * (SLICES // 2) + i
                for turn_way in range(2):

                    @pl.when((stage < last) & (stage + sub >= SLICES - 1))
                    def _():
                        x_arrival(stage, turn_way, sub).wait_recv()

                        @pl.when(stage < last - 1)
                        def _():
                            x_copy(stage + 1, turn_way, sub).start()

            for p in range(PARTS):
                pl.when((stage == part_stage[p]) & (way == 0))(functools.partial(rest_part, p))
            project_due(way, stage)
            return c

        lax.fori_loop(0, 2, side, 0)

        @pl.when(stage == 1)
        def _():
            for c in range(COLUMNS):
                send_away(base + c)

        @pl.when(stage == 2)
        def _():
            for kind in range(base, kinds):
                send_partner(kind)

        if n_out == 2:

            @pl.when((stage == 3) & jnp.logical_not(held))
            def _():
                send_second()

        return carry

    lax.fori_loop(0, n_mp, stage_of, 0)
    if n_out == 2:
        pl.when(held)(send_second)

    def turn(u, cosine, sine):
        return (u * cosine + pltpu.roll(u, HEAD_SIZE // 2, 1) * sine).astype(jnp.bfloat16)

    def attend(r, carry):
        rows = pl.ds(pl.multiple_of(r * ROW_TOKENS, ROW_TOKENS), ROW_TOKENS)
        power = jnp.sum(square[rows, :], axis=1, keepdims=True)
        scale = lax.rsqrt(power / (n_mp * chunk) + 1e-05)
        cosine = cos_ref[rows, :] * scale
        sine = sin_ref[rows, :] * scale
        seen = vis_ref[rows, :] > 0.5
        for kv in range(k_width // HEAD_SIZE):
            at_k = q_width + kv * HEAD_SIZE
            key = turn(acc[rows, at_k:at_k + HEAD_SIZE], cosine, sine)
            at_v = at_k + k_width
            value = (acc[rows, at_v:at_v + HEAD_SIZE] * scale).astype(jnp.bfloat16)
            heads = range(kv * QUERY_PER_KV, (kv + 1) * QUERY_PER_KV)
            queries = jnp.concatenate(
                [turn(acc[rows, h * HEAD_SIZE:(h + 1) * HEAD_SIZE], cosine, sine) for h in heads],
                axis=0,
            )
            scores = lax.dot_general(
                queries, key, (((1,), (1,)), ((), ())), preferred_element_type=jnp.float32
            ) * HEAD_SIZE ** (-0.5)
            probs = []
            for i in range(QUERY_PER_KV):
                own = scores[i * ROW_TOKENS:(i + 1) * ROW_TOKENS, :]
                own = jnp.where(seen, own, -1e30)
                expo = jnp.exp(own - jnp.max(own, axis=-1, keepdims=True))
                probs.append(
                    (expo / jnp.sum(expo, axis=-1, keepdims=True)).astype(jnp.bfloat16)
                )
            mixed = jnp.dot(
                jnp.concatenate(probs, axis=0), value, preferred_element_type=jnp.float32
            ).astype(jnp.bfloat16)
            for i, h in enumerate(heads):
                attn[rows, h * HEAD_SIZE:(h + 1) * HEAD_SIZE] = mixed[
                    i * ROW_TOKENS:(i + 1) * ROW_TOKENS, :
                ]
        return carry

    lax.fori_loop(0, tokens // ROW_TOKENS, attend, 0)
    owns[3].wait()

    if n_out == 1:
        for kind in range(base, kinds):
            for j in range(1, groups):
                owner = lax.rem(me_dp + n_dp - 2 * j, n_dp)
                held_copy(kind, owner, 0).wait_recv()
                held_copy(kind, owner, groups + j - 1).start()
            for i in range(groups):
                held_copy(kind, lax.rem(partner + 2 * i, n_dp), 0).wait_recv()

    def out_weights(g, c):
        return pl.ds(pl.multiple_of(g * chunk + c * column, 128), column)

    def need(g, c, way, hop):
        owner = g * chunk // width
        early = chunk * (hop_of(2 * owner + 1) < hop_of(2 * owner)).astype(jnp.int32)
        second = jnp.where(g * chunk - owner * width == early, 0, 1)
        kind = base + second * COLUMNS + c
        fresh = hop == hop_of(g)
        if way == 1:
            fresh = fresh & (2 * hop != n_mp) & (hop != n_mp)
        ref = wo.at[:, out_weights(g, c)]
        away = owner // 2 != group

        @pl.when(fresh & (lax.rem(owner, 2) == core) & away)
        def _():
            j = lax.rem(group - owner // 2 + groups, groups)
            weight_copy(kind, owner, ref, ref, 0, partner).wait_recv()
            weight_copy(kind, owner, ref, ref, groups + j - 1, partner).start()

        @pl.when(fresh & (lax.rem(owner, 2) != core))
        def _():
            weight_copy(kind, owner, ref, ref, 0, partner).wait_recv()

    def sum_copy(slot, way, c):
        cols = pl.ds(pl.multiple_of(c * column, 128), column)
        return pltpu.make_async_remote_copy(
            src_ref=sums.at[way, slot, :, cols],
            dst_ref=sums.at[way, slot + 1, :, cols],
            send_sem=s_send.at[way, c, slot],
            recv_sem=s_recv.at[way, c, slot],
            device_id={"mp": sides[way]},
            device_id_type=MESH,
        )

    def scatter(i, carry):
        hop = i // COLUMNS + 1
        c = lax.rem(i, COLUMNS)
        cols = pl.ds(pl.multiple_of(c * column, 128), column)
        for way in range(2):
            g = ring_member(place + (-hop if way == 0 else hop), n_mp)
            if n_out == 2:
                need(g, c, way, hop)
            terms[way] = jnp.dot(
                attn[way * half:(way + 1) * half, :],
                wo[:, out_weights(g, c)],
                preferred_element_type=jnp.float32,
            )
        for way in range(2):

            @pl.when(hop == 1)
            def _():
                sums[way, 0, :, cols] = terms[way].astype(jnp.bfloat16)

            @pl.when(hop > 1)
            def _():
                sum_copy(hop - 2, way, c).wait_recv()
                total = sums[way, hop - 1, :, cols].astype(jnp.float32) + terms[way]
                total = total.astype(jnp.bfloat16)

                @pl.when(hop < n_mp)
                def _():
                    sums[way, hop - 1, :, cols] = total

                @pl.when(hop == n_mp)
                def _():
                    out_ref[way * half:(way + 1) * half, cols] = total

            @pl.when(hop < n_mp)
            def _():
                sum_copy(hop - 1, way, c).start()

        return carry

    lax.fori_loop(0, n_mp * COLUMNS, scatter, 0)

    def drain(step, carry):
        for way in range(2):
            for sub in range(SLICES):
                x_copy(step, way, sub).wait_send()
            for c in range(COLUMNS):
                sum_copy(step, way, c).wait_send()
        return carry

    lax.fori_loop(0, n_mp - 1, drain, 0)
    for sub in range(SLICES):
        for j in range(1, n_dp):
            token_copy(j, sub, me_dp).wait_send()
    for kind in range(kinds):
        for i in range(2 * groups - 1):
            weight_copy(kind, me_dp, shard(kind), part(kind, me_dp), i, partner).wait_send()


def local(
    pair_tokens,
    norm_gain,
    q_weight,
    k_weight,
    value_weight,
    o_weight,
    pair_row,
    pair_span,
    block_ids,
):
    dp_count = lax.axis_size("dp")
    mp_count = lax.axis_size("mp")
    pairs_dev, pair_cap, width_local = pair_tokens.shape
    slots = dp_count * (-(-pairs_dev // dp_count))
    tok_dev = block_ids.shape[0]
    half = HEAD_SIZE // 2
    freq = 500000.0 ** (-(np.arange(half, dtype=np.float32) * 2.0 / HEAD_SIZE))
    freq = np.concatenate([freq, freq])[None, :].astype(np.float32)

    q_width = q_weight.shape[1]
    k_width = k_weight.shape[1]
    width = norm_gain.shape[0]
    n_out = pieces_of_output(mp_count, o_weight.shape[1], width_local)
    kinds = 3 * PARTS + n_out * COLUMNS
    far = dp_count - 1
    vmem = pl.BlockSpec(memory_space=pltpu.VMEM)
    smem = pl.BlockSpec(memory_space=pltpu.SMEM)
    anyspace = pl.BlockSpec(memory_space=pl.ANY)
    bf16 = jnp.bfloat16
    return pl.pallas_call(
        functools.partial(kernel, dp_count, mp_count),
        out_shape=jax.ShapeDtypeStruct((tok_dev, width_local), bf16),
        in_specs=[
            smem, smem, anyspace, vmem, anyspace, anyspace, anyspace, anyspace, vmem, vmem
        ],
        out_specs=vmem,
        scratch_shapes=[
            pltpu.VMEM((pairs_dev, pair_cap, width_local), bf16),
            pltpu.VMEM((slots * pair_cap, width_local), bf16),
            pltpu.VMEM((slots * pair_cap, width_local), bf16),
            pltpu.VMEM((mp_count, tok_dev, width_local), bf16),
            pltpu.VMEM((width, q_width + 2 * k_width), bf16),
            pltpu.VMEM((o_weight.shape[0], width), bf16),
            pltpu.VMEM((tok_dev, q_width + 2 * k_width), jnp.float32),
            pltpu.VMEM((tok_dev, 128), jnp.float32),
            pltpu.VMEM((tok_dev, q_width), bf16),
            pltpu.VMEM((2, mp_count, tok_dev // 2, width_local), bf16),
            pltpu.VMEM((2, tok_dev // 2, width_local // COLUMNS), jnp.float32),
            pltpu.VMEM((tok_dev, HEAD_SIZE), jnp.float32),
            pltpu.VMEM((tok_dev, HEAD_SIZE), jnp.float32),
            pltpu.VMEM((tok_dev, ROW_TOKENS), jnp.float32),
            pltpu.VMEM((tok_dev, slots * pair_cap), bf16),
            pltpu.SMEM((slots,), jnp.int32),
            pltpu.SMEM((slots,), jnp.int32),
            pltpu.SMEM((slots,), jnp.int32),
            pltpu.SemaphoreType.DMA((5,)),
            pltpu.SemaphoreType.DMA((SLICES, far)),
            pltpu.SemaphoreType.DMA((SLICES, dp_count)),
            pltpu.SemaphoreType.DMA((kinds, far)),
            pltpu.SemaphoreType.DMA((kinds, dp_count)),
            pltpu.SemaphoreType.DMA((2, SLICES, mp_count - 1)),
            pltpu.SemaphoreType.DMA((2, SLICES, mp_count - 1)),
            pltpu.SemaphoreType.DMA((2, COLUMNS, mp_count - 1)),
            pltpu.SemaphoreType.DMA((2, COLUMNS, mp_count - 1)),
        ],
        compiler_params=pltpu.CompilerParams(
            collective_id=0, has_side_effects=True, vmem_limit_bytes=60 * 1024 * 1024
        ),
    )(
        pair_row,
        pair_span,
        pair_tokens,
        norm_gain[None, :],
        q_weight,
        k_weight,
        value_weight,
        o_weight,
        block_ids.reshape(tok_dev // ROW_TOKENS, ROW_TOKENS),
        jnp.asarray(freq),
    )


def solution(mesh):
    placed = (
        P("dp", None, "mp"),
        P(),
        P("dp", "mp"),
        P("dp", "mp"),
        P("dp", "mp"),
        P("mp", "dp"),
        P(),
        P(),
        P("dp"),
    )
    return jax.shard_map(
        local, mesh=mesh, in_specs=placed, out_specs=P("dp", "mp"), check_vma=False
    )
```

```python
import functools

import jax
import jax.numpy as jnp
import numpy as np
from jax import lax
from jax.experimental import pallas as pl
from jax.experimental.pallas import tpu as pltpu
from jax.sharding import PartitionSpec as P

HEAD_SIZE = 128
ROW_TOKENS = 128
QUERY_PER_KV = 4
SLICES = 4
PARTS = 4
COLUMNS = 4
UNITS = 2
MESH = pl.DeviceIdType.MESH


def ring_member(place, count):
    place = lax.rem(place + 2 * count, count)
    return jnp.where(place < count // 2, 2 * place, 2 * (count - 1 - place) + 1)


def pairs_up(n_dp, n_mp, width, chunk):
    return n_dp // 2 == 2 and n_mp == 2 * n_dp and width == 2 * chunk


def line_plan(length, group, at):
    near = (2 * group, 2 * group + 1)
    rising = list(range(length - 1, 0, -1))
    if 1 in near:
        rising = [1] + rising[:-1]
    falling = list(range(length - 1))
    if length - 2 in near:
        falling = [length - 2] + falling[:-1]
    units = [(rising.index(z), 0, z) for z in range(at + 1, length)]
    units = sorted(units + [(falling.index(z), 1, z) for z in range(at)])
    ties = [i for i in range(length - 2) if units[i][0] == units[i + 1][0]]
    return [u[1] for u in units], [u[2] for u in units], (ties + [length])[0]


def kernel(
    n_dp, n_mp,
    row_ref, span_ref, tok_ref, gain_ref, q_ref, k_ref, v_ref, o_ref, ids_ref, freq_ref,
    out_ref,
    tokv, xout, xin, xg, wall, wo, acc, square, attn, sums, terms, cos_ref, sin_ref, vis_ref,
    put_ref, pick, first_of, length_of,
    own_sem, t_send, t_recv, w_send, w_recv, x_send, x_recv, s_send, s_recv,
    b_send, b_recv, a_send, a_recv,
):
    me_dp = lax.axis_index("dp")
    me_mp = lax.axis_index("mp")

    def place_of(g):
        return jnp.where(lax.rem(g, 2) == 0, g // 2, n_mp - 1 - g // 2)

    place = place_of(me_mp)
    sides = (ring_member(place + 1, n_mp), ring_member(place - 1, n_mp))
    groups = n_dp // 2
    core = lax.rem(me_dp, 2)
    group = me_dp // 2
    partner = me_dp + 1 - 2 * core
    others = [lax.rem(me_dp + 2 * j, n_dp) for j in range(1, groups)]
    tokens, chunk = out_ref.shape
    half = tokens // 2
    rows_dev = tokens // ROW_TOKENS
    pairs_dev, cap, _ = tok_ref.shape
    most = -(-pairs_dev // n_dp)
    slots = n_dp * most
    block = most * cap
    depth, q_width = q_ref.shape
    k_width = k_ref.shape[1]
    width = o_ref.shape[1]
    paired = pairs_up(n_dp, n_mp, width, chunk)
    slice_width = chunk // SLICES
    part_rows = depth // PARTS
    unit = chunk // UNITS
    column = chunk // COLUMNS
    out_column = width // COLUMNS
    base = 3 * PARTS
    kinds = base + (3 if paired else COLUMNS)
    out_rows = o_ref.shape[0]
    wide_half = chunk // 2
    line = n_mp // 2
    at_z = me_mp // 2
    at_x = lax.rem(me_mp, 2)
    mate = me_mp + 1 - 2 * at_x
    inner = (at_z > 0) & (at_z < line - 1)
    lead = jnp.where(at_z == 0, 1, jnp.where(at_z == line - 1, 0, group))
    urgent = core == lead
    last = n_mp - 1
    part_stage = [min(2, last), min(4, last), min(5, last), last]

    def token_slice(sub):
        return pl.ds(pl.multiple_of(sub * slice_width, 128), slice_width)

    own_tokens = pltpu.make_async_copy(tok_ref, tokv, own_sem.at[4])
    own_tokens.start()

    barrier = pltpu.get_barrier_semaphore()
    for side in sides:
        pl.semaphore_signal(barrier, inc=1, device_id={"mp": side}, device_id_type=MESH)
    for j in range(1, n_dp):
        peer = lax.rem(me_dp + j, n_dp)
        pl.semaphore_signal(barrier, inc=1, device_id={"dp": peer}, device_id_type=MESH)

    greeted = 2 + n_dp - 1
    if paired:
        pl.semaphore_signal(barrier, inc=1, device_id={"mp": mate}, device_id_type=MESH)

        @pl.when(at_z < line - 1)
        def _():
            above = jnp.minimum(me_mp + 2, n_mp - 1)
            pl.semaphore_signal(barrier, inc=1, device_id={"mp": above}, device_id_type=MESH)

        @pl.when(at_z > 0)
        def _():
            below = jnp.maximum(me_mp - 2, 0)
            pl.semaphore_signal(barrier, inc=1, device_id={"mp": below}, device_id_type=MESH)

        greeted = greeted + 1 + jnp.where(at_z < line - 1, 1, 0) + jnp.where(at_z > 0, 1, 0)

    owner_list = [lax.div(row_ref[me_dp * pairs_dev + p], rows_dev) for p in range(pairs_dev)]
    slot_list = []
    for p in range(pairs_dev):
        rank = jnp.int32(0)
        for e in range(p):
            rank = rank + jnp.where(owner_list[e] == owner_list[p], 1, 0)
        slot_list.append(owner_list[p] * most + rank)
    for s in range(slots):
        index = jnp.int32(0)
        for p in range(1, pairs_dev):
            index = jnp.where(slot_list[p] == s, p, index)
        pick[s] = index

    pl.semaphore_wait(barrier, greeted)

    def token_rows(owner):
        return pl.ds(pl.multiple_of(owner * block, 16), block)

    def token_copy(j, sub, landing):
        peer = lax.rem(me_dp + j, n_dp)
        return pltpu.make_async_remote_copy(
            src_ref=xout.at[token_rows(peer), token_slice(sub)],
            dst_ref=xin.at[token_rows(landing), token_slice(sub)],
            send_sem=t_send.at[sub, j - 1],
            recv_sem=t_recv.at[sub, landing],
            device_id={"dp": peer},
            device_id_type=MESH,
        )

    def send_tokens(sub, carry):
        def arrange(s, c):
            rows = pl.ds(pl.multiple_of(s * cap, 16), cap)
            xout[rows, token_slice(sub)] = tokv[pick[s], :, token_slice(sub)]
            return c

        lax.fori_loop(0, slots, arrange, 0)
        for j in range(1, n_dp):
            token_copy(j, sub, me_dp).start()
        xin[token_rows(me_dp), token_slice(sub)] = xout[token_rows(me_dp), token_slice(sub)]
        return carry

    own_tokens.wait()
    lax.fori_loop(0, SLICES, send_tokens, 0)

    starts = (0, q_width, q_width + k_width)
    spans = (q_width, k_width, k_width)

    def pair_part(piece, owner):
        side = at_x if piece == 0 else 1 - at_x
        start = owner * chunk + max(piece - 1, 0) * wide_half
        return wo.at[
            pl.ds(pl.multiple_of(side * out_rows, 16), out_rows),
            pl.ds(pl.multiple_of(start, 128), chunk if piece == 0 else wide_half),
        ]

    def part(kind, owner):
        if kind >= base and paired:
            return pair_part(kind - base, owner)
        if kind >= base:
            start = owner * width + (kind - base) * out_column
            return wo.at[:, pl.ds(pl.multiple_of(start, 128), out_column)]
        p, which = divmod(kind, 3)
        start = owner * depth + p * part_rows
        return wall.at[
            pl.ds(pl.multiple_of(start, 16), part_rows), pl.ds(starts[which], spans[which])
        ]

    def shard(kind):
        if kind >= base and paired:
            if kind > base:
                return pair_part(kind - base, me_dp)
            return o_ref.at[:, pl.ds(pl.multiple_of(at_x * chunk, 128), chunk)]
        if kind >= base:
            return o_ref.at[:, pl.ds((kind - base) * out_column, out_column)]
        p, which = divmod(kind, 3)
        return (q_ref, k_ref, v_ref)[which].at[pl.ds(p * part_rows, part_rows), :]

    def weight_copy(kind, owner, source, target, slot, peer):
        return pltpu.make_async_remote_copy(
            src_ref=source,
            dst_ref=target,
            send_sem=w_send.at[kind, slot],
            recv_sem=w_recv.at[kind, owner],
            device_id={"dp": peer},
            device_id_type=MESH,
        )

    def held_copy(kind, owner, slot):
        return weight_copy(kind, owner, part(kind, owner), part(kind, owner), slot, partner)

    def send_away(kind):
        for j, peer in enumerate(others):
            weight_copy(kind, me_dp, shard(kind), part(kind, me_dp), 1 + j, peer).start()

    def send_partner(kind):
        weight_copy(kind, me_dp, shard(kind), part(kind, me_dp), 0, partner).start()

    owns = [
        pltpu.make_async_copy(
            (q_ref, k_ref, v_ref)[w],
            wall.at[
                pl.ds(pl.multiple_of(me_dp * depth, 16), depth), pl.ds(starts[w], spans[w])
            ],
            own_sem.at[w],
        )
        for w in range(3)
    ]
    if paired:
        owns.append(pltpu.make_async_copy(shard(base), part(base, me_dp), own_sem.at[3]))
    else:
        owns.append(
            pltpu.make_async_copy(
                o_ref,
                wo.at[:, pl.ds(pl.multiple_of(me_dp * width, 128), width)],
                own_sem.at[3],
            )
        )

    def mate_copy(h, side):
        start = me_dp * chunk + h * wide_half
        taken = (1 - at_x) * chunk + h * wide_half
        return pltpu.make_async_remote_copy(
            src_ref=o_ref.at[:, pl.ds(pl.multiple_of(taken, 128), wide_half)],
            dst_ref=wo.at[
                pl.ds(pl.multiple_of(side * out_rows, 16), out_rows),
                pl.ds(pl.multiple_of(start, 128), wide_half),
            ],
            send_sem=b_send.at[h],
            recv_sem=b_recv.at[h],
            device_id={"mp": mate},
            device_id_type=MESH,
        )

    def mate_arrived():
        for h in range(2):
            mate_copy(h, 1 - at_x).wait_recv()
            send_partner(base + 1 + h)

    def mate_away():
        for h in range(2):
            send_away(base + 1 + h)

    if paired:
        pl.when(inner | urgent)(mate_copy(0, at_x).start)
        pl.when(inner)(mate_copy(1, at_x).start)

    for kind in range(base // 2):
        send_away(kind)
    for w in range(3):
        owns[w].start()
    for kind in range(base):
        send_partner(kind)

    def x_copy(step, way, sub):
        sign = -1 if way == 0 else 1
        chunk_of = ring_member(place + sign * step, n_mp)
        ref = xg.at[chunk_of, pl.ds(way * half, half), token_slice(sub)]
        return pltpu.make_async_remote_copy(
            src_ref=ref,
            dst_ref=ref,
            send_sem=x_send.at[way, sub, step],
            recv_sem=x_recv.at[way, sub, step],
            device_id={"mp": sides[way]},
            device_id_type=MESH,
        )

    def x_arrival(step, way, sub):
        sign = -1 if way == 0 else 1
        chunk_of = ring_member(place + sign * (step + 1), n_mp)
        ref = xg.at[chunk_of, pl.ds(way * half, half), token_slice(sub)]
        return pltpu.make_async_remote_copy(
            src_ref=ref,
            dst_ref=ref,
            send_sem=x_send.at[way, sub, step],
            recv_sem=x_recv.at[way, sub, step],
            device_id={"mp": sides[way]},
            device_id_type=MESH,
        )

    def find_places(j, carry):
        firsts = [jnp.int32(0)] * most
        lengths = [jnp.int32(0)] * most
        found = jnp.int32(0)
        for p in range(pairs_dev):
            i = j * pairs_dev + p
            row = row_ref[i]
            begin = span_ref[0, i]
            end = span_ref[1, i]
            first = lax.rem(row, rows_dev) * ROW_TOKENS + begin
            spot = jnp.where(lax.div(row, rows_dev) == me_dp, found, most)
            for k in range(most):
                firsts[k] = jnp.where(spot == k, first, firsts[k])
                lengths[k] = jnp.where(spot == k, end - begin, lengths[k])
            found = jnp.where(spot == most, found, found + 1)
        for k in range(most):
            first_of[j * most + k] = firsts[k]
            length_of[j * most + k] = lengths[k]
        return carry

    lax.fori_loop(0, n_dp, find_places, 0)
    lane = lax.broadcasted_iota(jnp.int32, (1, slots * cap), 1)
    target = jnp.full((1, slots * cap), tokens, jnp.int32)
    for s in range(slots):
        offset = lane - s * cap
        inside = (offset >= 0) & (offset < length_of[s])
        target = jnp.where(inside, offset + first_of[s], target)
    at = lax.broadcasted_iota(jnp.int32, (tokens, slots * cap), 0)
    put_ref[...] = jnp.where(at == target, 1.0, 0.0).astype(jnp.bfloat16)

    def tables(r, carry):
        rows = pl.ds(pl.multiple_of(r * ROW_TOKENS, ROW_TOKENS), ROW_TOKENS)
        ids_j = jnp.broadcast_to(ids_ref[pl.ds(r, 1), :], (ROW_TOKENS, ROW_TOKENS)).astype(
            jnp.float32
        )
        ids_i = jnp.transpose(ids_j)
        pair_i = jnp.floor((ids_i + 0.5) * (1.0 / 3.0))
        pair_j = jnp.floor((ids_j + 0.5) * (1.0 / 3.0))
        at_i = lax.broadcasted_iota(jnp.int32, (ROW_TOKENS, ROW_TOKENS), 0)
        at_j = lax.broadcasted_iota(jnp.int32, (ROW_TOKENS, ROW_TOKENS), 1)
        hidden = (ids_i - 3.0 * pair_i == 2.0) & (ids_j - 3.0 * pair_j == 1.0)
        seen = jnp.where((at_j <= at_i) & (pair_i == pair_j), 1.0, 0.0)
        seen = jnp.where(hidden, 0.0, seen)
        vis_ref[rows, :] = seen
        angle = (jnp.sum(seen, axis=1, keepdims=True) - 1.0) * freq_ref[...]
        lane_at = lax.broadcasted_iota(jnp.int32, (ROW_TOKENS, HEAD_SIZE), 1)
        sine = jnp.sin(angle)
        cos_ref[rows, :] = jnp.cos(angle)
        sin_ref[rows, :] = jnp.where(lane_at < HEAD_SIZE // 2, -sine, sine)
        return carry

    acc[...] = jnp.zeros_like(acc)
    square[...] = jnp.zeros_like(square)

    def ramp(sub, carry):
        for j in range(1, n_dp):
            token_copy(j, sub, lax.rem(me_dp + j, n_dp)).wait_recv()
        xg[me_mp, :, token_slice(sub)] = jnp.dot(
            put_ref[...], xin[:, token_slice(sub)], preferred_element_type=jnp.float32
        ).astype(jnp.bfloat16)
        for way in range(2):
            x_copy(0, way, sub).start()

        def forward(k, c):
            for way in range(2):
                x_arrival(k, way, sub - 1 - k).wait_recv()
                x_copy(k + 1, way, sub - 1 - k).start()
            return c

        lax.fori_loop(0, sub, forward, 0)
        lax.fori_loop(sub * rows_dev // SLICES, (sub + 1) * rows_dev // SLICES, tables, 0)
        return carry

    lax.fori_loop(0, SLICES, ramp, 0)

    for kind in range(base // 2, base):
        send_away(kind)
    owns[3].start()
    for w in range(3):
        owns[w].wait()
    for kind in range(base):
        held_copy(kind, partner, 0).wait_recv()

    def pass_part(p):
        for kind in range(3 * p, 3 * p + 3):
            for j in range(1, groups):
                owner = lax.rem(me_dp + n_dp - 2 * j, n_dp)
                held_copy(kind, owner, 0).wait_recv()
                held_copy(kind, owner, groups + j - 1).start()

    def rest_part(p):
        for kind in range(3 * p, 3 * p + 3):
            for i in range(1, groups):
                held_copy(kind, lax.rem(partner + 2 * i, n_dp), 0).wait_recv()

    def project(way, g, u):
        halves = pl.ds(pl.multiple_of(way * half, 16), half)
        wide = xg[g, halves, pl.ds(pl.multiple_of(u * unit, 128), unit)].astype(jnp.float32)
        power = wide * wide
        total = power[:, 0:128]
        for i in range(1, unit // 128):
            total = total + power[:, i * 128:(i + 1) * 128]
        square[halves, :] += total
        start = g * chunk + u * unit
        scaled = (wide * gain_ref[:, pl.ds(pl.multiple_of(start, 128), unit)]).astype(jnp.bfloat16)
        acc[halves, :] += jnp.dot(
            scaled,
            wall[pl.ds(pl.multiple_of(start, 16), unit), :],
            preferred_element_type=jnp.float32,
        )

    def project_due(way, stage):
        def one(i, carry):
            hop = i // UNITS
            u = lax.rem(i, UNITS)
            g = ring_member(place + jnp.where(way == 0, -hop, hop), n_mp)
            start = g * chunk + u * unit
            owner = start // depth
            near = (owner // 2 == group) & ((start + unit - 1) // depth // 2 == group)
            if depth % unit == 0:
                needed = lax.rem(start + unit - 1, depth) // part_rows
            else:
                needed = PARTS - 1
            when = last
            for p in range(PARTS - 2, -1, -1):
                when = jnp.where(needed == p, part_stage[p], when)
            due = jnp.where(near, hop, jnp.maximum(hop, when))

            @pl.when(due == stage)
            def _():
                project(way, g, u)

            return carry

        lowest = jnp.where(stage >= part_stage[0], 0, stage)
        lax.fori_loop(lowest * UNITS, (stage + 1) * UNITS, one, 0)

    def stage_of(stage, carry):
        for p in range(PARTS):
            pl.when(stage == part_stage[p])(functools.partial(pass_part, p))

        def side(way, c):
            for i in range(SLICES // 2):
                sub = way * (SLICES // 2) + i
                for turn_way in range(2):

                    @pl.when((stage < last) & (stage + sub >= SLICES - 1))
                    def _():
                        x_arrival(stage, turn_way, sub).wait_recv()

                        @pl.when(stage < last - 1)
                        def _():
                            x_copy(stage + 1, turn_way, sub).start()

            for p in range(PARTS):
                pl.when((stage == part_stage[p]) & (way == 0))(functools.partial(rest_part, p))
            project_due(way, stage)
            return c

        lax.fori_loop(0, 2, side, 0)

        if paired:

            @pl.when((stage == 1) & urgent)
            def _():
                send_away(base)

            @pl.when(stage == 2)
            def _():
                send_partner(base)

            @pl.when((stage == min(3, last)) & inner)
            def _():
                mate_arrived()
                pl.when(urgent)(mate_away)

        else:

            @pl.when(stage == min(1, last))
            def _():
                for kind in range(base, kinds):
                    send_away(kind)
                    send_partner(kind)

        return carry

    lax.fori_loop(0, n_mp, stage_of, 0)
    if paired:
        pl.when(jnp.logical_not(inner) & urgent)(mate_copy(1, at_x).start)

    def turn(u, cosine, sine):
        return (u * cosine + pltpu.roll(u, HEAD_SIZE // 2, 1) * sine).astype(jnp.bfloat16)

    def share(r, side):
        ref = attn.at[
            pl.ds(pl.multiple_of(r * ROW_TOKENS, ROW_TOKENS), ROW_TOKENS),
            pl.ds(pl.multiple_of(side * q_width, 128), q_width),
        ]
        return pltpu.make_async_remote_copy(
            src_ref=ref,
            dst_ref=ref,
            send_sem=a_send.at[r],
            recv_sem=a_recv.at[r],
            device_id={"mp": mate},
            device_id_type=MESH,
        )

    def attend(r, carry):
        rows = pl.ds(pl.multiple_of(r * ROW_TOKENS, ROW_TOKENS), ROW_TOKENS)
        power = jnp.sum(square[rows, :], axis=1, keepdims=True)
        scale = lax.rsqrt(power / (n_mp * chunk) + 1e-05)
        cosine = cos_ref[rows, :] * scale
        sine = sin_ref[rows, :] * scale
        seen = vis_ref[rows, :] > 0.5
        left = at_x * q_width if paired else 0
        for kv in range(k_width // HEAD_SIZE):
            at_k = q_width + kv * HEAD_SIZE
            key = turn(acc[rows, at_k:at_k + HEAD_SIZE], cosine, sine)
            at_v = at_k + k_width
            value = (acc[rows, at_v:at_v + HEAD_SIZE] * scale).astype(jnp.bfloat16)
            heads = range(kv * QUERY_PER_KV, (kv + 1) * QUERY_PER_KV)
            queries = jnp.concatenate(
                [turn(acc[rows, h * HEAD_SIZE:(h + 1) * HEAD_SIZE], cosine, sine) for h in heads],
                axis=0,
            )
            scores = lax.dot_general(
                queries, key, (((1,), (1,)), ((), ())), preferred_element_type=jnp.float32
            ) * HEAD_SIZE ** (-0.5)
            probs = []
            for i in range(QUERY_PER_KV):
                own = scores[i * ROW_TOKENS:(i + 1) * ROW_TOKENS, :]
                own = jnp.where(seen, own, -1e30)
                expo = jnp.exp(own - jnp.max(own, axis=-1, keepdims=True))
                probs.append(
                    (expo / jnp.sum(expo, axis=-1, keepdims=True)).astype(jnp.bfloat16)
                )
            mixed = jnp.dot(
                jnp.concatenate(probs, axis=0), value, preferred_element_type=jnp.float32
            ).astype(jnp.bfloat16)
            for i, h in enumerate(heads):
                spot = pl.ds(pl.multiple_of(left + h * HEAD_SIZE, 128), HEAD_SIZE)
                attn[rows, spot] = mixed[i * ROW_TOKENS:(i + 1) * ROW_TOKENS, :]
        if paired:
            share(r, at_x).start()
        return carry

    lax.fori_loop(0, tokens // ROW_TOKENS, attend, 0)
    owns[3].wait()

    def line_copy(way, z, r):
        ref = sums.at[way, z, pl.ds(pl.multiple_of(r * ROW_TOKENS, ROW_TOKENS), ROW_TOKENS), :]
        ahead = jnp.clip(me_mp + 2 - 4 * way, 0, n_mp - 1)
        return pltpu.make_async_remote_copy(
            src_ref=ref,
            dst_ref=ref,
            send_sem=s_send.at[way, z, r],
            recv_sem=s_recv.at[way, z, r],
            device_id={"mp": ahead},
            device_id_type=MESH,
        )

    def need(z):
        away = z // 2 != group

        @pl.when(z == partner)
        def _():
            for piece in range(3):
                ref = pair_part(piece, z)
                weight_copy(base + piece, z, ref, ref, 0, partner).wait_recv()

        @pl.when(away & (lax.rem(z, 2) == core))
        def _():
            for piece in range(3):
                ref = pair_part(piece, z)
                weight_copy(base + piece, z, ref, ref, 0, partner).wait_recv()
                weight_copy(base + piece, z, ref, ref, groups, partner).start()

        @pl.when(away & (lax.rem(z, 2) != core))
        def _():
            for piece in range(3):
                ref = pair_part(piece, z)
                weight_copy(base + piece, z, ref, ref, 0, partner).wait_recv()

    def along_line():
        pl.when(jnp.logical_not(inner | urgent))(mate_copy(0, at_x).start)
        pl.when(jnp.logical_not(inner | urgent))(mate_copy(1, at_x).start)
        pl.when(jnp.logical_not(urgent))(functools.partial(send_away, base))

        @pl.when(jnp.logical_not(inner) & urgent)
        def _():
            mate_arrived()
            mate_away()

        units = line - 1
        ways = [jnp.int32(0)] * units
        ends = [jnp.int32(0)] * units
        tie = jnp.int32(line)
        for plane in range(groups):
            for z in range(line):
                plan = line_plan(line, plane, z)
                here = (group == plane) & (at_z == z)
                for i in range(units):
                    ways[i] = jnp.where(here, plan[0][i], ways[i])
                    ends[i] = jnp.where(here, plan[1][i], ends[i])
                tie = jnp.where(here, plan[2], tie)

        def entry(i, carry):
            @pl.when((i == rows_dev) & jnp.logical_not(urgent))
            def _():
                pl.when(jnp.logical_not(inner))(mate_arrived)
                mate_away()

            within = i - tie * rows_dev
            mixed = (within >= 0) & (within < 2 * rows_dev)
            u = jnp.where(mixed, tie + lax.rem(within, 2), i // rows_dev)
            r = jnp.where(mixed, within // 2, lax.rem(i, rows_dev))
            own = u == units
            way = jnp.int32(0)
            z = at_z
            for k in range(units):
                way = jnp.where(u == k, ways[k], way)
                z = jnp.where(u == k, ends[k], z)
            rows = pl.ds(pl.multiple_of(r * ROW_TOKENS, ROW_TOKENS), ROW_TOKENS)

            pl.when(r == 0)(functools.partial(need, z))

            @pl.when(u == 0)
            def _():
                share(r, 1 - at_x).wait_recv()

            terms[...] = jnp.dot(
                attn[rows, :],
                wo[:, pl.ds(pl.multiple_of(z * chunk, 128), chunk)],
                preferred_element_type=jnp.float32,
            )
            for side in range(2):
                more = at_z > 0 if side == 0 else at_z < line - 1

                @pl.when(more & (own | (way == side)))
                def _():
                    line_copy(side, z, r).wait_recv()
                    terms[...] += sums[side, z, rows, :].astype(jnp.float32)

            @pl.when(own)
            def _():
                out_ref[rows, :] = terms[...].astype(jnp.bfloat16)

            for side in range(2):

                @pl.when(jnp.logical_not(own) & (way == side))
                def _():
                    sums[side, z, rows, :] = terms[...].astype(jnp.bfloat16)
                    line_copy(side, z, r).start()

            return carry

        lax.fori_loop(0, line * rows_dev, entry, 0)

        def sent(i, carry):
            z = i // rows_dev
            r = lax.rem(i, rows_dev)
            pl.when(z > at_z)(line_copy(0, z, r).wait_send)
            pl.when(z < at_z)(line_copy(1, z, r).wait_send)
            return carry

        lax.fori_loop(0, line * rows_dev, sent, 0)
        for h in range(2):
            mate_copy(h, at_x).wait_send()
        for r in range(rows_dev):
            share(r, at_x).wait_send()

    def sum_copy(slot, way, c):
        cols = pl.ds(pl.multiple_of(c * column, 128), column)
        return pltpu.make_async_remote_copy(
            src_ref=sums.at[way, slot, :, cols],
            dst_ref=sums.at[way, slot + 1, :, cols],
            send_sem=s_send.at[way, c, slot],
            recv_sem=s_recv.at[way, c, slot],
            device_id={"mp": sides[way]},
            device_id_type=MESH,
        )

    def scatter(i, carry):
        hop = i // COLUMNS + 1
        c = lax.rem(i, COLUMNS)
        cols = pl.ds(pl.multiple_of(c * column, 128), column)
        for way in range(2):
            g = ring_member(place + (-hop if way == 0 else hop), n_mp)
            terms[way] = jnp.dot(
                attn[way * half:(way + 1) * half, :],
                wo[:, pl.ds(pl.multiple_of(g * chunk + c * column, 128), column)],
                preferred_element_type=jnp.float32,
            )
        for way in range(2):

            @pl.when(hop == 1)
            def _():
                sums[way, 0, :, cols] = terms[way].astype(jnp.bfloat16)

            @pl.when(hop > 1)
            def _():
                sum_copy(hop - 2, way, c).wait_recv()
                total = sums[way, hop - 1, :, cols].astype(jnp.float32) + terms[way]
                total = total.astype(jnp.bfloat16)

                @pl.when(hop < n_mp)
                def _():
                    sums[way, hop - 1, :, cols] = total

                @pl.when(hop == n_mp)
                def _():
                    out_ref[way * half:(way + 1) * half, cols] = total

            @pl.when(hop < n_mp)
            def _():
                sum_copy(hop - 1, way, c).start()

        return carry

    def around_ring():
        for kind in range(base, kinds):
            for j in range(1, groups):
                owner = lax.rem(me_dp + n_dp - 2 * j, n_dp)
                held_copy(kind, owner, 0).wait_recv()
                held_copy(kind, owner, groups + j - 1).start()
            for i in range(groups):
                held_copy(kind, lax.rem(partner + 2 * i, n_dp), 0).wait_recv()
        lax.fori_loop(0, n_mp * COLUMNS, scatter, 0)

        def sent(step, carry):
            for way in range(2):
                for c in range(COLUMNS):
                    sum_copy(step, way, c).wait_send()
            return carry

        lax.fori_loop(0, n_mp - 1, sent, 0)

    if paired:
        along_line()
    else:
        around_ring()

    def drain(step, carry):
        for way in range(2):
            for sub in range(SLICES):
                x_copy(step, way, sub).wait_send()
        return carry

    lax.fori_loop(0, n_mp - 1, drain, 0)
    for sub in range(SLICES):
        for j in range(1, n_dp):
            token_copy(j, sub, me_dp).wait_send()
    for kind in range(kinds):
        for i in range(2 * groups - 1):
            weight_copy(kind, me_dp, shard(kind), part(kind, me_dp), i, partner).wait_send()


def local(
    pair_tokens,
    norm_gain,
    q_weight,
    k_weight,
    value_weight,
    o_weight,
    pair_row,
    pair_span,
    block_ids,
):
    dp_count = lax.axis_size("dp")
    mp_count = lax.axis_size("mp")
    pairs_dev, pair_cap, width_local = pair_tokens.shape
    slots = dp_count * (-(-pairs_dev // dp_count))
    tok_dev = block_ids.shape[0]
    half = HEAD_SIZE // 2
    freq = 500000.0 ** (-(np.arange(half, dtype=np.float32) * 2.0 / HEAD_SIZE))
    freq = np.concatenate([freq, freq])[None, :].astype(np.float32)

    q_width = q_weight.shape[1]
    k_width = k_weight.shape[1]
    width = norm_gain.shape[0]
    out_rows = o_weight.shape[0]
    if pairs_up(dp_count, mp_count, o_weight.shape[1], width_local):
        kinds = 3 * PARTS + 3
        line = mp_count // 2
        attn_shape = (tok_dev, 2 * q_width)
        wo_shape = (2 * out_rows, width // 2)
        sums_shape = (2, line, tok_dev, width_local)
        terms_shape = (ROW_TOKENS, width_local)
        sum_sems = (2, line, tok_dev // ROW_TOKENS)
    else:
        kinds = 3 * PARTS + COLUMNS
        attn_shape = (tok_dev, q_width)
        wo_shape = (out_rows, width)
        sums_shape = (2, mp_count, tok_dev // 2, width_local)
        terms_shape = (2, tok_dev // 2, width_local // COLUMNS)
        sum_sems = (2, COLUMNS, mp_count - 1)
    far = dp_count - 1
    vmem = pl.BlockSpec(memory_space=pltpu.VMEM)
    smem = pl.BlockSpec(memory_space=pltpu.SMEM)
    anyspace = pl.BlockSpec(memory_space=pl.ANY)
    bf16 = jnp.bfloat16
    return pl.pallas_call(
        functools.partial(kernel, dp_count, mp_count),
        out_shape=jax.ShapeDtypeStruct((tok_dev, width_local), bf16),
        in_specs=[
            smem, smem, anyspace, vmem, anyspace, anyspace, anyspace, anyspace, vmem, vmem
        ],
        out_specs=vmem,
        scratch_shapes=[
            pltpu.VMEM((pairs_dev, pair_cap, width_local), bf16),
            pltpu.VMEM((slots * pair_cap, width_local), bf16),
            pltpu.VMEM((slots * pair_cap, width_local), bf16),
            pltpu.VMEM((mp_count, tok_dev, width_local), bf16),
            pltpu.VMEM((width, q_width + 2 * k_width), bf16),
            pltpu.VMEM(wo_shape, bf16),
            pltpu.VMEM((tok_dev, q_width + 2 * k_width), jnp.float32),
            pltpu.VMEM((tok_dev, 128), jnp.float32),
            pltpu.VMEM(attn_shape, bf16),
            pltpu.VMEM(sums_shape, bf16),
            pltpu.VMEM(terms_shape, jnp.float32),
            pltpu.VMEM((tok_dev, HEAD_SIZE), jnp.float32),
            pltpu.VMEM((tok_dev, HEAD_SIZE), jnp.float32),
            pltpu.VMEM((tok_dev, ROW_TOKENS), jnp.float32),
            pltpu.VMEM((tok_dev, slots * pair_cap), bf16),
            pltpu.SMEM((slots,), jnp.int32),
            pltpu.SMEM((slots,), jnp.int32),
            pltpu.SMEM((slots,), jnp.int32),
            pltpu.SemaphoreType.DMA((5,)),
            pltpu.SemaphoreType.DMA((SLICES, far)),
            pltpu.SemaphoreType.DMA((SLICES, dp_count)),
            pltpu.SemaphoreType.DMA((kinds, far)),
            pltpu.SemaphoreType.DMA((kinds, dp_count)),
            pltpu.SemaphoreType.DMA((2, SLICES, mp_count - 1)),
            pltpu.SemaphoreType.DMA((2, SLICES, mp_count - 1)),
            pltpu.SemaphoreType.DMA(sum_sems),
            pltpu.SemaphoreType.DMA(sum_sems),
            pltpu.SemaphoreType.DMA((2,)),
            pltpu.SemaphoreType.DMA((2,)),
            pltpu.SemaphoreType.DMA((tok_dev // ROW_TOKENS,)),
            pltpu.SemaphoreType.DMA((tok_dev // ROW_TOKENS,)),
        ],
        compiler_params=pltpu.CompilerParams(
            collective_id=0, has_side_effects=True, vmem_limit_bytes=60 * 1024 * 1024
        ),
    )(
        pair_row,
        jnp.transpose(pair_span),
        pair_tokens,
        norm_gain[None, :],
        q_weight,
        k_weight,
        value_weight,
        o_weight,
        block_ids.reshape(tok_dev // ROW_TOKENS, ROW_TOKENS),
        jnp.asarray(freq),
    )


def solution(mesh):
    placed = (
        P("dp", None, "mp"),
        P(),
        P("dp", "mp"),
        P("dp", "mp"),
        P("dp", "mp"),
        P("mp", "dp"),
        P(),
        P(),
        P("dp"),
    )
    return jax.shard_map(
        local, mesh=mesh, in_specs=placed, out_specs=P("dp", "mp"), check_vma=False
    )
```

```python
import functools

import jax
import jax.numpy as jnp
import numpy as np
from jax import lax
from jax.experimental import pallas as pl
from jax.experimental.pallas import tpu as pltpu
from jax.sharding import PartitionSpec as P

HEAD_SIZE = 128
ROW_TOKENS = 128
QUERY_PER_KV = 4
SLICES = 2
PARTS = 4
COLUMNS = 4
UNITS = 2
MESH = pl.DeviceIdType.MESH


def ring_member(place, count):
    place = lax.rem(place + 2 * count, count)
    return jnp.where(place < count // 2, 2 * place, 2 * (count - 1 - place) + 1)


def pairs_up(n_dp, n_mp, width, chunk):
    return n_dp // 2 == 2 and n_mp == 2 * n_dp and width == 2 * chunk


def line_plan(length, group, at):
    near = (2 * group, 2 * group + 1)
    rising = list(range(length - 1, 0, -1))
    if 1 in near:
        rising = [1] + rising[:-1]
    falling = list(range(length - 1))
    if length - 2 in near:
        falling = [length - 2] + falling[:-1]
    units = [(rising.index(z), 0, z) for z in range(at + 1, length)]
    units = sorted(units + [(falling.index(z), 1, z) for z in range(at)])
    ties = [i for i in range(length - 2) if units[i][0] == units[i + 1][0]]
    return [u[1] for u in units], [u[2] for u in units], (ties + [length])[0]


def kernel(
    n_dp, n_mp,
    row_ref, span_ref, tok_ref, gain_ref, q_ref, k_ref, v_ref, o_ref, ids_ref, freq_ref,
    out_ref,
    tokv, xout, xin, xg, wall, wo, acc, square, attn, sums, terms, cos_ref, sin_ref, vis_ref,
    put_ref, pick, first_of, length_of,
    own_sem, t_send, t_recv, w_send, w_recv, x_send, x_recv, s_send, s_recv,
    b_send, b_recv, a_send, a_recv,
):
    me_dp = lax.axis_index("dp")
    me_mp = lax.axis_index("mp")

    def place_of(g):
        return jnp.where(lax.rem(g, 2) == 0, g // 2, n_mp - 1 - g // 2)

    place = place_of(me_mp)
    sides = (ring_member(place + 1, n_mp), ring_member(place - 1, n_mp))
    groups = n_dp // 2
    core = lax.rem(me_dp, 2)
    group = me_dp // 2
    partner = me_dp + 1 - 2 * core
    others = [lax.rem(me_dp + 2 * j, n_dp) for j in range(1, groups)]
    tokens, chunk = out_ref.shape
    half = tokens // 2
    rows_dev = tokens // ROW_TOKENS
    pairs_dev, cap, _ = tok_ref.shape
    most = -(-pairs_dev // n_dp)
    slots = n_dp * most
    block = most * cap
    depth, q_width = q_ref.shape
    k_width = k_ref.shape[1]
    width = o_ref.shape[1]
    paired = pairs_up(n_dp, n_mp, width, chunk)
    slice_width = chunk // SLICES
    part_rows = depth // PARTS
    unit = chunk // UNITS
    column = chunk // COLUMNS
    out_column = width // COLUMNS
    base = 3 * PARTS
    kinds = base + (3 if paired else COLUMNS)
    out_rows = o_ref.shape[0]
    wide_half = chunk // 2
    line = n_mp // 2
    at_z = me_mp // 2
    at_x = lax.rem(me_mp, 2)
    mate = me_mp + 1 - 2 * at_x
    inner = (at_z > 0) & (at_z < line - 1)
    lead = jnp.where(at_z == 0, 1, jnp.where(at_z == line - 1, 0, group))
    urgent = core == lead
    last = n_mp - 1
    final = 2 * last
    part_slot = [min(2 * p, final - 1) for p in (2, 4, 6, n_mp)]

    def token_slice(sub):
        return pl.ds(pl.multiple_of(sub * slice_width, 128), slice_width)

    own_tokens = pltpu.make_async_copy(tok_ref, tokv, own_sem.at[4])
    own_tokens.start()

    barrier = pltpu.get_barrier_semaphore()
    for side in sides:
        pl.semaphore_signal(barrier, inc=1, device_id={"mp": side}, device_id_type=MESH)
    for j in range(1, n_dp):
        peer = lax.rem(me_dp + j, n_dp)
        pl.semaphore_signal(barrier, inc=1, device_id={"dp": peer}, device_id_type=MESH)

    greeted = 2 + n_dp - 1
    if paired:
        pl.semaphore_signal(barrier, inc=1, device_id={"mp": mate}, device_id_type=MESH)

        @pl.when(at_z < line - 1)
        def _():
            above = jnp.minimum(me_mp + 2, n_mp - 1)
            pl.semaphore_signal(barrier, inc=1, device_id={"mp": above}, device_id_type=MESH)

        @pl.when(at_z > 0)
        def _():
            below = jnp.maximum(me_mp - 2, 0)
            pl.semaphore_signal(barrier, inc=1, device_id={"mp": below}, device_id_type=MESH)

        greeted = greeted + 1 + jnp.where(at_z < line - 1, 1, 0) + jnp.where(at_z > 0, 1, 0)

    owner_list = [lax.div(row_ref[me_dp * pairs_dev + p], rows_dev) for p in range(pairs_dev)]
    slot_list = []
    for p in range(pairs_dev):
        rank = jnp.int32(0)
        for e in range(p):
            rank = rank + jnp.where(owner_list[e] == owner_list[p], 1, 0)
        slot_list.append(owner_list[p] * most + rank)
    for s in range(slots):
        index = jnp.int32(0)
        for p in range(1, pairs_dev):
            index = jnp.where(slot_list[p] == s, p, index)
        pick[s] = index

    pl.semaphore_wait(barrier, greeted)

    def token_rows(owner):
        return pl.ds(pl.multiple_of(owner * block, 16), block)

    def token_copy(j, sub, landing):
        peer = lax.rem(me_dp + j, n_dp)
        return pltpu.make_async_remote_copy(
            src_ref=xout.at[token_rows(peer), token_slice(sub)],
            dst_ref=xin.at[token_rows(landing), token_slice(sub)],
            send_sem=t_send.at[sub, j - 1],
            recv_sem=t_recv.at[sub, landing],
            device_id={"dp": peer},
            device_id_type=MESH,
        )

    def send_tokens(sub, carry):
        def arrange(s, c):
            rows = pl.ds(pl.multiple_of(s * cap, 16), cap)
            xout[rows, token_slice(sub)] = tokv[pick[s], :, token_slice(sub)]
            return c

        lax.fori_loop(0, slots, arrange, 0)
        for j in range(1, n_dp):
            token_copy(j, sub, me_dp).start()
        xin[token_rows(me_dp), token_slice(sub)] = xout[token_rows(me_dp), token_slice(sub)]
        return carry

    own_tokens.wait()
    lax.fori_loop(0, SLICES, send_tokens, 0)

    starts = (0, q_width, q_width + k_width)
    spans = (q_width, k_width, k_width)

    def pair_part(piece, owner):
        side = at_x if piece == 0 else 1 - at_x
        start = owner * chunk + max(piece - 1, 0) * wide_half
        return wo.at[
            pl.ds(pl.multiple_of(side * out_rows, 16), out_rows),
            pl.ds(pl.multiple_of(start, 128), chunk if piece == 0 else wide_half),
        ]

    def part(kind, owner):
        if kind >= base and paired:
            return pair_part(kind - base, owner)
        if kind >= base:
            start = owner * width + (kind - base) * out_column
            return wo.at[:, pl.ds(pl.multiple_of(start, 128), out_column)]
        p, which = divmod(kind, 3)
        start = owner * depth + p * part_rows
        return wall.at[
            pl.ds(pl.multiple_of(start, 16), part_rows), pl.ds(starts[which], spans[which])
        ]

    def shard(kind):
        if kind >= base and paired:
            if kind > base:
                return pair_part(kind - base, me_dp)
            return o_ref.at[:, pl.ds(pl.multiple_of(at_x * chunk, 128), chunk)]
        if kind >= base:
            return o_ref.at[:, pl.ds((kind - base) * out_column, out_column)]
        p, which = divmod(kind, 3)
        return (q_ref, k_ref, v_ref)[which].at[pl.ds(p * part_rows, part_rows), :]

    def weight_copy(kind, owner, source, target, slot, peer):
        return pltpu.make_async_remote_copy(
            src_ref=source,
            dst_ref=target,
            send_sem=w_send.at[kind, slot],
            recv_sem=w_recv.at[kind, owner],
            device_id={"dp": peer},
            device_id_type=MESH,
        )

    def held_copy(kind, owner, slot):
        return weight_copy(kind, owner, part(kind, owner), part(kind, owner), slot, partner)

    def send_away(kind):
        for j, peer in enumerate(others):
            weight_copy(kind, me_dp, shard(kind), part(kind, me_dp), 1 + j, peer).start()

    def send_partner(kind):
        weight_copy(kind, me_dp, shard(kind), part(kind, me_dp), 0, partner).start()

    owns = [
        pltpu.make_async_copy(
            (q_ref, k_ref, v_ref)[w],
            wall.at[
                pl.ds(pl.multiple_of(me_dp * depth, 16), depth), pl.ds(starts[w], spans[w])
            ],
            own_sem.at[w],
        )
        for w in range(3)
    ]
    if paired:
        owns.append(pltpu.make_async_copy(shard(base), part(base, me_dp), own_sem.at[3]))
    else:
        owns.append(
            pltpu.make_async_copy(
                o_ref,
                wo.at[:, pl.ds(pl.multiple_of(me_dp * width, 128), width)],
                own_sem.at[3],
            )
        )

    def mate_copy(h, side):
        start = me_dp * chunk + h * wide_half
        taken = (1 - at_x) * chunk + h * wide_half
        return pltpu.make_async_remote_copy(
            src_ref=o_ref.at[:, pl.ds(pl.multiple_of(taken, 128), wide_half)],
            dst_ref=wo.at[
                pl.ds(pl.multiple_of(side * out_rows, 16), out_rows),
                pl.ds(pl.multiple_of(start, 128), wide_half),
            ],
            send_sem=b_send.at[h],
            recv_sem=b_recv.at[h],
            device_id={"mp": mate},
            device_id_type=MESH,
        )

    def mate_arrived(h):
        mate_copy(h, 1 - at_x).wait_recv()
        send_partner(base + 1 + h)

    def mate_away(h):
        send_away(base + 1 + h)

    if paired:
        for h in range(2):
            pl.when(inner | urgent)(mate_copy(h, at_x).start)

    for kind in range(base // 2):
        send_away(kind)
    for w in range(3):
        owns[w].start()
    for kind in range(base):
        send_partner(kind)

    def x_copy(step, way, sub):
        sign = -1 if way == 0 else 1
        chunk_of = ring_member(place + sign * step, n_mp)
        ref = xg.at[chunk_of, pl.ds(way * half, half), token_slice(sub)]
        return pltpu.make_async_remote_copy(
            src_ref=ref,
            dst_ref=ref,
            send_sem=x_send.at[way, sub, step],
            recv_sem=x_recv.at[way, sub, step],
            device_id={"mp": sides[way]},
            device_id_type=MESH,
        )

    def x_arrival(step, way, sub):
        sign = -1 if way == 0 else 1
        chunk_of = ring_member(place + sign * (step + 1), n_mp)
        ref = xg.at[chunk_of, pl.ds(way * half, half), token_slice(sub)]
        return pltpu.make_async_remote_copy(
            src_ref=ref,
            dst_ref=ref,
            send_sem=x_send.at[way, sub, step],
            recv_sem=x_recv.at[way, sub, step],
            device_id={"mp": sides[way]},
            device_id_type=MESH,
        )

    def find_places(j, carry):
        firsts = [jnp.int32(0)] * most
        lengths = [jnp.int32(0)] * most
        found = jnp.int32(0)
        for p in range(pairs_dev):
            i = j * pairs_dev + p
            row = row_ref[i]
            begin = span_ref[0, i]
            end = span_ref[1, i]
            first = lax.rem(row, rows_dev) * ROW_TOKENS + begin
            spot = jnp.where(lax.div(row, rows_dev) == me_dp, found, most)
            for k in range(most):
                firsts[k] = jnp.where(spot == k, first, firsts[k])
                lengths[k] = jnp.where(spot == k, end - begin, lengths[k])
            found = jnp.where(spot == most, found, found + 1)
        for k in range(most):
            first_of[j * most + k] = firsts[k]
            length_of[j * most + k] = lengths[k]
        return carry

    lax.fori_loop(0, n_dp, find_places, 0)
    lane = lax.broadcasted_iota(jnp.int32, (1, slots * cap), 1)
    target = jnp.full((1, slots * cap), tokens, jnp.int32)
    for s in range(slots):
        offset = lane - s * cap
        inside = (offset >= 0) & (offset < length_of[s])
        target = jnp.where(inside, offset + first_of[s], target)
    at = lax.broadcasted_iota(jnp.int32, (tokens, slots * cap), 0)
    put_ref[...] = jnp.where(at == target, 1.0, 0.0).astype(jnp.bfloat16)

    def tables(r, carry):
        rows = pl.ds(pl.multiple_of(r * ROW_TOKENS, ROW_TOKENS), ROW_TOKENS)
        ids_j = jnp.broadcast_to(ids_ref[pl.ds(r, 1), :], (ROW_TOKENS, ROW_TOKENS)).astype(
            jnp.float32
        )
        ids_i = jnp.transpose(ids_j)
        pair_i = jnp.floor((ids_i + 0.5) * (1.0 / 3.0))
        pair_j = jnp.floor((ids_j + 0.5) * (1.0 / 3.0))
        at_i = lax.broadcasted_iota(jnp.int32, (ROW_TOKENS, ROW_TOKENS), 0)
        at_j = lax.broadcasted_iota(jnp.int32, (ROW_TOKENS, ROW_TOKENS), 1)
        hidden = (ids_i - 3.0 * pair_i == 2.0) & (ids_j - 3.0 * pair_j == 1.0)
        seen = jnp.where((at_j <= at_i) & (pair_i == pair_j), 1.0, 0.0)
        seen = jnp.where(hidden, 0.0, seen)
        vis_ref[rows, :] = seen
        angle = (jnp.sum(seen, axis=1, keepdims=True) - 1.0) * freq_ref[...]
        lane_at = lax.broadcasted_iota(jnp.int32, (ROW_TOKENS, HEAD_SIZE), 1)
        sine = jnp.sin(angle)
        cos_ref[rows, :] = jnp.cos(angle)
        sin_ref[rows, :] = jnp.where(lane_at < HEAD_SIZE // 2, -sine, sine)
        return carry

    acc[...] = jnp.zeros_like(acc)
    square[...] = jnp.zeros_like(square)

    def ramp(sub, carry):
        for j in range(1, n_dp):
            token_copy(j, sub, lax.rem(me_dp + j, n_dp)).wait_recv()
        xg[me_mp, :, token_slice(sub)] = jnp.dot(
            put_ref[...], xin[:, token_slice(sub)], preferred_element_type=jnp.float32
        ).astype(jnp.bfloat16)
        for way in range(2):
            x_copy(0, way, sub).start()

        def forward(k, c):
            for way in range(2):
                x_arrival(k, way, sub - 1 - k).wait_recv()
                x_copy(k + 1, way, sub - 1 - k).start()
            return c

        lax.fori_loop(0, jnp.minimum(sub, last - 1), forward, 0)
        lax.fori_loop(sub * rows_dev // SLICES, (sub + 1) * rows_dev // SLICES, tables, 0)
        return carry

    lax.fori_loop(0, SLICES, ramp, 0)

    for kind in range(base // 2, base):
        send_away(kind)
    owns[3].start()
    for w in range(3):
        owns[w].wait()
    for kind in range(base):
        held_copy(kind, partner, 0).wait_recv()

    def pass_part(p):
        for kind in range(3 * p, 3 * p + 3):
            for j in range(1, groups):
                owner = lax.rem(me_dp + n_dp - 2 * j, n_dp)
                held_copy(kind, owner, 0).wait_recv()
                held_copy(kind, owner, groups + j - 1).start()

    def rest_part(p):
        for kind in range(3 * p, 3 * p + 3):
            for i in range(1, groups):
                held_copy(kind, lax.rem(partner + 2 * i, n_dp), 0).wait_recv()

    def project(way, g, u):
        halves = pl.ds(pl.multiple_of(way * half, 16), half)
        wide = xg[g, halves, pl.ds(pl.multiple_of(u * unit, 128), unit)].astype(jnp.float32)
        power = wide * wide
        total = power[:, 0:128]
        for i in range(1, unit // 128):
            total = total + power[:, i * 128:(i + 1) * 128]
        square[halves, :] += total
        start = g * chunk + u * unit
        scaled = (wide * gain_ref[:, pl.ds(pl.multiple_of(start, 128), unit)]).astype(jnp.bfloat16)
        acc[halves, :] += jnp.dot(
            scaled,
            wall[pl.ds(pl.multiple_of(start, 16), unit), :],
            preferred_element_type=jnp.float32,
        )

    def project_due(slot):
        stage = slot // 2
        newest = jnp.minimum(stage + 1, last)
        catch_up = slot == 0
        for p in range(PARTS):
            catch_up = catch_up | (slot == part_slot[p])

        def one(i, carry):
            hop = i // (2 * UNITS)
            u = lax.rem(i // 2, UNITS)
            way = lax.rem(i, 2)
            g = ring_member(place + jnp.where(way == 0, -hop, hop), n_mp)
            start = g * chunk + u * unit
            owner = start // depth
            near = (owner // 2 == group) & ((start + unit - 1) // depth // 2 == group)
            if depth % unit == 0:
                needed = lax.rem(start + unit - 1, depth) // part_rows
            else:
                needed = PARTS - 1
            when = part_slot[PARTS - 1]
            for p in range(PARTS - 2, -1, -1):
                when = jnp.where(needed == p, part_slot[p], when)
            here = jnp.where(hop == 0, 0, 2 * (hop - 1) + u)
            here = jnp.where(here == final - 1, final, here)
            due = jnp.where(near, here, jnp.maximum(here, when))

            @pl.when(due == slot)
            def _():
                project(way, g, u)

            return carry

        lowest = jnp.where(catch_up, 0, newest)
        lax.fori_loop(lowest * 2 * UNITS, (newest + 1) * 2 * UNITS, one, 0)

    def slot_of(slot, carry):
        for p in range(PARTS):
            pl.when(slot == part_slot[p])(functools.partial(pass_part, p))
        stage = jnp.minimum(slot // 2, last - 1)
        side = jnp.where(slot == final, 1, lax.rem(slot, 2))
        for i in range(SLICES // 2):
            sub = side * (SLICES // 2) + i
            for way in range(2):
                fresh = (slot != final - 1) & ((stage + sub >= SLICES - 1) | (stage == last - 1))

                @pl.when(fresh)
                def _():
                    x_arrival(stage, way, sub).wait_recv()

                    @pl.when(stage < last - 1)
                    def _():
                        x_copy(stage + 1, way, sub).start()

        for p in range(PARTS):
            pl.when(slot == part_slot[p])(functools.partial(rest_part, p))
        project_due(slot)

        if paired:

            @pl.when((slot == 2) & urgent)
            def _():
                send_away(base)

            @pl.when(slot == 3)
            def _():
                send_partner(base)

            @pl.when(slot == min(6, final))
            def _():
                for h in range(2):
                    pl.when(inner | urgent)(functools.partial(mate_arrived, h))
                    pl.when(urgent)(functools.partial(mate_away, h))

        else:

            @pl.when(slot == min(2, final))
            def _():
                for kind in range(base, kinds):
                    send_away(kind)
                    send_partner(kind)

        return carry

    lax.fori_loop(0, final + 1, slot_of, 0)
    def turn(u, cosine, sine):
        return (u * cosine + pltpu.roll(u, HEAD_SIZE // 2, 1) * sine).astype(jnp.bfloat16)

    def share(r, side):
        ref = attn.at[
            pl.ds(pl.multiple_of(r * ROW_TOKENS, ROW_TOKENS), ROW_TOKENS),
            pl.ds(pl.multiple_of(side * q_width, 128), q_width),
        ]
        return pltpu.make_async_remote_copy(
            src_ref=ref,
            dst_ref=ref,
            send_sem=a_send.at[r],
            recv_sem=a_recv.at[r],
            device_id={"mp": mate},
            device_id_type=MESH,
        )

    def attend(r, carry):
        rows = pl.ds(pl.multiple_of(r * ROW_TOKENS, ROW_TOKENS), ROW_TOKENS)
        power = jnp.sum(square[rows, :], axis=1, keepdims=True)
        scale = lax.rsqrt(power / (n_mp * chunk) + 1e-05)
        cosine = cos_ref[rows, :] * scale
        sine = sin_ref[rows, :] * scale
        seen = vis_ref[rows, :] > 0.5
        left = at_x * q_width if paired else 0
        for kv in range(k_width // HEAD_SIZE):
            at_k = q_width + kv * HEAD_SIZE
            key = turn(acc[rows, at_k:at_k + HEAD_SIZE], cosine, sine)
            at_v = at_k + k_width
            value = (acc[rows, at_v:at_v + HEAD_SIZE] * scale).astype(jnp.bfloat16)
            heads = range(kv * QUERY_PER_KV, (kv + 1) * QUERY_PER_KV)
            queries = jnp.concatenate(
                [turn(acc[rows, h * HEAD_SIZE:(h + 1) * HEAD_SIZE], cosine, sine) for h in heads],
                axis=0,
            )
            scores = lax.dot_general(
                queries, key, (((1,), (1,)), ((), ())), preferred_element_type=jnp.float32
            ) * HEAD_SIZE ** (-0.5)
            probs = []
            for i in range(QUERY_PER_KV):
                own = scores[i * ROW_TOKENS:(i + 1) * ROW_TOKENS, :]
                own = jnp.where(seen, own, -1e30)
                expo = jnp.exp(own - jnp.max(own, axis=-1, keepdims=True))
                probs.append(
                    (expo / jnp.sum(expo, axis=-1, keepdims=True)).astype(jnp.bfloat16)
                )
            mixed = jnp.dot(
                jnp.concatenate(probs, axis=0), value, preferred_element_type=jnp.float32
            ).astype(jnp.bfloat16)
            for i, h in enumerate(heads):
                spot = pl.ds(pl.multiple_of(left + h * HEAD_SIZE, 128), HEAD_SIZE)
                attn[rows, spot] = mixed[i * ROW_TOKENS:(i + 1) * ROW_TOKENS, :]
        if paired:
            share(r, at_x).start()
        return carry

    lax.fori_loop(0, tokens // ROW_TOKENS, attend, 0)
    owns[3].wait()

    def line_copy(way, z, r):
        h = r // rows_dev
        ref = sums.at[
            way,
            z,
            pl.ds(pl.multiple_of(lax.rem(r, rows_dev) * ROW_TOKENS, ROW_TOKENS), ROW_TOKENS),
            pl.ds(pl.multiple_of(h * wide_half, 128), wide_half),
        ]
        ahead = jnp.clip(me_mp + 2 - 4 * way, 0, n_mp - 1)
        return pltpu.make_async_remote_copy(
            src_ref=ref,
            dst_ref=ref,
            send_sem=s_send.at[way, z, r],
            recv_sem=s_recv.at[way, z, r],
            device_id={"mp": ahead},
            device_id_type=MESH,
        )

    def need(z, pieces):
        away = z // 2 != group

        @pl.when(z == partner)
        def _():
            for piece in pieces:
                ref = pair_part(piece, z)
                weight_copy(base + piece, z, ref, ref, 0, partner).wait_recv()

        @pl.when(away & (lax.rem(z, 2) == core))
        def _():
            for piece in pieces:
                ref = pair_part(piece, z)
                weight_copy(base + piece, z, ref, ref, 0, partner).wait_recv()
                weight_copy(base + piece, z, ref, ref, groups, partner).start()

        @pl.when(away & (lax.rem(z, 2) != core))
        def _():
            for piece in pieces:
                ref = pair_part(piece, z)
                weight_copy(base + piece, z, ref, ref, 0, partner).wait_recv()

    def along_line():
        outer = jnp.logical_not(inner)
        lazy = jnp.logical_not(urgent)
        for h in range(2):
            pl.when(outer & lazy)(mate_copy(h, at_x).start)
        pl.when(lazy)(functools.partial(send_away, base))
        entries = 2 * rows_dev

        units = line - 1
        ways = [jnp.int32(0)] * units
        ends = [jnp.int32(0)] * units
        tie = jnp.int32(line)
        for plane in range(groups):
            for z in range(line):
                plan = line_plan(line, plane, z)
                here = (group == plane) & (at_z == z)
                for i in range(units):
                    ways[i] = jnp.where(here, plan[0][i], ways[i])
                    ends[i] = jnp.where(here, plan[1][i], ends[i])
                tie = jnp.where(here, plan[2], tie)

        def entry(i, carry):
            @pl.when((i == entries) & lazy)
            def _():
                for h in range(2):
                    pl.when(outer)(functools.partial(mate_arrived, h))
                    mate_away(h)

            within = i - tie * entries
            mixed = (within >= 0) & (within < 2 * entries)
            u = jnp.where(mixed, tie + lax.rem(within, 2), i // entries)
            e = jnp.where(mixed, within // 2, lax.rem(i, entries))
            h = e // rows_dev
            r = lax.rem(e, rows_dev)
            own = u == units
            way = jnp.int32(0)
            z = at_z
            for k in range(units):
                way = jnp.where(u == k, ways[k], way)
                z = jnp.where(u == k, ends[k], z)
            rows = pl.ds(pl.multiple_of(r * ROW_TOKENS, ROW_TOKENS), ROW_TOKENS)

            cols = pl.ds(pl.multiple_of(h * wide_half, 128), wide_half)
            pl.when(e == 0)(functools.partial(need, z, (0, 1)))
            pl.when(e == rows_dev)(functools.partial(need, z, (2,)))

            @pl.when((u == 0) & (h == 0))
            def _():
                share(r, 1 - at_x).wait_recv()

            terms[...] = jnp.dot(
                attn[rows, :],
                wo[:, pl.ds(pl.multiple_of(z * chunk + h * wide_half, 128), wide_half)],
                preferred_element_type=jnp.float32,
            )
            for side in range(2):
                more = at_z > 0 if side == 0 else at_z < line - 1

                @pl.when(more & (own | (way == side)))
                def _():
                    line_copy(side, z, e).wait_recv()
                    terms[...] += sums[side, z, rows, cols].astype(jnp.float32)

            @pl.when(own)
            def _():
                out_ref[rows, cols] = terms[...].astype(jnp.bfloat16)

            for side in range(2):

                @pl.when(jnp.logical_not(own) & (way == side))
                def _():
                    sums[side, z, rows, cols] = terms[...].astype(jnp.bfloat16)
                    line_copy(side, z, e).start()

            return carry

        lax.fori_loop(0, line * entries, entry, 0)

        def sent(i, carry):
            z = i // entries
            e = lax.rem(i, entries)
            pl.when(z > at_z)(line_copy(0, z, e).wait_send)
            pl.when(z < at_z)(line_copy(1, z, e).wait_send)
            return carry

        lax.fori_loop(0, line * entries, sent, 0)
        for h in range(2):
            mate_copy(h, at_x).wait_send()
        for r in range(rows_dev):
            share(r, at_x).wait_send()

    def sum_copy(slot, way, c):
        cols = pl.ds(pl.multiple_of(c * column, 128), column)
        return pltpu.make_async_remote_copy(
            src_ref=sums.at[way, slot, :, cols],
            dst_ref=sums.at[way, slot + 1, :, cols],
            send_sem=s_send.at[way, c, slot],
            recv_sem=s_recv.at[way, c, slot],
            device_id={"mp": sides[way]},
            device_id_type=MESH,
        )

    def scatter(i, carry):
        hop = i // COLUMNS + 1
        c = lax.rem(i, COLUMNS)
        cols = pl.ds(pl.multiple_of(c * column, 128), column)
        for way in range(2):
            g = ring_member(place + (-hop if way == 0 else hop), n_mp)
            terms[way] = jnp.dot(
                attn[way * half:(way + 1) * half, :],
                wo[:, pl.ds(pl.multiple_of(g * chunk + c * column, 128), column)],
                preferred_element_type=jnp.float32,
            )
        for way in range(2):

            @pl.when(hop == 1)
            def _():
                sums[way, 0, :, cols] = terms[way].astype(jnp.bfloat16)

            @pl.when(hop > 1)
            def _():
                sum_copy(hop - 2, way, c).wait_recv()
                total = sums[way, hop - 1, :, cols].astype(jnp.float32) + terms[way]
                total = total.astype(jnp.bfloat16)

                @pl.when(hop < n_mp)
                def _():
                    sums[way, hop - 1, :, cols] = total

                @pl.when(hop == n_mp)
                def _():
                    out_ref[way * half:(way + 1) * half, cols] = total

            @pl.when(hop < n_mp)
            def _():
                sum_copy(hop - 1, way, c).start()

        return carry

    def around_ring():
        for kind in range(base, kinds):
            for j in range(1, groups):
                owner = lax.rem(me_dp + n_dp - 2 * j, n_dp)
                held_copy(kind, owner, 0).wait_recv()
                held_copy(kind, owner, groups + j - 1).start()
            for i in range(groups):
                held_copy(kind, lax.rem(partner + 2 * i, n_dp), 0).wait_recv()
        lax.fori_loop(0, n_mp * COLUMNS, scatter, 0)

        def sent(step, carry):
            for way in range(2):
                for c in range(COLUMNS):
                    sum_copy(step, way, c).wait_send()
            return carry

        lax.fori_loop(0, n_mp - 1, sent, 0)

    if paired:
        along_line()
    else:
        around_ring()

    def drain(step, carry):
        for way in range(2):
            for sub in range(SLICES):
                x_copy(step, way, sub).wait_send()
        return carry

    lax.fori_loop(0, n_mp - 1, drain, 0)
    for sub in range(SLICES):
        for j in range(1, n_dp):
            token_copy(j, sub, me_dp).wait_send()
    for kind in range(kinds):
        for i in range(2 * groups - 1):
            weight_copy(kind, me_dp, shard(kind), part(kind, me_dp), i, partner).wait_send()


def local(
    pair_tokens,
    norm_gain,
    q_weight,
    k_weight,
    value_weight,
    o_weight,
    pair_row,
    pair_span,
    block_ids,
):
    dp_count = lax.axis_size("dp")
    mp_count = lax.axis_size("mp")
    pairs_dev, pair_cap, width_local = pair_tokens.shape
    slots = dp_count * (-(-pairs_dev // dp_count))
    tok_dev = block_ids.shape[0]
    half = HEAD_SIZE // 2
    freq = 500000.0 ** (-(np.arange(half, dtype=np.float32) * 2.0 / HEAD_SIZE))
    freq = np.concatenate([freq, freq])[None, :].astype(np.float32)

    q_width = q_weight.shape[1]
    k_width = k_weight.shape[1]
    width = norm_gain.shape[0]
    out_rows = o_weight.shape[0]
    if pairs_up(dp_count, mp_count, o_weight.shape[1], width_local):
        kinds = 3 * PARTS + 3
        line = mp_count // 2
        attn_shape = (tok_dev, 2 * q_width)
        wo_shape = (2 * out_rows, width // 2)
        sums_shape = (2, line, tok_dev, width_local)
        terms_shape = (ROW_TOKENS, width_local // 2)
        sum_sems = (2, line, 2 * (tok_dev // ROW_TOKENS))
    else:
        kinds = 3 * PARTS + COLUMNS
        attn_shape = (tok_dev, q_width)
        wo_shape = (out_rows, width)
        sums_shape = (2, mp_count, tok_dev // 2, width_local)
        terms_shape = (2, tok_dev // 2, width_local // COLUMNS)
        sum_sems = (2, COLUMNS, mp_count - 1)
    far = dp_count - 1
    vmem = pl.BlockSpec(memory_space=pltpu.VMEM)
    smem = pl.BlockSpec(memory_space=pltpu.SMEM)
    anyspace = pl.BlockSpec(memory_space=pl.ANY)
    bf16 = jnp.bfloat16
    return pl.pallas_call(
        functools.partial(kernel, dp_count, mp_count),
        out_shape=pltpu.VMEM((tok_dev, width_local), bf16),
        in_specs=[
            smem, smem, anyspace, vmem, anyspace, anyspace, anyspace, anyspace, vmem, vmem
        ],
        out_specs=vmem,
        scratch_shapes=[
            pltpu.VMEM((pairs_dev, pair_cap, width_local), bf16),
            pltpu.VMEM((slots * pair_cap, width_local), bf16),
            pltpu.VMEM((slots * pair_cap, width_local), bf16),
            pltpu.VMEM((mp_count, tok_dev, width_local), bf16),
            pltpu.VMEM((width, q_width + 2 * k_width), bf16),
            pltpu.VMEM(wo_shape, bf16),
            pltpu.VMEM((tok_dev, q_width + 2 * k_width), jnp.float32),
            pltpu.VMEM((tok_dev, 128), jnp.float32),
            pltpu.VMEM(attn_shape, bf16),
            pltpu.VMEM(sums_shape, bf16),
            pltpu.VMEM(terms_shape, jnp.float32),
            pltpu.VMEM((tok_dev, HEAD_SIZE), jnp.float32),
            pltpu.VMEM((tok_dev, HEAD_SIZE), jnp.float32),
            pltpu.VMEM((tok_dev, ROW_TOKENS), jnp.float32),
            pltpu.VMEM((tok_dev, slots * pair_cap), bf16),
            pltpu.SMEM((slots,), jnp.int32),
            pltpu.SMEM((slots,), jnp.int32),
            pltpu.SMEM((slots,), jnp.int32),
            pltpu.SemaphoreType.DMA((5,)),
            pltpu.SemaphoreType.DMA((SLICES, far)),
            pltpu.SemaphoreType.DMA((SLICES, dp_count)),
            pltpu.SemaphoreType.DMA((kinds, far)),
            pltpu.SemaphoreType.DMA((kinds, dp_count)),
            pltpu.SemaphoreType.DMA((2, SLICES, mp_count - 1)),
            pltpu.SemaphoreType.DMA((2, SLICES, mp_count - 1)),
            pltpu.SemaphoreType.DMA(sum_sems),
            pltpu.SemaphoreType.DMA(sum_sems),
            pltpu.SemaphoreType.DMA((2,)),
            pltpu.SemaphoreType.DMA((2,)),
            pltpu.SemaphoreType.DMA((tok_dev // ROW_TOKENS,)),
            pltpu.SemaphoreType.DMA((tok_dev // ROW_TOKENS,)),
        ],
        compiler_params=pltpu.CompilerParams(
            collective_id=0, has_side_effects=True, vmem_limit_bytes=60 * 1024 * 1024
        ),
    )(
        pair_row,
        jnp.transpose(pair_span),
        pair_tokens,
        norm_gain[None, :],
        q_weight,
        k_weight,
        value_weight,
        o_weight,
        block_ids.reshape(tok_dev // ROW_TOKENS, ROW_TOKENS),
        jnp.asarray(freq),
    )


def solution(mesh):
    placed = (
        P("dp", None, "mp"),
        P(),
        P("dp", "mp"),
        P("dp", "mp"),
        P("dp", "mp"),
        P("mp", "dp"),
        P(),
        P(),
        P("dp"),
    )
    return jax.shard_map(
        local, mesh=mesh, in_specs=placed, out_specs=P("dp", "mp"), check_vma=False
    )
```

```python
import functools

import jax
import jax.numpy as jnp
import numpy as np
from jax import lax
from jax.experimental import pallas as pl
from jax.experimental.pallas import tpu as pltpu
from jax.sharding import PartitionSpec as P

HEAD_SIZE = 128
ROW_TOKENS = 128
QUERY_PER_KV = 4
SLICES = 2
PARTS = 2
COLUMNS = 4
LINE_COLUMNS = 1
UNITS = 2
MESH = pl.DeviceIdType.MESH


def ring_member(place, count):
    place = lax.rem(place + 2 * count, count)
    return jnp.where(place < count // 2, 2 * place, 2 * (count - 1 - place) + 1)


def pairs_up(n_dp, n_mp, width, chunk):
    return n_dp // 2 == 2 and n_mp == 2 * n_dp and width == 2 * chunk


def line_plan(length, group, at):
    near = (2 * group, 2 * group + 1)
    rising = list(range(length - 1, 0, -1))
    if 1 in near:
        rising = [1] + rising[:-1]
    falling = list(range(length - 1))
    if length - 2 in near:
        falling = [length - 2] + falling[:-1]
    units = [(rising.index(z), 0, z) for z in range(at + 1, length)]
    units = sorted(units + [(falling.index(z), 1, z) for z in range(at)])
    ties = [i for i in range(length - 2) if units[i][0] == units[i + 1][0]]
    return [u[1] for u in units], [u[2] for u in units], (ties + [length])[0]


def kernel(
    n_dp, n_mp,
    row_ref, span_ref, tok_ref, gain_ref, q_ref, k_ref, v_ref, o_ref, ids_ref, freq_ref,
    out_ref,
    tokv, xout, xin, xg, wall, wo, acc, square, attn, sums, terms, cos_ref, sin_ref, vis_ref,
    put_ref, pick, first_of, length_of,
    own_sem, t_send, t_recv, w_send, w_recv, x_send, x_recv, s_send, s_recv,
    b_send, b_recv, a_send, a_recv,
):
    me_dp = lax.axis_index("dp")
    me_mp = lax.axis_index("mp")

    def place_of(g):
        return jnp.where(lax.rem(g, 2) == 0, g // 2, n_mp - 1 - g // 2)

    place = place_of(me_mp)
    sides = (ring_member(place + 1, n_mp), ring_member(place - 1, n_mp))
    groups = n_dp // 2
    core = lax.rem(me_dp, 2)
    group = me_dp // 2
    partner = me_dp + 1 - 2 * core
    others = [lax.rem(me_dp + 2 * j, n_dp) for j in range(1, groups)]
    tokens, chunk = out_ref.shape
    half = tokens // 2
    rows_dev = tokens // ROW_TOKENS
    pairs_dev, cap, _ = tok_ref.shape
    most = -(-pairs_dev // n_dp)
    slots = n_dp * most
    block = most * cap
    depth, q_width = q_ref.shape
    k_width = k_ref.shape[1]
    width = o_ref.shape[1]
    paired = pairs_up(n_dp, n_mp, width, chunk)
    slice_width = chunk // SLICES
    part_rows = depth // PARTS
    unit = chunk // UNITS
    column = chunk // COLUMNS
    out_column = width // COLUMNS
    base = 3 * PARTS
    kinds = base + (3 if paired else COLUMNS)
    out_rows = o_ref.shape[0]
    wide_half = chunk // 2
    line_width = chunk // LINE_COLUMNS
    line = n_mp // 2
    at_z = me_mp // 2
    at_x = lax.rem(me_mp, 2)
    mate = me_mp + 1 - 2 * at_x
    inner = (at_z > 0) & (at_z < line - 1)
    lead = jnp.where(at_z == 0, 1, jnp.where(at_z == line - 1, 0, group))
    urgent = core == lead
    last = n_mp - 1
    final = 2 * last
    part_slot = [min(2 * p, final - 1) for p in (4, n_mp)]

    def token_slice(sub):
        return pl.ds(pl.multiple_of(sub * slice_width, 128), slice_width)

    own_tokens = pltpu.make_async_copy(tok_ref, tokv, own_sem.at[4])
    own_tokens.start()

    barrier = pltpu.get_barrier_semaphore()
    for side in sides:
        pl.semaphore_signal(barrier, inc=1, device_id={"mp": side}, device_id_type=MESH)
    for j in range(1, n_dp):
        peer = lax.rem(me_dp + j, n_dp)
        pl.semaphore_signal(barrier, inc=1, device_id={"dp": peer}, device_id_type=MESH)

    greeted = 2 + n_dp - 1
    if paired:
        pl.semaphore_signal(barrier, inc=1, device_id={"mp": mate}, device_id_type=MESH)

        @pl.when(at_z < line - 1)
        def _():
            above = jnp.minimum(me_mp + 2, n_mp - 1)
            pl.semaphore_signal(barrier, inc=1, device_id={"mp": above}, device_id_type=MESH)

        @pl.when(at_z > 0)
        def _():
            below = jnp.maximum(me_mp - 2, 0)
            pl.semaphore_signal(barrier, inc=1, device_id={"mp": below}, device_id_type=MESH)

        greeted = greeted + 1 + jnp.where(at_z < line - 1, 1, 0) + jnp.where(at_z > 0, 1, 0)

    owner_list = [lax.div(row_ref[me_dp * pairs_dev + p], rows_dev) for p in range(pairs_dev)]
    slot_list = []
    for p in range(pairs_dev):
        rank = jnp.int32(0)
        for e in range(p):
            rank = rank + jnp.where(owner_list[e] == owner_list[p], 1, 0)
        slot_list.append(owner_list[p] * most + rank)
    for s in range(slots):
        index = jnp.int32(0)
        for p in range(1, pairs_dev):
            index = jnp.where(slot_list[p] == s, p, index)
        pick[s] = index

    pl.semaphore_wait(barrier, greeted)

    def token_rows(owner):
        return pl.ds(pl.multiple_of(owner * block, 16), block)

    def token_copy(j, sub, landing):
        peer = lax.rem(me_dp + j, n_dp)
        return pltpu.make_async_remote_copy(
            src_ref=xout.at[token_rows(peer), token_slice(sub)],
            dst_ref=xin.at[token_rows(landing), token_slice(sub)],
            send_sem=t_send.at[sub, j - 1],
            recv_sem=t_recv.at[sub, landing],
            device_id={"dp": peer},
            device_id_type=MESH,
        )

    def send_tokens(sub, carry):
        def arrange(s, c):
            rows = pl.ds(pl.multiple_of(s * cap, 16), cap)
            xout[rows, token_slice(sub)] = tokv[pick[s], :, token_slice(sub)]
            return c

        lax.fori_loop(0, slots, arrange, 0)
        for j in range(1, n_dp):
            token_copy(j, sub, me_dp).start()
        xin[token_rows(me_dp), token_slice(sub)] = xout[token_rows(me_dp), token_slice(sub)]
        return carry

    own_tokens.wait()
    lax.fori_loop(0, SLICES, send_tokens, 0)

    starts = (0, q_width, q_width + k_width)
    spans = (q_width, k_width, k_width)

    def pair_part(piece, owner):
        side = at_x if piece == 0 else 1 - at_x
        start = owner * chunk + max(piece - 1, 0) * wide_half
        return wo.at[
            pl.ds(pl.multiple_of(side * out_rows, 16), out_rows),
            pl.ds(pl.multiple_of(start, 128), chunk if piece == 0 else wide_half),
        ]

    def part(kind, owner):
        if kind >= base and paired:
            return pair_part(kind - base, owner)
        if kind >= base:
            start = owner * width + (kind - base) * out_column
            return wo.at[:, pl.ds(pl.multiple_of(start, 128), out_column)]
        p, which = divmod(kind, 3)
        start = owner * depth + p * part_rows
        return wall.at[
            pl.ds(pl.multiple_of(start, 16), part_rows), pl.ds(starts[which], spans[which])
        ]

    def shard(kind):
        if kind >= base and paired:
            if kind > base:
                return pair_part(kind - base, me_dp)
            return o_ref.at[:, pl.ds(pl.multiple_of(at_x * chunk, 128), chunk)]
        if kind >= base:
            return o_ref.at[:, pl.ds((kind - base) * out_column, out_column)]
        p, which = divmod(kind, 3)
        return (q_ref, k_ref, v_ref)[which].at[pl.ds(p * part_rows, part_rows), :]

    def weight_copy(kind, owner, source, target, slot, peer):
        return pltpu.make_async_remote_copy(
            src_ref=source,
            dst_ref=target,
            send_sem=w_send.at[kind, slot],
            recv_sem=w_recv.at[kind, owner],
            device_id={"dp": peer},
            device_id_type=MESH,
        )

    def held_copy(kind, owner, slot):
        return weight_copy(kind, owner, part(kind, owner), part(kind, owner), slot, partner)

    def send_away(kind):
        for j, peer in enumerate(others):
            weight_copy(kind, me_dp, shard(kind), part(kind, me_dp), 1 + j, peer).start()

    def send_partner(kind):
        weight_copy(kind, me_dp, shard(kind), part(kind, me_dp), 0, partner).start()

    owns = [
        pltpu.make_async_copy(
            (q_ref, k_ref, v_ref)[w],
            wall.at[
                pl.ds(pl.multiple_of(me_dp * depth, 16), depth), pl.ds(starts[w], spans[w])
            ],
            own_sem.at[w],
        )
        for w in range(3)
    ]
    if paired:
        owns.append(pltpu.make_async_copy(shard(base), part(base, me_dp), own_sem.at[3]))
    else:
        owns.append(
            pltpu.make_async_copy(
                o_ref,
                wo.at[:, pl.ds(pl.multiple_of(me_dp * width, 128), width)],
                own_sem.at[3],
            )
        )

    def mate_copy(h, side):
        start = me_dp * chunk + h * wide_half
        taken = (1 - at_x) * chunk + h * wide_half
        return pltpu.make_async_remote_copy(
            src_ref=o_ref.at[:, pl.ds(pl.multiple_of(taken, 128), wide_half)],
            dst_ref=wo.at[
                pl.ds(pl.multiple_of(side * out_rows, 16), out_rows),
                pl.ds(pl.multiple_of(start, 128), wide_half),
            ],
            send_sem=b_send.at[h],
            recv_sem=b_recv.at[h],
            device_id={"mp": mate},
            device_id_type=MESH,
        )

    def mate_arrived(h):
        mate_copy(h, 1 - at_x).wait_recv()
        send_partner(base + 1 + h)

    def mate_away(h):
        send_away(base + 1 + h)

    if paired:
        for h in range(2):
            pl.when(inner | urgent)(mate_copy(h, at_x).start)

    for kind in range(base // 2):
        send_away(kind)
    for w in range(3):
        owns[w].start()
    for kind in range(base):
        send_partner(kind)

    def x_copy(step, way, sub):
        sign = -1 if way == 0 else 1
        chunk_of = ring_member(place + sign * step, n_mp)
        ref = xg.at[chunk_of, pl.ds(way * half, half), token_slice(sub)]
        return pltpu.make_async_remote_copy(
            src_ref=ref,
            dst_ref=ref,
            send_sem=x_send.at[way, sub, step],
            recv_sem=x_recv.at[way, sub, step],
            device_id={"mp": sides[way]},
            device_id_type=MESH,
        )

    def x_arrival(step, way, sub):
        sign = -1 if way == 0 else 1
        chunk_of = ring_member(place + sign * (step + 1), n_mp)
        ref = xg.at[chunk_of, pl.ds(way * half, half), token_slice(sub)]
        return pltpu.make_async_remote_copy(
            src_ref=ref,
            dst_ref=ref,
            send_sem=x_send.at[way, sub, step],
            recv_sem=x_recv.at[way, sub, step],
            device_id={"mp": sides[way]},
            device_id_type=MESH,
        )

    def find_places(j, carry):
        firsts = [jnp.int32(0)] * most
        lengths = [jnp.int32(0)] * most
        found = jnp.int32(0)
        for p in range(pairs_dev):
            i = j * pairs_dev + p
            row = row_ref[i]
            begin = span_ref[0, i]
            end = span_ref[1, i]
            first = lax.rem(row, rows_dev) * ROW_TOKENS + begin
            spot = jnp.where(lax.div(row, rows_dev) == me_dp, found, most)
            for k in range(most):
                firsts[k] = jnp.where(spot == k, first, firsts[k])
                lengths[k] = jnp.where(spot == k, end - begin, lengths[k])
            found = jnp.where(spot == most, found, found + 1)
        for k in range(most):
            first_of[j * most + k] = firsts[k]
            length_of[j * most + k] = lengths[k]
        return carry

    lax.fori_loop(0, n_dp, find_places, 0)
    lane = lax.broadcasted_iota(jnp.int32, (1, slots * cap), 1)
    target = jnp.full((1, slots * cap), tokens, jnp.int32)
    for s in range(slots):
        offset = lane - s * cap
        inside = (offset >= 0) & (offset < length_of[s])
        target = jnp.where(inside, offset + first_of[s], target)
    at = lax.broadcasted_iota(jnp.int32, (tokens, slots * cap), 0)
    put_ref[...] = jnp.where(at == target, 1.0, 0.0).astype(jnp.bfloat16)

    def tables(r, carry):
        rows = pl.ds(pl.multiple_of(r * ROW_TOKENS, ROW_TOKENS), ROW_TOKENS)
        ids_j = jnp.broadcast_to(ids_ref[pl.ds(r, 1), :], (ROW_TOKENS, ROW_TOKENS)).astype(
            jnp.float32
        )
        ids_i = jnp.transpose(ids_j)
        pair_i = jnp.floor((ids_i + 0.5) * (1.0 / 3.0))
        pair_j = jnp.floor((ids_j + 0.5) * (1.0 / 3.0))
        at_i = lax.broadcasted_iota(jnp.int32, (ROW_TOKENS, ROW_TOKENS), 0)
        at_j = lax.broadcasted_iota(jnp.int32, (ROW_TOKENS, ROW_TOKENS), 1)
        hidden = (ids_i - 3.0 * pair_i == 2.0) & (ids_j - 3.0 * pair_j == 1.0)
        seen = jnp.where((at_j <= at_i) & (pair_i == pair_j), 1.0, 0.0)
        seen = jnp.where(hidden, 0.0, seen)
        vis_ref[rows, :] = seen
        angle = (jnp.sum(seen, axis=1, keepdims=True) - 1.0) * freq_ref[...]
        lane_at = lax.broadcasted_iota(jnp.int32, (ROW_TOKENS, HEAD_SIZE), 1)
        sine = jnp.sin(angle)
        cos_ref[rows, :] = jnp.cos(angle)
        sin_ref[rows, :] = jnp.where(lane_at < HEAD_SIZE // 2, -sine, sine)
        return carry

    acc[...] = jnp.zeros_like(acc)
    square[...] = jnp.zeros_like(square)

    def ramp(sub, carry):
        for j in range(1, n_dp):
            token_copy(j, sub, lax.rem(me_dp + j, n_dp)).wait_recv()
        xg[me_mp, :, token_slice(sub)] = jnp.dot(
            put_ref[...], xin[:, token_slice(sub)], preferred_element_type=jnp.float32
        ).astype(jnp.bfloat16)
        for way in range(2):
            x_copy(0, way, sub).start()

        def forward(k, c):
            for way in range(2):
                x_arrival(k, way, sub - 1 - k).wait_recv()
                x_copy(k + 1, way, sub - 1 - k).start()
            return c

        lax.fori_loop(0, jnp.minimum(sub, last - 1), forward, 0)
        lax.fori_loop(sub * rows_dev // SLICES, (sub + 1) * rows_dev // SLICES, tables, 0)
        return carry

    lax.fori_loop(0, SLICES, ramp, 0)

    for kind in range(base // 2, base):
        send_away(kind)
    owns[3].start()
    for w in range(3):
        owns[w].wait()
    for kind in range(base):
        held_copy(kind, partner, 0).wait_recv()

    def pass_part(p):
        for kind in range(3 * p, 3 * p + 3):
            for j in range(1, groups):
                owner = lax.rem(me_dp + n_dp - 2 * j, n_dp)
                held_copy(kind, owner, 0).wait_recv()
                held_copy(kind, owner, groups + j - 1).start()

    def rest_part(p):
        for kind in range(3 * p, 3 * p + 3):
            for i in range(1, groups):
                held_copy(kind, lax.rem(partner + 2 * i, n_dp), 0).wait_recv()

    def project(way, g, u):
        halves = pl.ds(pl.multiple_of(way * half, 16), half)
        wide = xg[g, halves, pl.ds(pl.multiple_of(u * unit, 128), unit)].astype(jnp.float32)
        power = wide * wide
        total = power[:, 0:128]
        for i in range(1, unit // 128):
            total = total + power[:, i * 128:(i + 1) * 128]
        square[halves, :] += total
        start = g * chunk + u * unit
        scaled = (wide * gain_ref[:, pl.ds(pl.multiple_of(start, 128), unit)]).astype(jnp.bfloat16)
        acc[halves, :] += jnp.dot(
            scaled,
            wall[pl.ds(pl.multiple_of(start, 16), unit), :],
            preferred_element_type=jnp.float32,
        )

    def project_due(slot):
        stage = slot // 2
        newest = jnp.minimum(stage + 1, last)
        catch_up = slot == 0
        for p in range(PARTS):
            catch_up = catch_up | (slot == part_slot[p])

        def one(i, carry):
            hop = i // (2 * UNITS)
            u = lax.rem(i // 2, UNITS)
            way = lax.rem(i, 2)
            g = ring_member(place + jnp.where(way == 0, -hop, hop), n_mp)
            start = g * chunk + u * unit
            owner = start // depth
            near = (owner // 2 == group) & ((start + unit - 1) // depth // 2 == group)
            if depth % unit == 0:
                needed = lax.rem(start + unit - 1, depth) // part_rows
            else:
                needed = PARTS - 1
            when = part_slot[PARTS - 1]
            for p in range(PARTS - 2, -1, -1):
                when = jnp.where(needed == p, part_slot[p], when)
            here = jnp.where(hop == 0, 0, 2 * (hop - 1) + u)
            here = jnp.where(here == final - 1, final, here)
            due = jnp.where(near, here, jnp.maximum(here, when))

            @pl.when(due == slot)
            def _():
                project(way, g, u)

            return carry

        lowest = jnp.where(catch_up, 0, newest)
        lax.fori_loop(lowest * 2 * UNITS, (newest + 1) * 2 * UNITS, one, 0)

    def slot_of(slot, carry):
        for p in range(PARTS):
            pl.when(slot == part_slot[p])(functools.partial(pass_part, p))
        stage = jnp.minimum(slot // 2, last - 1)
        side = jnp.where(slot == final, 1, lax.rem(slot, 2))
        for i in range(SLICES // 2):
            sub = side * (SLICES // 2) + i
            for way in range(2):
                fresh = (slot != final - 1) & ((stage + sub >= SLICES - 1) | (stage == last - 1))

                @pl.when(fresh)
                def _():
                    x_arrival(stage, way, sub).wait_recv()

                    @pl.when(stage < last - 1)
                    def _():
                        x_copy(stage + 1, way, sub).start()

        for p in range(PARTS):
            pl.when(slot == part_slot[p])(functools.partial(rest_part, p))
        project_due(slot)

        if paired:

            @pl.when((slot == 2) & urgent)
            def _():
                send_away(base)

            @pl.when(slot == 3)
            def _():
                send_partner(base)

            @pl.when(slot == min(6, final))
            def _():
                for h in range(2):
                    pl.when(inner | urgent)(functools.partial(mate_arrived, h))
                    pl.when(urgent)(functools.partial(mate_away, h))

        else:

            @pl.when(slot == min(2, final))
            def _():
                for kind in range(base, kinds):
                    send_away(kind)
                    send_partner(kind)

        return carry

    lax.fori_loop(0, final + 1, slot_of, 0)
    def turn(u, cosine, sine):
        return (u * cosine + pltpu.roll(u, HEAD_SIZE // 2, 1) * sine).astype(jnp.bfloat16)

    def share(r, side):
        ref = attn.at[
            pl.ds(pl.multiple_of(r * ROW_TOKENS, ROW_TOKENS), ROW_TOKENS),
            pl.ds(pl.multiple_of(side * q_width, 128), q_width),
        ]
        return pltpu.make_async_remote_copy(
            src_ref=ref,
            dst_ref=ref,
            send_sem=a_send.at[r],
            recv_sem=a_recv.at[r],
            device_id={"mp": mate},
            device_id_type=MESH,
        )

    def attend(r, carry):
        rows = pl.ds(pl.multiple_of(r * ROW_TOKENS, ROW_TOKENS), ROW_TOKENS)
        power = jnp.sum(square[rows, :], axis=1, keepdims=True)
        scale = lax.rsqrt(power / (n_mp * chunk) + 1e-05)
        cosine = cos_ref[rows, :] * scale
        sine = sin_ref[rows, :] * scale
        seen = vis_ref[rows, :] > 0.5
        left = at_x * q_width if paired else 0
        for kv in range(k_width // HEAD_SIZE):
            at_k = q_width + kv * HEAD_SIZE
            key = turn(acc[rows, at_k:at_k + HEAD_SIZE], cosine, sine)
            at_v = at_k + k_width
            value = (acc[rows, at_v:at_v + HEAD_SIZE] * scale).astype(jnp.bfloat16)
            heads = range(kv * QUERY_PER_KV, (kv + 1) * QUERY_PER_KV)
            queries = jnp.concatenate(
                [turn(acc[rows, h * HEAD_SIZE:(h + 1) * HEAD_SIZE], cosine, sine) for h in heads],
                axis=0,
            )
            scores = lax.dot_general(
                queries, key, (((1,), (1,)), ((), ())), preferred_element_type=jnp.float32
            ) * HEAD_SIZE ** (-0.5)
            probs = []
            for i in range(QUERY_PER_KV):
                own = scores[i * ROW_TOKENS:(i + 1) * ROW_TOKENS, :]
                own = jnp.where(seen, own, -1e30)
                expo = jnp.exp(own - jnp.max(own, axis=-1, keepdims=True))
                probs.append(
                    (expo / jnp.sum(expo, axis=-1, keepdims=True)).astype(jnp.bfloat16)
                )
            mixed = jnp.dot(
                jnp.concatenate(probs, axis=0), value, preferred_element_type=jnp.float32
            ).astype(jnp.bfloat16)
            for i, h in enumerate(heads):
                spot = pl.ds(pl.multiple_of(left + h * HEAD_SIZE, 128), HEAD_SIZE)
                attn[rows, spot] = mixed[i * ROW_TOKENS:(i + 1) * ROW_TOKENS, :]
        if paired:
            share(r, at_x).start()
        return carry

    lax.fori_loop(0, tokens // ROW_TOKENS, attend, 0)
    owns[3].wait()

    def line_copy(way, z, r):
        h = r // rows_dev
        ref = sums.at[
            way,
            z,
            pl.ds(pl.multiple_of(lax.rem(r, rows_dev) * ROW_TOKENS, ROW_TOKENS), ROW_TOKENS),
            pl.ds(pl.multiple_of(h * line_width, 128), line_width),
        ]
        ahead = jnp.clip(me_mp + 2 - 4 * way, 0, n_mp - 1)
        return pltpu.make_async_remote_copy(
            src_ref=ref,
            dst_ref=ref,
            send_sem=s_send.at[way, z, r],
            recv_sem=s_recv.at[way, z, r],
            device_id={"mp": ahead},
            device_id_type=MESH,
        )

    def need(z, pieces):
        away = z // 2 != group

        @pl.when(z == partner)
        def _():
            for piece in pieces:
                ref = pair_part(piece, z)
                weight_copy(base + piece, z, ref, ref, 0, partner).wait_recv()

        @pl.when(away & (lax.rem(z, 2) == core))
        def _():
            for piece in pieces:
                ref = pair_part(piece, z)
                weight_copy(base + piece, z, ref, ref, 0, partner).wait_recv()
                weight_copy(base + piece, z, ref, ref, groups, partner).start()

        @pl.when(away & (lax.rem(z, 2) != core))
        def _():
            for piece in pieces:
                ref = pair_part(piece, z)
                weight_copy(base + piece, z, ref, ref, 0, partner).wait_recv()

    def along_line():
        outer = jnp.logical_not(inner)
        lazy = jnp.logical_not(urgent)
        for h in range(2):
            pl.when(outer & lazy)(mate_copy(h, at_x).start)
        pl.when(lazy)(functools.partial(send_away, base))
        entries = LINE_COLUMNS * rows_dev

        units = line - 1
        ways = [jnp.int32(0)] * units
        ends = [jnp.int32(0)] * units
        tie = jnp.int32(line)
        for plane in range(groups):
            for z in range(line):
                plan = line_plan(line, plane, z)
                here = (group == plane) & (at_z == z)
                for i in range(units):
                    ways[i] = jnp.where(here, plan[0][i], ways[i])
                    ends[i] = jnp.where(here, plan[1][i], ends[i])
                tie = jnp.where(here, plan[2], tie)

        def entry(i, carry):
            @pl.when((i == entries) & lazy)
            def _():
                for h in range(2):
                    pl.when(outer)(functools.partial(mate_arrived, h))
                    mate_away(h)

            within = i - tie * entries
            mixed = (within >= 0) & (within < 2 * entries)
            u = jnp.where(mixed, tie + lax.rem(within, 2), i // entries)
            e = jnp.where(mixed, within // 2, lax.rem(i, entries))
            h = e // rows_dev
            r = lax.rem(e, rows_dev)
            own = u == units
            way = jnp.int32(0)
            z = at_z
            for k in range(units):
                way = jnp.where(u == k, ways[k], way)
                z = jnp.where(u == k, ends[k], z)
            rows = pl.ds(pl.multiple_of(r * ROW_TOKENS, ROW_TOKENS), ROW_TOKENS)

            cols = pl.ds(pl.multiple_of(h * line_width, 128), line_width)
            pl.when(e == 0)(functools.partial(need, z, (0, 1) if LINE_COLUMNS > 1 else (0, 1, 2)))
            if LINE_COLUMNS > 1:
                second = rows_dev * LINE_COLUMNS // 2
                pl.when(e == second)(functools.partial(need, z, (2,)))

            @pl.when((u == 0) & (h == 0))
            def _():
                share(r, 1 - at_x).wait_recv()

            terms[...] = jnp.dot(
                attn[rows, :],
                wo[:, pl.ds(pl.multiple_of(z * chunk + h * line_width, 128), line_width)],
                preferred_element_type=jnp.float32,
            )
            for side in range(2):
                more = at_z > 0 if side == 0 else at_z < line - 1

                @pl.when(more & (own | (way == side)))
                def _():
                    line_copy(side, z, e).wait_recv()
                    terms[...] += sums[side, z, rows, cols].astype(jnp.float32)

            @pl.when(own)
            def _():
                out_ref[rows, cols] = terms[...].astype(jnp.bfloat16)

            for side in range(2):

                @pl.when(jnp.logical_not(own) & (way == side))
                def _():
                    sums[side, z, rows, cols] = terms[...].astype(jnp.bfloat16)
                    line_copy(side, z, e).start()

            return carry

        lax.fori_loop(0, line * entries, entry, 0)

        def sent(i, carry):
            z = i // entries
            e = lax.rem(i, entries)
            pl.when(z > at_z)(line_copy(0, z, e).wait_send)
            pl.when(z < at_z)(line_copy(1, z, e).wait_send)
            return carry

        lax.fori_loop(0, line * entries, sent, 0)
        for h in range(2):
            mate_copy(h, at_x).wait_send()
        for r in range(rows_dev):
            share(r, at_x).wait_send()

    def sum_copy(slot, way, c):
        cols = pl.ds(pl.multiple_of(c * column, 128), column)
        return pltpu.make_async_remote_copy(
            src_ref=sums.at[way, slot, :, cols],
            dst_ref=sums.at[way, slot + 1, :, cols],
            send_sem=s_send.at[way, c, slot],
            recv_sem=s_recv.at[way, c, slot],
            device_id={"mp": sides[way]},
            device_id_type=MESH,
        )

    def scatter(i, carry):
        hop = i // COLUMNS + 1
        c = lax.rem(i, COLUMNS)
        cols = pl.ds(pl.multiple_of(c * column, 128), column)
        for way in range(2):
            g = ring_member(place + (-hop if way == 0 else hop), n_mp)
            terms[way] = jnp.dot(
                attn[way * half:(way + 1) * half, :],
                wo[:, pl.ds(pl.multiple_of(g * chunk + c * column, 128), column)],
                preferred_element_type=jnp.float32,
            )
        for way in range(2):

            @pl.when(hop == 1)
            def _():
                sums[way, 0, :, cols] = terms[way].astype(jnp.bfloat16)

            @pl.when(hop > 1)
            def _():
                sum_copy(hop - 2, way, c).wait_recv()
                total = sums[way, hop - 1, :, cols].astype(jnp.float32) + terms[way]
                total = total.astype(jnp.bfloat16)

                @pl.when(hop < n_mp)
                def _():
                    sums[way, hop - 1, :, cols] = total

                @pl.when(hop == n_mp)
                def _():
                    out_ref[way * half:(way + 1) * half, cols] = total

            @pl.when(hop < n_mp)
            def _():
                sum_copy(hop - 1, way, c).start()

        return carry

    def around_ring():
        for kind in range(base, kinds):
            for j in range(1, groups):
                owner = lax.rem(me_dp + n_dp - 2 * j, n_dp)
                held_copy(kind, owner, 0).wait_recv()
                held_copy(kind, owner, groups + j - 1).start()
            for i in range(groups):
                held_copy(kind, lax.rem(partner + 2 * i, n_dp), 0).wait_recv()
        lax.fori_loop(0, n_mp * COLUMNS, scatter, 0)

        def sent(step, carry):
            for way in range(2):
                for c in range(COLUMNS):
                    sum_copy(step, way, c).wait_send()
            return carry

        lax.fori_loop(0, n_mp - 1, sent, 0)

    if paired:
        along_line()
    else:
        around_ring()

    def drain(step, carry):
        for way in range(2):
            for sub in range(SLICES):
                x_copy(step, way, sub).wait_send()
        return carry

    lax.fori_loop(0, n_mp - 1, drain, 0)
    for sub in range(SLICES):
        for j in range(1, n_dp):
            token_copy(j, sub, me_dp).wait_send()
    for kind in range(kinds):
        for i in range(2 * groups - 1):
            weight_copy(kind, me_dp, shard(kind), part(kind, me_dp), i, partner).wait_send()


def local(
    pair_tokens,
    norm_gain,
    q_weight,
    k_weight,
    value_weight,
    o_weight,
    pair_row,
    pair_span,
    block_ids,
):
    dp_count = lax.axis_size("dp")
    mp_count = lax.axis_size("mp")
    pairs_dev, pair_cap, width_local = pair_tokens.shape
    slots = dp_count * (-(-pairs_dev // dp_count))
    tok_dev = block_ids.shape[0]
    half = HEAD_SIZE // 2
    freq = 500000.0 ** (-(np.arange(half, dtype=np.float32) * 2.0 / HEAD_SIZE))
    freq = np.concatenate([freq, freq])[None, :].astype(np.float32)

    q_width = q_weight.shape[1]
    k_width = k_weight.shape[1]
    width = norm_gain.shape[0]
    out_rows = o_weight.shape[0]
    if pairs_up(dp_count, mp_count, o_weight.shape[1], width_local):
        kinds = 3 * PARTS + 3
        line = mp_count // 2
        attn_shape = (tok_dev, 2 * q_width)
        wo_shape = (2 * out_rows, width // 2)
        sums_shape = (2, line, tok_dev, width_local)
        terms_shape = (ROW_TOKENS, width_local // LINE_COLUMNS)
        sum_sems = (2, line, LINE_COLUMNS * (tok_dev // ROW_TOKENS))
    else:
        kinds = 3 * PARTS + COLUMNS
        attn_shape = (tok_dev, q_width)
        wo_shape = (out_rows, width)
        sums_shape = (2, mp_count, tok_dev // 2, width_local)
        terms_shape = (2, tok_dev // 2, width_local // COLUMNS)
        sum_sems = (2, COLUMNS, mp_count - 1)
    far = dp_count - 1
    vmem = pl.BlockSpec(memory_space=pltpu.VMEM)
    smem = pl.BlockSpec(memory_space=pltpu.SMEM)
    anyspace = pl.BlockSpec(memory_space=pl.ANY)
    bf16 = jnp.bfloat16
    return pl.pallas_call(
        functools.partial(kernel, dp_count, mp_count),
        out_shape=pltpu.VMEM((tok_dev, width_local), bf16),
        in_specs=[
            smem, smem, anyspace, vmem, anyspace, anyspace, anyspace, anyspace, vmem, vmem
        ],
        out_specs=vmem,
        scratch_shapes=[
            pltpu.VMEM((pairs_dev, pair_cap, width_local), bf16),
            pltpu.VMEM((slots * pair_cap, width_local), bf16),
            pltpu.VMEM((slots * pair_cap, width_local), bf16),
            pltpu.VMEM((mp_count, tok_dev, width_local), bf16),
            pltpu.VMEM((width, q_width + 2 * k_width), bf16),
            pltpu.VMEM(wo_shape, bf16),
            pltpu.VMEM((tok_dev, q_width + 2 * k_width), jnp.float32),
            pltpu.VMEM((tok_dev, 128), jnp.float32),
            pltpu.VMEM(attn_shape, bf16),
            pltpu.VMEM(sums_shape, bf16),
            pltpu.VMEM(terms_shape, jnp.float32),
            pltpu.VMEM((tok_dev, HEAD_SIZE), jnp.float32),
            pltpu.VMEM((tok_dev, HEAD_SIZE), jnp.float32),
            pltpu.VMEM((tok_dev, ROW_TOKENS), jnp.float32),
            pltpu.VMEM((tok_dev, slots * pair_cap), bf16),
            pltpu.SMEM((slots,), jnp.int32),
            pltpu.SMEM((slots,), jnp.int32),
            pltpu.SMEM((slots,), jnp.int32),
            pltpu.SemaphoreType.DMA((5,)),
            pltpu.SemaphoreType.DMA((SLICES, far)),
            pltpu.SemaphoreType.DMA((SLICES, dp_count)),
            pltpu.SemaphoreType.DMA((kinds, far)),
            pltpu.SemaphoreType.DMA((kinds, dp_count)),
            pltpu.SemaphoreType.DMA((2, SLICES, mp_count - 1)),
            pltpu.SemaphoreType.DMA((2, SLICES, mp_count - 1)),
            pltpu.SemaphoreType.DMA(sum_sems),
            pltpu.SemaphoreType.DMA(sum_sems),
            pltpu.SemaphoreType.DMA((2,)),
            pltpu.SemaphoreType.DMA((2,)),
            pltpu.SemaphoreType.DMA((tok_dev // ROW_TOKENS,)),
            pltpu.SemaphoreType.DMA((tok_dev // ROW_TOKENS,)),
        ],
        compiler_params=pltpu.CompilerParams(
            collective_id=0, has_side_effects=True, vmem_limit_bytes=60 * 1024 * 1024
        ),
    )(
        pair_row,
        jnp.transpose(pair_span),
        pair_tokens,
        norm_gain[None, :],
        q_weight,
        k_weight,
        value_weight,
        o_weight,
        block_ids.reshape(tok_dev // ROW_TOKENS, ROW_TOKENS),
        jnp.asarray(freq),
    )


def solution(mesh):
    placed = (
        P("dp", None, "mp"),
        P(),
        P("dp", "mp"),
        P("dp", "mp"),
        P("dp", "mp"),
        P("mp", "dp"),
        P(),
        P(),
        P("dp"),
    )
    return jax.shard_map(
        local, mesh=mesh, in_specs=placed, out_specs=P("dp", "mp"), check_vma=False
    )
```

```python
import functools

import jax
import jax.numpy as jnp
import numpy as np
from jax import lax
from jax.experimental import pallas as pl
from jax.experimental.pallas import tpu as pltpu
from jax.sharding import PartitionSpec as P

HEAD_SIZE = 128
ROW_TOKENS = 128
QUERY_PER_KV = 4
SLICES = 2
PART_EDGES = (0, 2, 3, 4)
PARTS = len(PART_EDGES) - 1
COLUMNS = 4
LINE_COLUMNS = 1
UNITS = 2
MESH = pl.DeviceIdType.MESH


def ring_member(place, count):
    place = lax.rem(place + 2 * count, count)
    return jnp.where(place < count // 2, 2 * place, 2 * (count - 1 - place) + 1)


def pairs_up(n_dp, n_mp, width, chunk):
    return n_dp // 2 == 2 and n_mp == 2 * n_dp and width == 2 * chunk


def line_plan(length, group, at):
    near = (2 * group, 2 * group + 1)
    rising = list(range(length - 1, 0, -1))
    if 1 in near:
        rising = [1] + rising[:-1]
    falling = list(range(length - 1))
    if length - 2 in near:
        falling = [length - 2] + falling[:-1]
    units = [(rising.index(z), 0, z) for z in range(at + 1, length)]
    units = sorted(units + [(falling.index(z), 1, z) for z in range(at)])
    ties = [i for i in range(length - 2) if units[i][0] == units[i + 1][0]]
    return [u[1] for u in units], [u[2] for u in units], (ties + [length])[0]


def kernel(
    n_dp, n_mp,
    row_ref, span_ref, tok_ref, gain_ref, q_ref, k_ref, v_ref, o_ref, ids_ref, freq_ref,
    out_ref,
    tokv, xout, xin, xg, wall, wo, acc, square, attn, sums, terms, cos_ref, sin_ref, vis_ref,
    put_ref, pick, first_of, length_of,
    own_sem, t_send, t_recv, w_send, w_recv, x_send, x_recv, s_send, s_recv,
    b_send, b_recv, a_send, a_recv,
):
    me_dp = lax.axis_index("dp")
    me_mp = lax.axis_index("mp")

    def place_of(g):
        return jnp.where(lax.rem(g, 2) == 0, g // 2, n_mp - 1 - g // 2)

    place = place_of(me_mp)
    sides = (ring_member(place + 1, n_mp), ring_member(place - 1, n_mp))
    groups = n_dp // 2
    core = lax.rem(me_dp, 2)
    group = me_dp // 2
    partner = me_dp + 1 - 2 * core
    others = [lax.rem(me_dp + 2 * j, n_dp) for j in range(1, groups)]
    tokens, chunk = out_ref.shape
    half = tokens // 2
    rows_dev = tokens // ROW_TOKENS
    pairs_dev, cap, _ = tok_ref.shape
    most = -(-pairs_dev // n_dp)
    slots = n_dp * most
    block = most * cap
    depth, q_width = q_ref.shape
    k_width = k_ref.shape[1]
    width = o_ref.shape[1]
    paired = pairs_up(n_dp, n_mp, width, chunk)
    slice_width = chunk // SLICES
    part_edges = [depth * e // PART_EDGES[-1] for e in PART_EDGES]
    unit = chunk // UNITS
    column = chunk // COLUMNS
    out_column = width // COLUMNS
    base = 3 * PARTS
    kinds = base + (3 if paired else COLUMNS)
    out_rows = o_ref.shape[0]
    wide_half = chunk // 2
    line_width = chunk // LINE_COLUMNS
    line = n_mp // 2
    at_z = me_mp // 2
    at_x = lax.rem(me_mp, 2)
    mate = me_mp + 1 - 2 * at_x
    inner = (at_z > 0) & (at_z < line - 1)
    lead = jnp.where(at_z == 0, 1, jnp.where(at_z == line - 1, 0, group))
    urgent = core == lead
    last = n_mp - 1
    final = 2 * last
    part_slot = [min(p, final - 1) for p in (8, 11, 2 * n_mp)]

    def token_slice(sub):
        return pl.ds(pl.multiple_of(sub * slice_width, 128), slice_width)

    own_tokens = pltpu.make_async_copy(tok_ref, tokv, own_sem.at[4])
    own_tokens.start()

    barrier = pltpu.get_barrier_semaphore()
    for side in sides:
        pl.semaphore_signal(barrier, inc=1, device_id={"mp": side}, device_id_type=MESH)
    for j in range(1, n_dp):
        peer = lax.rem(me_dp + j, n_dp)
        pl.semaphore_signal(barrier, inc=1, device_id={"dp": peer}, device_id_type=MESH)

    greeted = 2 + n_dp - 1
    if paired:
        pl.semaphore_signal(barrier, inc=1, device_id={"mp": mate}, device_id_type=MESH)

        @pl.when(at_z < line - 1)
        def _():
            above = jnp.minimum(me_mp + 2, n_mp - 1)
            pl.semaphore_signal(barrier, inc=1, device_id={"mp": above}, device_id_type=MESH)

        @pl.when(at_z > 0)
        def _():
            below = jnp.maximum(me_mp - 2, 0)
            pl.semaphore_signal(barrier, inc=1, device_id={"mp": below}, device_id_type=MESH)

        greeted = greeted + 1 + jnp.where(at_z < line - 1, 1, 0) + jnp.where(at_z > 0, 1, 0)

    owner_list = [lax.div(row_ref[me_dp * pairs_dev + p], rows_dev) for p in range(pairs_dev)]
    slot_list = []
    for p in range(pairs_dev):
        rank = jnp.int32(0)
        for e in range(p):
            rank = rank + jnp.where(owner_list[e] == owner_list[p], 1, 0)
        slot_list.append(owner_list[p] * most + rank)
    for s in range(slots):
        index = jnp.int32(0)
        for p in range(1, pairs_dev):
            index = jnp.where(slot_list[p] == s, p, index)
        pick[s] = index

    pl.semaphore_wait(barrier, greeted)

    def token_rows(owner):
        return pl.ds(pl.multiple_of(owner * block, 16), block)

    def token_copy(j, sub, landing):
        peer = lax.rem(me_dp + j, n_dp)
        return pltpu.make_async_remote_copy(
            src_ref=xout.at[token_rows(peer), token_slice(sub)],
            dst_ref=xin.at[token_rows(landing), token_slice(sub)],
            send_sem=t_send.at[sub, j - 1],
            recv_sem=t_recv.at[sub, landing],
            device_id={"dp": peer},
            device_id_type=MESH,
        )

    def send_tokens(sub, carry):
        def arrange(s, c):
            rows = pl.ds(pl.multiple_of(s * cap, 16), cap)
            xout[rows, token_slice(sub)] = tokv[pick[s], :, token_slice(sub)]
            return c

        lax.fori_loop(0, slots, arrange, 0)
        for j in range(1, n_dp):
            token_copy(j, sub, me_dp).start()
        xin[token_rows(me_dp), token_slice(sub)] = xout[token_rows(me_dp), token_slice(sub)]
        return carry

    own_tokens.wait()
    lax.fori_loop(0, SLICES, send_tokens, 0)

    starts = (0, q_width, q_width + k_width)
    spans = (q_width, k_width, k_width)

    def pair_part(piece, owner):
        side = at_x if piece == 0 else 1 - at_x
        start = owner * chunk + max(piece - 1, 0) * wide_half
        return wo.at[
            pl.ds(pl.multiple_of(side * out_rows, 16), out_rows),
            pl.ds(pl.multiple_of(start, 128), chunk if piece == 0 else wide_half),
        ]

    def part(kind, owner):
        if kind >= base and paired:
            return pair_part(kind - base, owner)
        if kind >= base:
            start = owner * width + (kind - base) * out_column
            return wo.at[:, pl.ds(pl.multiple_of(start, 128), out_column)]
        p, which = divmod(kind, 3)
        start = owner * depth + part_edges[p]
        part_rows = part_edges[p + 1] - part_edges[p]
        return wall.at[
            pl.ds(pl.multiple_of(start, 16), part_rows), pl.ds(starts[which], spans[which])
        ]

    def shard(kind):
        if kind >= base and paired:
            if kind > base:
                return pair_part(kind - base, me_dp)
            return o_ref.at[:, pl.ds(pl.multiple_of(at_x * chunk, 128), chunk)]
        if kind >= base:
            return o_ref.at[:, pl.ds((kind - base) * out_column, out_column)]
        p, which = divmod(kind, 3)
        return (q_ref, k_ref, v_ref)[which].at[
            pl.ds(part_edges[p], part_edges[p + 1] - part_edges[p]), :
        ]

    def weight_copy(kind, owner, source, target, slot, peer):
        return pltpu.make_async_remote_copy(
            src_ref=source,
            dst_ref=target,
            send_sem=w_send.at[kind, slot],
            recv_sem=w_recv.at[kind, owner],
            device_id={"dp": peer},
            device_id_type=MESH,
        )

    def held_copy(kind, owner, slot):
        return weight_copy(kind, owner, part(kind, owner), part(kind, owner), slot, partner)

    def send_away(kind):
        for j, peer in enumerate(others):
            weight_copy(kind, me_dp, shard(kind), part(kind, me_dp), 1 + j, peer).start()

    def send_partner(kind):
        weight_copy(kind, me_dp, shard(kind), part(kind, me_dp), 0, partner).start()

    owns = [
        pltpu.make_async_copy(
            (q_ref, k_ref, v_ref)[w],
            wall.at[
                pl.ds(pl.multiple_of(me_dp * depth, 16), depth), pl.ds(starts[w], spans[w])
            ],
            own_sem.at[w],
        )
        for w in range(3)
    ]
    if paired:
        owns.append(pltpu.make_async_copy(shard(base), part(base, me_dp), own_sem.at[3]))
    else:
        owns.append(
            pltpu.make_async_copy(
                o_ref,
                wo.at[:, pl.ds(pl.multiple_of(me_dp * width, 128), width)],
                own_sem.at[3],
            )
        )

    def mate_copy(h, side):
        start = me_dp * chunk + h * wide_half
        taken = (1 - at_x) * chunk + h * wide_half
        return pltpu.make_async_remote_copy(
            src_ref=o_ref.at[:, pl.ds(pl.multiple_of(taken, 128), wide_half)],
            dst_ref=wo.at[
                pl.ds(pl.multiple_of(side * out_rows, 16), out_rows),
                pl.ds(pl.multiple_of(start, 128), wide_half),
            ],
            send_sem=b_send.at[h],
            recv_sem=b_recv.at[h],
            device_id={"mp": mate},
            device_id_type=MESH,
        )

    def mate_arrived(h):
        mate_copy(h, 1 - at_x).wait_recv()
        send_partner(base + 1 + h)

    def mate_away(h):
        send_away(base + 1 + h)

    if paired:
        for h in range(2):
            pl.when(inner | urgent)(mate_copy(h, at_x).start)

    for kind in range(6):
        send_away(kind)
    for w in range(3):
        owns[w].start()
    for kind in range(base):
        send_partner(kind)

    def x_copy(step, way, sub):
        sign = -1 if way == 0 else 1
        chunk_of = ring_member(place + sign * step, n_mp)
        ref = xg.at[chunk_of, pl.ds(way * half, half), token_slice(sub)]
        return pltpu.make_async_remote_copy(
            src_ref=ref,
            dst_ref=ref,
            send_sem=x_send.at[way, sub, step],
            recv_sem=x_recv.at[way, sub, step],
            device_id={"mp": sides[way]},
            device_id_type=MESH,
        )

    def x_arrival(step, way, sub):
        sign = -1 if way == 0 else 1
        chunk_of = ring_member(place + sign * (step + 1), n_mp)
        ref = xg.at[chunk_of, pl.ds(way * half, half), token_slice(sub)]
        return pltpu.make_async_remote_copy(
            src_ref=ref,
            dst_ref=ref,
            send_sem=x_send.at[way, sub, step],
            recv_sem=x_recv.at[way, sub, step],
            device_id={"mp": sides[way]},
            device_id_type=MESH,
        )

    def find_places(j, carry):
        firsts = [jnp.int32(0)] * most
        lengths = [jnp.int32(0)] * most
        found = jnp.int32(0)
        for p in range(pairs_dev):
            i = j * pairs_dev + p
            row = row_ref[i]
            begin = span_ref[0, i]
            end = span_ref[1, i]
            first = lax.rem(row, rows_dev) * ROW_TOKENS + begin
            spot = jnp.where(lax.div(row, rows_dev) == me_dp, found, most)
            for k in range(most):
                firsts[k] = jnp.where(spot == k, first, firsts[k])
                lengths[k] = jnp.where(spot == k, end - begin, lengths[k])
            found = jnp.where(spot == most, found, found + 1)
        for k in range(most):
            first_of[j * most + k] = firsts[k]
            length_of[j * most + k] = lengths[k]
        return carry

    lax.fori_loop(0, n_dp, find_places, 0)
    lane = lax.broadcasted_iota(jnp.int32, (1, slots * cap), 1)
    target = jnp.full((1, slots * cap), tokens, jnp.int32)
    for s in range(slots):
        offset = lane - s * cap
        inside = (offset >= 0) & (offset < length_of[s])
        target = jnp.where(inside, offset + first_of[s], target)
    at = lax.broadcasted_iota(jnp.int32, (tokens, slots * cap), 0)
    put_ref[...] = jnp.where(at == target, 1.0, 0.0).astype(jnp.bfloat16)

    def tables(r, carry):
        rows = pl.ds(pl.multiple_of(r * ROW_TOKENS, ROW_TOKENS), ROW_TOKENS)
        ids_j = jnp.broadcast_to(ids_ref[pl.ds(r, 1), :], (ROW_TOKENS, ROW_TOKENS)).astype(
            jnp.float32
        )
        ids_i = jnp.transpose(ids_j)
        pair_i = jnp.floor((ids_i + 0.5) * (1.0 / 3.0))
        pair_j = jnp.floor((ids_j + 0.5) * (1.0 / 3.0))
        at_i = lax.broadcasted_iota(jnp.int32, (ROW_TOKENS, ROW_TOKENS), 0)
        at_j = lax.broadcasted_iota(jnp.int32, (ROW_TOKENS, ROW_TOKENS), 1)
        hidden = (ids_i - 3.0 * pair_i == 2.0) & (ids_j - 3.0 * pair_j == 1.0)
        seen = jnp.where((at_j <= at_i) & (pair_i == pair_j), 1.0, 0.0)
        seen = jnp.where(hidden, 0.0, seen)
        vis_ref[rows, :] = seen
        angle = (jnp.sum(seen, axis=1, keepdims=True) - 1.0) * freq_ref[...]
        lane_at = lax.broadcasted_iota(jnp.int32, (ROW_TOKENS, HEAD_SIZE), 1)
        sine = jnp.sin(angle)
        cos_ref[rows, :] = jnp.cos(angle)
        sin_ref[rows, :] = jnp.where(lane_at < HEAD_SIZE // 2, -sine, sine)
        return carry

    acc[...] = jnp.zeros_like(acc)
    square[...] = jnp.zeros_like(square)

    def ramp(sub, carry):
        for j in range(1, n_dp):
            token_copy(j, sub, lax.rem(me_dp + j, n_dp)).wait_recv()
        xg[me_mp, :, token_slice(sub)] = jnp.dot(
            put_ref[...], xin[:, token_slice(sub)], preferred_element_type=jnp.float32
        ).astype(jnp.bfloat16)
        for way in range(2):
            x_copy(0, way, sub).start()

        def forward(k, c):
            for way in range(2):
                x_arrival(k, way, sub - 1 - k).wait_recv()
                x_copy(k + 1, way, sub - 1 - k).start()
            return c

        lax.fori_loop(0, jnp.minimum(sub, last - 1), forward, 0)
        lax.fori_loop(sub * rows_dev // SLICES, (sub + 1) * rows_dev // SLICES, tables, 0)
        return carry

    lax.fori_loop(0, SLICES, ramp, 0)

    for kind in range(6, base):
        send_away(kind)
    owns[3].start()
    for w in range(3):
        owns[w].wait()
    for kind in range(base):
        held_copy(kind, partner, 0).wait_recv()

    def pass_part(p):
        for kind in range(3 * p, 3 * p + 3):
            for j in range(1, groups):
                owner = lax.rem(me_dp + n_dp - 2 * j, n_dp)
                held_copy(kind, owner, 0).wait_recv()
                held_copy(kind, owner, groups + j - 1).start()

    def rest_part(p):
        for kind in range(3 * p, 3 * p + 3):
            for i in range(1, groups):
                held_copy(kind, lax.rem(partner + 2 * i, n_dp), 0).wait_recv()

    def project(way, g, u):
        halves = pl.ds(pl.multiple_of(way * half, 16), half)
        wide = xg[g, halves, pl.ds(pl.multiple_of(u * unit, 128), unit)].astype(jnp.float32)
        power = wide * wide
        total = power[:, 0:128]
        for i in range(1, unit // 128):
            total = total + power[:, i * 128:(i + 1) * 128]
        square[halves, :] += total
        start = g * chunk + u * unit
        scaled = (wide * gain_ref[:, pl.ds(pl.multiple_of(start, 128), unit)]).astype(jnp.bfloat16)
        acc[halves, :] += jnp.dot(
            scaled,
            wall[pl.ds(pl.multiple_of(start, 16), unit), :],
            preferred_element_type=jnp.float32,
        )

    def project_due(slot):
        stage = slot // 2
        newest = jnp.minimum(stage + 1, last)
        catch_up = slot == 0
        for p in range(PARTS):
            catch_up = catch_up | (slot == part_slot[p])

        def one(i, carry):
            hop = i // (2 * UNITS)
            u = lax.rem(i // 2, UNITS)
            way = lax.rem(i, 2)
            g = ring_member(place + jnp.where(way == 0, -hop, hop), n_mp)
            start = g * chunk + u * unit
            owner = start // depth
            near = (owner // 2 == group) & ((start + unit - 1) // depth // 2 == group)
            if depth % unit == 0:
                needed = jnp.int32(0)
                for p in range(1, PARTS):
                    reached = lax.rem(start + unit - 1, depth) >= part_edges[p]
                    needed = needed + jnp.where(reached, 1, 0)
            else:
                needed = PARTS - 1
            when = part_slot[PARTS - 1]
            for p in range(PARTS - 2, -1, -1):
                when = jnp.where(needed == p, part_slot[p], when)
            here = jnp.where(hop == 0, 0, 2 * (hop - 1) + u)
            here = jnp.where(here == final - 1, final, here)
            due = jnp.where(near, here, jnp.maximum(here, when))

            @pl.when(due == slot)
            def _():
                project(way, g, u)

            return carry

        lowest = jnp.where(catch_up, 0, newest)
        lax.fori_loop(lowest * 2 * UNITS, (newest + 1) * 2 * UNITS, one, 0)

    def slot_of(slot, carry):
        for p in range(PARTS):
            pl.when(slot == part_slot[p])(functools.partial(pass_part, p))
        stage = jnp.minimum(slot // 2, last - 1)
        side = jnp.where(slot == final, 1, lax.rem(slot, 2))
        for i in range(SLICES // 2):
            sub = side * (SLICES // 2) + i
            for way in range(2):
                fresh = (slot != final - 1) & ((stage + sub >= SLICES - 1) | (stage == last - 1))

                @pl.when(fresh)
                def _():
                    x_arrival(stage, way, sub).wait_recv()

                    @pl.when(stage < last - 1)
                    def _():
                        x_copy(stage + 1, way, sub).start()

        for p in range(PARTS):
            pl.when(slot == part_slot[p])(functools.partial(rest_part, p))
        project_due(slot)

        if paired:

            @pl.when((slot == 2) & urgent)
            def _():
                send_away(base)

            @pl.when(slot == 3)
            def _():
                send_partner(base)

            @pl.when(slot == min(6, final))
            def _():
                for h in range(2):
                    pl.when(inner | urgent)(functools.partial(mate_arrived, h))
                    pl.when(urgent)(functools.partial(mate_away, h))

        else:

            @pl.when(slot == min(2, final))
            def _():
                for kind in range(base, kinds):
                    send_away(kind)
                    send_partner(kind)

        return carry

    lax.fori_loop(0, final + 1, slot_of, 0)
    def turn(u, cosine, sine):
        return (u * cosine + pltpu.roll(u, HEAD_SIZE // 2, 1) * sine).astype(jnp.bfloat16)

    def share(r, side):
        ref = attn.at[
            pl.ds(pl.multiple_of(r * ROW_TOKENS, ROW_TOKENS), ROW_TOKENS),
            pl.ds(pl.multiple_of(side * q_width, 128), q_width),
        ]
        return pltpu.make_async_remote_copy(
            src_ref=ref,
            dst_ref=ref,
            send_sem=a_send.at[r],
            recv_sem=a_recv.at[r],
            device_id={"mp": mate},
            device_id_type=MESH,
        )

    def attend(r, carry):
        rows = pl.ds(pl.multiple_of(r * ROW_TOKENS, ROW_TOKENS), ROW_TOKENS)
        power = jnp.sum(square[rows, :], axis=1, keepdims=True)
        scale = lax.rsqrt(power / (n_mp * chunk) + 1e-05)
        cosine = cos_ref[rows, :] * scale
        sine = sin_ref[rows, :] * scale
        seen = vis_ref[rows, :] > 0.5
        left = at_x * q_width if paired else 0
        for kv in range(k_width // HEAD_SIZE):
            at_k = q_width + kv * HEAD_SIZE
            key = turn(acc[rows, at_k:at_k + HEAD_SIZE], cosine, sine)
            at_v = at_k + k_width
            value = (acc[rows, at_v:at_v + HEAD_SIZE] * scale).astype(jnp.bfloat16)
            heads = range(kv * QUERY_PER_KV, (kv + 1) * QUERY_PER_KV)
            queries = jnp.concatenate(
                [turn(acc[rows, h * HEAD_SIZE:(h + 1) * HEAD_SIZE], cosine, sine) for h in heads],
                axis=0,
            )
            scores = lax.dot_general(
                queries, key, (((1,), (1,)), ((), ())), preferred_element_type=jnp.float32
            ) * HEAD_SIZE ** (-0.5)
            probs = []
            for i in range(QUERY_PER_KV):
                own = scores[i * ROW_TOKENS:(i + 1) * ROW_TOKENS, :]
                own = jnp.where(seen, own, -1e30)
                expo = jnp.exp(own - jnp.max(own, axis=-1, keepdims=True))
                probs.append(
                    (expo / jnp.sum(expo, axis=-1, keepdims=True)).astype(jnp.bfloat16)
                )
            mixed = jnp.dot(
                jnp.concatenate(probs, axis=0), value, preferred_element_type=jnp.float32
            ).astype(jnp.bfloat16)
            for i, h in enumerate(heads):
                spot = pl.ds(pl.multiple_of(left + h * HEAD_SIZE, 128), HEAD_SIZE)
                attn[rows, spot] = mixed[i * ROW_TOKENS:(i + 1) * ROW_TOKENS, :]
        if paired:
            share(r, at_x).start()
        return carry

    lax.fori_loop(0, tokens // ROW_TOKENS, attend, 0)
    owns[3].wait()

    def line_copy(way, z, r):
        h = r // rows_dev
        ref = sums.at[
            way,
            z,
            pl.ds(pl.multiple_of(lax.rem(r, rows_dev) * ROW_TOKENS, ROW_TOKENS), ROW_TOKENS),
            pl.ds(pl.multiple_of(h * line_width, 128), line_width),
        ]
        ahead = jnp.clip(me_mp + 2 - 4 * way, 0, n_mp - 1)
        return pltpu.make_async_remote_copy(
            src_ref=ref,
            dst_ref=ref,
            send_sem=s_send.at[way, z, r],
            recv_sem=s_recv.at[way, z, r],
            device_id={"mp": ahead},
            device_id_type=MESH,
        )

    def need(z, pieces):
        away = z // 2 != group

        @pl.when(z == partner)
        def _():
            for piece in pieces:
                ref = pair_part(piece, z)
                weight_copy(base + piece, z, ref, ref, 0, partner).wait_recv()

        @pl.when(away & (lax.rem(z, 2) == core))
        def _():
            for piece in pieces:
                ref = pair_part(piece, z)
                weight_copy(base + piece, z, ref, ref, 0, partner).wait_recv()
                weight_copy(base + piece, z, ref, ref, groups, partner).start()

        @pl.when(away & (lax.rem(z, 2) != core))
        def _():
            for piece in pieces:
                ref = pair_part(piece, z)
                weight_copy(base + piece, z, ref, ref, 0, partner).wait_recv()

    def along_line():
        outer = jnp.logical_not(inner)
        lazy = jnp.logical_not(urgent)
        for h in range(2):
            pl.when(outer & lazy)(mate_copy(h, at_x).start)
        pl.when(lazy)(functools.partial(send_away, base))
        entries = LINE_COLUMNS * rows_dev

        units = line - 1
        ways = [jnp.int32(0)] * units
        ends = [jnp.int32(0)] * units
        tie = jnp.int32(line)
        for plane in range(groups):
            for z in range(line):
                plan = line_plan(line, plane, z)
                here = (group == plane) & (at_z == z)
                for i in range(units):
                    ways[i] = jnp.where(here, plan[0][i], ways[i])
                    ends[i] = jnp.where(here, plan[1][i], ends[i])
                tie = jnp.where(here, plan[2], tie)

        def entry(i, carry):
            @pl.when((i == entries) & lazy)
            def _():
                for h in range(2):
                    pl.when(outer)(functools.partial(mate_arrived, h))
                    mate_away(h)

            within = i - tie * entries
            mixed = (within >= 0) & (within < 2 * entries)
            u = jnp.where(mixed, tie + lax.rem(within, 2), i // entries)
            e = jnp.where(mixed, within // 2, lax.rem(i, entries))
            h = e // rows_dev
            r = lax.rem(e, rows_dev)
            own = u == units
            way = jnp.int32(0)
            z = at_z
            for k in range(units):
                way = jnp.where(u == k, ways[k], way)
                z = jnp.where(u == k, ends[k], z)
            rows = pl.ds(pl.multiple_of(r * ROW_TOKENS, ROW_TOKENS), ROW_TOKENS)

            cols = pl.ds(pl.multiple_of(h * line_width, 128), line_width)
            pl.when(e == 0)(functools.partial(need, z, (0, 1) if LINE_COLUMNS > 1 else (0, 1, 2)))
            if LINE_COLUMNS > 1:
                second = rows_dev * LINE_COLUMNS // 2
                pl.when(e == second)(functools.partial(need, z, (2,)))

            @pl.when((u == 0) & (h == 0))
            def _():
                share(r, 1 - at_x).wait_recv()

            terms[...] = jnp.dot(
                attn[rows, :],
                wo[:, pl.ds(pl.multiple_of(z * chunk + h * line_width, 128), line_width)],
                preferred_element_type=jnp.float32,
            )
            for side in range(2):
                more = at_z > 0 if side == 0 else at_z < line - 1

                @pl.when(more & (own | (way == side)))
                def _():
                    line_copy(side, z, e).wait_recv()
                    terms[...] += sums[side, z, rows, cols].astype(jnp.float32)

            @pl.when(own)
            def _():
                out_ref[rows, cols] = terms[...].astype(jnp.bfloat16)

            for side in range(2):

                @pl.when(jnp.logical_not(own) & (way == side))
                def _():
                    sums[side, z, rows, cols] = terms[...].astype(jnp.bfloat16)
                    line_copy(side, z, e).start()

            return carry

        lax.fori_loop(0, line * entries, entry, 0)

        def sent(i, carry):
            z = i // entries
            e = lax.rem(i, entries)
            pl.when(z > at_z)(line_copy(0, z, e).wait_send)
            pl.when(z < at_z)(line_copy(1, z, e).wait_send)
            return carry

        lax.fori_loop(0, line * entries, sent, 0)
        for h in range(2):
            mate_copy(h, at_x).wait_send()
        for r in range(rows_dev):
            share(r, at_x).wait_send()

    def sum_copy(slot, way, c):
        cols = pl.ds(pl.multiple_of(c * column, 128), column)
        return pltpu.make_async_remote_copy(
            src_ref=sums.at[way, slot, :, cols],
            dst_ref=sums.at[way, slot + 1, :, cols],
            send_sem=s_send.at[way, c, slot],
            recv_sem=s_recv.at[way, c, slot],
            device_id={"mp": sides[way]},
            device_id_type=MESH,
        )

    def scatter(i, carry):
        hop = i // COLUMNS + 1
        c = lax.rem(i, COLUMNS)
        cols = pl.ds(pl.multiple_of(c * column, 128), column)
        for way in range(2):
            g = ring_member(place + (-hop if way == 0 else hop), n_mp)
            terms[way] = jnp.dot(
                attn[way * half:(way + 1) * half, :],
                wo[:, pl.ds(pl.multiple_of(g * chunk + c * column, 128), column)],
                preferred_element_type=jnp.float32,
            )
        for way in range(2):

            @pl.when(hop == 1)
            def _():
                sums[way, 0, :, cols] = terms[way].astype(jnp.bfloat16)

            @pl.when(hop > 1)
            def _():
                sum_copy(hop - 2, way, c).wait_recv()
                total = sums[way, hop - 1, :, cols].astype(jnp.float32) + terms[way]
                total = total.astype(jnp.bfloat16)

                @pl.when(hop < n_mp)
                def _():
                    sums[way, hop - 1, :, cols] = total

                @pl.when(hop == n_mp)
                def _():
                    out_ref[way * half:(way + 1) * half, cols] = total

            @pl.when(hop < n_mp)
            def _():
                sum_copy(hop - 1, way, c).start()

        return carry

    def around_ring():
        for kind in range(base, kinds):
            for j in range(1, groups):
                owner = lax.rem(me_dp + n_dp - 2 * j, n_dp)
                held_copy(kind, owner, 0).wait_recv()
                held_copy(kind, owner, groups + j - 1).start()
            for i in range(groups):
                held_copy(kind, lax.rem(partner + 2 * i, n_dp), 0).wait_recv()
        lax.fori_loop(0, n_mp * COLUMNS, scatter, 0)

        def sent(step, carry):
            for way in range(2):
                for c in range(COLUMNS):
                    sum_copy(step, way, c).wait_send()
            return carry

        lax.fori_loop(0, n_mp - 1, sent, 0)

    if paired:
        along_line()
    else:
        around_ring()

    def drain(step, carry):
        for way in range(2):
            for sub in range(SLICES):
                x_copy(step, way, sub).wait_send()
        return carry

    lax.fori_loop(0, n_mp - 1, drain, 0)
    for sub in range(SLICES):
        for j in range(1, n_dp):
            token_copy(j, sub, me_dp).wait_send()
    for kind in range(kinds):
        for i in range(2 * groups - 1):
            weight_copy(kind, me_dp, shard(kind), part(kind, me_dp), i, partner).wait_send()


def local(
    pair_tokens,
    norm_gain,
    q_weight,
    k_weight,
    value_weight,
    o_weight,
    pair_row,
    pair_span,
    block_ids,
):
    dp_count = lax.axis_size("dp")
    mp_count = lax.axis_size("mp")
    pairs_dev, pair_cap, width_local = pair_tokens.shape
    slots = dp_count * (-(-pairs_dev // dp_count))
    tok_dev = block_ids.shape[0]
    half = HEAD_SIZE // 2
    freq = 500000.0 ** (-(np.arange(half, dtype=np.float32) * 2.0 / HEAD_SIZE))
    freq = np.concatenate([freq, freq])[None, :].astype(np.float32)

    q_width = q_weight.shape[1]
    k_width = k_weight.shape[1]
    width = norm_gain.shape[0]
    out_rows = o_weight.shape[0]
    if pairs_up(dp_count, mp_count, o_weight.shape[1], width_local):
        kinds = 3 * PARTS + 3
        line = mp_count // 2
        attn_shape = (tok_dev, 2 * q_width)
        wo_shape = (2 * out_rows, width // 2)
        sums_shape = (2, line, tok_dev, width_local)
        terms_shape = (ROW_TOKENS, width_local // LINE_COLUMNS)
        sum_sems = (2, line, LINE_COLUMNS * (tok_dev // ROW_TOKENS))
    else:
        kinds = 3 * PARTS + COLUMNS
        attn_shape = (tok_dev, q_width)
        wo_shape = (out_rows, width)
        sums_shape = (2, mp_count, tok_dev // 2, width_local)
        terms_shape = (2, tok_dev // 2, width_local // COLUMNS)
        sum_sems = (2, COLUMNS, mp_count - 1)
    far = dp_count - 1
    vmem = pl.BlockSpec(memory_space=pltpu.VMEM)
    smem = pl.BlockSpec(memory_space=pltpu.SMEM)
    anyspace = pl.BlockSpec(memory_space=pl.ANY)
    bf16 = jnp.bfloat16
    return pl.pallas_call(
        functools.partial(kernel, dp_count, mp_count),
        out_shape=pltpu.VMEM((tok_dev, width_local), bf16),
        in_specs=[
            smem, smem, anyspace, vmem, anyspace, anyspace, anyspace, anyspace, vmem, vmem
        ],
        out_specs=vmem,
        scratch_shapes=[
            pltpu.VMEM((pairs_dev, pair_cap, width_local), bf16),
            pltpu.VMEM((slots * pair_cap, width_local), bf16),
            pltpu.VMEM((slots * pair_cap, width_local), bf16),
            pltpu.VMEM((mp_count, tok_dev, width_local), bf16),
            pltpu.VMEM((width, q_width + 2 * k_width), bf16),
            pltpu.VMEM(wo_shape, bf16),
            pltpu.VMEM((tok_dev, q_width + 2 * k_width), jnp.float32),
            pltpu.VMEM((tok_dev, 128), jnp.float32),
            pltpu.VMEM(attn_shape, bf16),
            pltpu.VMEM(sums_shape, bf16),
            pltpu.VMEM(terms_shape, jnp.float32),
            pltpu.VMEM((tok_dev, HEAD_SIZE), jnp.float32),
            pltpu.VMEM((tok_dev, HEAD_SIZE), jnp.float32),
            pltpu.VMEM((tok_dev, ROW_TOKENS), jnp.float32),
            pltpu.VMEM((tok_dev, slots * pair_cap), bf16),
            pltpu.SMEM((slots,), jnp.int32),
            pltpu.SMEM((slots,), jnp.int32),
            pltpu.SMEM((slots,), jnp.int32),
            pltpu.SemaphoreType.DMA((5,)),
            pltpu.SemaphoreType.DMA((SLICES, far)),
            pltpu.SemaphoreType.DMA((SLICES, dp_count)),
            pltpu.SemaphoreType.DMA((kinds, far)),
            pltpu.SemaphoreType.DMA((kinds, dp_count)),
            pltpu.SemaphoreType.DMA((2, SLICES, mp_count - 1)),
            pltpu.SemaphoreType.DMA((2, SLICES, mp_count - 1)),
            pltpu.SemaphoreType.DMA(sum_sems),
            pltpu.SemaphoreType.DMA(sum_sems),
            pltpu.SemaphoreType.DMA((2,)),
            pltpu.SemaphoreType.DMA((2,)),
            pltpu.SemaphoreType.DMA((tok_dev // ROW_TOKENS,)),
            pltpu.SemaphoreType.DMA((tok_dev // ROW_TOKENS,)),
        ],
        compiler_params=pltpu.CompilerParams(
            collective_id=0, has_side_effects=True, vmem_limit_bytes=60 * 1024 * 1024
        ),
    )(
        pair_row,
        jnp.transpose(pair_span),
        pair_tokens,
        norm_gain[None, :],
        q_weight,
        k_weight,
        value_weight,
        o_weight,
        block_ids.reshape(tok_dev // ROW_TOKENS, ROW_TOKENS),
        jnp.asarray(freq),
    )


def solution(mesh):
    placed = (
        P("dp", None, "mp"),
        P(),
        P("dp", "mp"),
        P("dp", "mp"),
        P("dp", "mp"),
        P("mp", "dp"),
        P(),
        P(),
        P("dp"),
    )
    return jax.shard_map(
        local, mesh=mesh, in_specs=placed, out_specs=P("dp", "mp"), check_vma=False
    )
```

```python
import functools

import jax
import jax.numpy as jnp
import numpy as np
from jax import lax
from jax.experimental import pallas as pl
from jax.experimental.pallas import tpu as pltpu
from jax.sharding import PartitionSpec as P

HEAD_SIZE = 128
ROW_TOKENS = 128
QUERY_PER_KV = 4
SLICES = 2
PART_EDGES = (0, 2, 3, 4)
PARTS = len(PART_EDGES) - 1
COLUMNS = 4
LINE_COLUMNS = 1
UNITS = 2
MESH = pl.DeviceIdType.MESH


def ring_member(place, count):
    place = lax.rem(place + 2 * count, count)
    return jnp.where(place < count // 2, 2 * place, 2 * (count - 1 - place) + 1)


def pairs_up(n_dp, n_mp, width, chunk):
    return n_dp // 2 == 2 and n_mp == 2 * n_dp and width == 2 * chunk


def line_plan(length, group, at):
    near = (2 * group, 2 * group + 1)
    rising = list(range(length - 1, 0, -1))
    if 1 in near:
        rising = [1] + rising[:-1]
    falling = list(range(length - 1))
    if length - 2 in near:
        falling = [length - 2] + falling[:-1]
    units = [(rising.index(z), 0, z) for z in range(at + 1, length)]
    units = sorted(units + [(falling.index(z), 1, z) for z in range(at)])
    ties = [i for i in range(length - 2) if units[i][0] == units[i + 1][0]]
    return [u[1] for u in units], [u[2] for u in units], (ties + [length])[0]


def kernel(
    n_dp, n_mp,
    row_ref, span_ref, tok_ref, gain_ref, q_ref, k_ref, v_ref, o_ref, ids_ref, freq_ref,
    out_ref,
    tokv, xout, xin, xg, wall, wo, acc, square, attn, sums, terms, cos_ref, sin_ref, vis_ref,
    put_ref, pick, first_of, length_of,
    own_sem, t_send, t_recv, w_send, w_recv, x_send, x_recv, s_send, s_recv,
    b_send, b_recv, a_send, a_recv,
):
    me_dp = lax.axis_index("dp")
    me_mp = lax.axis_index("mp")

    def place_of(g):
        return jnp.where(lax.rem(g, 2) == 0, g // 2, n_mp - 1 - g // 2)

    place = place_of(me_mp)
    sides = (ring_member(place + 1, n_mp), ring_member(place - 1, n_mp))
    groups = n_dp // 2
    core = lax.rem(me_dp, 2)
    group = me_dp // 2
    partner = me_dp + 1 - 2 * core
    others = [lax.rem(me_dp + 2 * j, n_dp) for j in range(1, groups)]
    tokens, chunk = out_ref.shape
    half = tokens // 2
    rows_dev = tokens // ROW_TOKENS
    pairs_dev, cap, _ = tok_ref.shape
    most = -(-pairs_dev // n_dp)
    slots = n_dp * most
    block = most * cap
    depth, q_width = q_ref.shape
    k_width = k_ref.shape[1]
    width = o_ref.shape[1]
    paired = pairs_up(n_dp, n_mp, width, chunk)
    slice_width = chunk // SLICES
    part_edges = [depth * e // PART_EDGES[-1] for e in PART_EDGES]
    unit = chunk // UNITS
    column = chunk // COLUMNS
    out_column = width // COLUMNS
    base = 3 * PARTS
    kinds = base + (3 if paired else COLUMNS)
    out_rows = o_ref.shape[0]
    wide_half = chunk // 2
    line_width = chunk // LINE_COLUMNS
    line = n_mp // 2
    at_z = me_mp // 2
    at_x = lax.rem(me_mp, 2)
    mate = me_mp + 1 - 2 * at_x
    inner = (at_z > 0) & (at_z < line - 1)
    lead = jnp.where(at_z == 0, 1, jnp.where(at_z == line - 1, 0, group))
    urgent = core == lead
    last = n_mp - 1
    final = 2 * last
    part_slot = [min(p, final - 1) for p in (8, 11, 2 * n_mp)]

    def token_slice(sub):
        return pl.ds(pl.multiple_of(sub * slice_width, 128), slice_width)

    own_tokens = pltpu.make_async_copy(tok_ref, tokv, own_sem.at[4])
    own_tokens.start()

    barrier = pltpu.get_barrier_semaphore()
    for side in sides:
        pl.semaphore_signal(barrier, inc=1, device_id={"mp": side}, device_id_type=MESH)
    for j in range(1, n_dp):
        peer = lax.rem(me_dp + j, n_dp)
        pl.semaphore_signal(barrier, inc=1, device_id={"dp": peer}, device_id_type=MESH)

    greeted = 2 + n_dp - 1
    if paired:
        pl.semaphore_signal(barrier, inc=1, device_id={"mp": mate}, device_id_type=MESH)

        @pl.when(at_z < line - 1)
        def _():
            above = jnp.minimum(me_mp + 2, n_mp - 1)
            pl.semaphore_signal(barrier, inc=1, device_id={"mp": above}, device_id_type=MESH)

        @pl.when(at_z > 0)
        def _():
            below = jnp.maximum(me_mp - 2, 0)
            pl.semaphore_signal(barrier, inc=1, device_id={"mp": below}, device_id_type=MESH)

        greeted = greeted + 1 + jnp.where(at_z < line - 1, 1, 0) + jnp.where(at_z > 0, 1, 0)

    owner_list = [lax.div(row_ref[me_dp * pairs_dev + p], rows_dev) for p in range(pairs_dev)]
    slot_list = []
    for p in range(pairs_dev):
        rank = jnp.int32(0)
        for e in range(p):
            rank = rank + jnp.where(owner_list[e] == owner_list[p], 1, 0)
        slot_list.append(owner_list[p] * most + rank)
    for s in range(slots):
        index = jnp.int32(0)
        for p in range(1, pairs_dev):
            index = jnp.where(slot_list[p] == s, p, index)
        pick[s] = index

    pl.semaphore_wait(barrier, greeted)

    def token_rows(owner):
        return pl.ds(pl.multiple_of(owner * block, 16), block)

    def token_copy(j, sub, landing):
        peer = lax.rem(me_dp + j, n_dp)
        return pltpu.make_async_remote_copy(
            src_ref=xout.at[token_rows(peer), token_slice(sub)],
            dst_ref=xin.at[token_rows(landing), token_slice(sub)],
            send_sem=t_send.at[sub, j - 1],
            recv_sem=t_recv.at[sub, landing],
            device_id={"dp": peer},
            device_id_type=MESH,
        )

    def send_tokens(sub, carry):
        def arrange(s, c):
            rows = pl.ds(pl.multiple_of(s * cap, 16), cap)
            xout[rows, token_slice(sub)] = tokv[pick[s], :, token_slice(sub)]
            return c

        lax.fori_loop(0, slots, arrange, 0)
        for j in range(1, n_dp):
            token_copy(j, sub, me_dp).start()
        xin[token_rows(me_dp), token_slice(sub)] = xout[token_rows(me_dp), token_slice(sub)]
        return carry

    own_tokens.wait()
    lax.fori_loop(0, SLICES, send_tokens, 0)

    starts = (0, q_width, q_width + k_width)
    spans = (q_width, k_width, k_width)

    def pair_part(piece, owner):
        side = at_x if piece == 0 else 1 - at_x
        start = owner * chunk + max(piece - 1, 0) * wide_half
        return wo.at[
            pl.ds(pl.multiple_of(side * out_rows, 16), out_rows),
            pl.ds(pl.multiple_of(start, 128), chunk if piece == 0 else wide_half),
        ]

    def part(kind, owner):
        if kind >= base and paired:
            return pair_part(kind - base, owner)
        if kind >= base:
            start = owner * width + (kind - base) * out_column
            return wo.at[:, pl.ds(pl.multiple_of(start, 128), out_column)]
        p, which = divmod(kind, 3)
        start = owner * depth + part_edges[p]
        part_rows = part_edges[p + 1] - part_edges[p]
        return wall.at[
            pl.ds(pl.multiple_of(start, 16), part_rows), pl.ds(starts[which], spans[which])
        ]

    def shard(kind):
        if kind >= base and paired:
            if kind > base:
                return pair_part(kind - base, me_dp)
            return o_ref.at[:, pl.ds(pl.multiple_of(at_x * chunk, 128), chunk)]
        if kind >= base:
            return o_ref.at[:, pl.ds((kind - base) * out_column, out_column)]
        p, which = divmod(kind, 3)
        return (q_ref, k_ref, v_ref)[which].at[
            pl.ds(part_edges[p], part_edges[p + 1] - part_edges[p]), :
        ]

    def weight_copy(kind, owner, source, target, slot, peer):
        return pltpu.make_async_remote_copy(
            src_ref=source,
            dst_ref=target,
            send_sem=w_send.at[kind, slot],
            recv_sem=w_recv.at[kind, owner],
            device_id={"dp": peer},
            device_id_type=MESH,
        )

    def held_copy(kind, owner, slot):
        return weight_copy(kind, owner, part(kind, owner), part(kind, owner), slot, partner)

    def send_away(kind):
        for j, peer in enumerate(others):
            weight_copy(kind, me_dp, shard(kind), part(kind, me_dp), 1 + j, peer).start()

    def send_partner(kind):
        weight_copy(kind, me_dp, shard(kind), part(kind, me_dp), 0, partner).start()

    owns = [
        pltpu.make_async_copy(
            (q_ref, k_ref, v_ref)[w],
            wall.at[
                pl.ds(pl.multiple_of(me_dp * depth, 16), depth), pl.ds(starts[w], spans[w])
            ],
            own_sem.at[w],
        )
        for w in range(3)
    ]
    if paired:
        owns.append(pltpu.make_async_copy(shard(base), part(base, me_dp), own_sem.at[3]))
    else:
        owns.append(
            pltpu.make_async_copy(
                o_ref,
                wo.at[:, pl.ds(pl.multiple_of(me_dp * width, 128), width)],
                own_sem.at[3],
            )
        )

    def mate_copy(h, side):
        start = me_dp * chunk + h * wide_half
        taken = (1 - at_x) * chunk + h * wide_half
        return pltpu.make_async_remote_copy(
            src_ref=o_ref.at[:, pl.ds(pl.multiple_of(taken, 128), wide_half)],
            dst_ref=wo.at[
                pl.ds(pl.multiple_of(side * out_rows, 16), out_rows),
                pl.ds(pl.multiple_of(start, 128), wide_half),
            ],
            send_sem=b_send.at[h],
            recv_sem=b_recv.at[h],
            device_id={"mp": mate},
            device_id_type=MESH,
        )

    def mate_arrived(h):
        mate_copy(h, 1 - at_x).wait_recv()
        send_partner(base + 1 + h)

    def mate_away(h):
        send_away(base + 1 + h)

    if paired:
        for h in range(2):
            pl.when(inner | urgent)(mate_copy(h, at_x).start)

    for kind in range(6):
        send_away(kind)
    for w in range(3):
        owns[w].start()
    for kind in range(base):
        send_partner(kind)

    def x_copy(step, way, sub):
        sign = -1 if way == 0 else 1
        chunk_of = ring_member(place + sign * step, n_mp)
        ref = xg.at[chunk_of, pl.ds(way * half, half), token_slice(sub)]
        return pltpu.make_async_remote_copy(
            src_ref=ref,
            dst_ref=ref,
            send_sem=x_send.at[way, sub, step],
            recv_sem=x_recv.at[way, sub, step],
            device_id={"mp": sides[way]},
            device_id_type=MESH,
        )

    def x_arrival(step, way, sub):
        sign = -1 if way == 0 else 1
        chunk_of = ring_member(place + sign * (step + 1), n_mp)
        ref = xg.at[chunk_of, pl.ds(way * half, half), token_slice(sub)]
        return pltpu.make_async_remote_copy(
            src_ref=ref,
            dst_ref=ref,
            send_sem=x_send.at[way, sub, step],
            recv_sem=x_recv.at[way, sub, step],
            device_id={"mp": sides[way]},
            device_id_type=MESH,
        )

    def find_places(j, carry):
        firsts = [jnp.int32(0)] * most
        lengths = [jnp.int32(0)] * most
        found = jnp.int32(0)
        for p in range(pairs_dev):
            i = j * pairs_dev + p
            row = row_ref[i]
            begin = span_ref[0, i]
            end = span_ref[1, i]
            first = lax.rem(row, rows_dev) * ROW_TOKENS + begin
            spot = jnp.where(lax.div(row, rows_dev) == me_dp, found, most)
            for k in range(most):
                firsts[k] = jnp.where(spot == k, first, firsts[k])
                lengths[k] = jnp.where(spot == k, end - begin, lengths[k])
            found = jnp.where(spot == most, found, found + 1)
        for k in range(most):
            first_of[j * most + k] = firsts[k]
            length_of[j * most + k] = lengths[k]
        return carry

    lax.fori_loop(0, n_dp, find_places, 0)
    lane = lax.broadcasted_iota(jnp.int32, (1, slots * cap), 1)
    target = jnp.full((1, slots * cap), tokens, jnp.int32)
    for s in range(slots):
        offset = lane - s * cap
        inside = (offset >= 0) & (offset < length_of[s])
        target = jnp.where(inside, offset + first_of[s], target)
    at = lax.broadcasted_iota(jnp.int32, (tokens, slots * cap), 0)
    put_ref[...] = jnp.where(at == target, 1.0, 0.0).astype(jnp.bfloat16)

    def tables(r, carry):
        rows = pl.ds(pl.multiple_of(r * ROW_TOKENS, ROW_TOKENS), ROW_TOKENS)
        ids_j = jnp.broadcast_to(ids_ref[pl.ds(r, 1), :], (ROW_TOKENS, ROW_TOKENS)).astype(
            jnp.float32
        )
        ids_i = jnp.transpose(ids_j)
        pair_i = jnp.floor((ids_i + 0.5) * (1.0 / 3.0))
        pair_j = jnp.floor((ids_j + 0.5) * (1.0 / 3.0))
        at_i = lax.broadcasted_iota(jnp.int32, (ROW_TOKENS, ROW_TOKENS), 0)
        at_j = lax.broadcasted_iota(jnp.int32, (ROW_TOKENS, ROW_TOKENS), 1)
        hidden = (ids_i - 3.0 * pair_i == 2.0) & (ids_j - 3.0 * pair_j == 1.0)
        seen = jnp.where((at_j <= at_i) & (pair_i == pair_j), 1.0, 0.0)
        seen = jnp.where(hidden, 0.0, seen)
        vis_ref[rows, :] = seen
        angle = (jnp.sum(seen, axis=1, keepdims=True) - 1.0) * freq_ref[...]
        lane_at = lax.broadcasted_iota(jnp.int32, (ROW_TOKENS, HEAD_SIZE), 1)
        sine = jnp.sin(angle)
        cos_ref[rows, :] = jnp.cos(angle)
        sin_ref[rows, :] = jnp.where(lane_at < HEAD_SIZE // 2, -sine, sine)
        return carry

    acc[...] = jnp.zeros_like(acc)
    square[...] = jnp.zeros_like(square)

    def ramp(sub, carry):
        for j in range(1, n_dp):
            token_copy(j, sub, lax.rem(me_dp + j, n_dp)).wait_recv()
        xg[me_mp, :, token_slice(sub)] = jnp.dot(
            put_ref[...], xin[:, token_slice(sub)], preferred_element_type=jnp.float32
        ).astype(jnp.bfloat16)
        for way in range(2):
            x_copy(0, way, sub).start()

        def forward(k, c):
            for way in range(2):
                x_arrival(k, way, sub - 1 - k).wait_recv()
                x_copy(k + 1, way, sub - 1 - k).start()
            return c

        lax.fori_loop(0, jnp.minimum(sub, last - 1), forward, 0)
        lax.fori_loop(sub * rows_dev // SLICES, (sub + 1) * rows_dev // SLICES, tables, 0)
        return carry

    lax.fori_loop(0, SLICES, ramp, 0)

    for kind in range(6, base):
        send_away(kind)
    owns[3].start()
    for w in range(3):
        owns[w].wait()
    for kind in range(base):
        held_copy(kind, partner, 0).wait_recv()

    def pass_part(p):
        for kind in range(3 * p, 3 * p + 3):
            for j in range(1, groups):
                owner = lax.rem(me_dp + n_dp - 2 * j, n_dp)
                held_copy(kind, owner, 0).wait_recv()
                held_copy(kind, owner, groups + j - 1).start()

    def rest_part(p):
        for kind in range(3 * p, 3 * p + 3):
            for i in range(1, groups):
                held_copy(kind, lax.rem(partner + 2 * i, n_dp), 0).wait_recv()

    def project(way, g, u):
        halves = pl.ds(pl.multiple_of(way * half, 16), half)
        wide = xg[g, halves, pl.ds(pl.multiple_of(u * unit, 128), unit)].astype(jnp.float32)
        power = wide * wide
        total = power[:, 0:128]
        for i in range(1, unit // 128):
            total = total + power[:, i * 128:(i + 1) * 128]
        square[halves, :] += total
        start = g * chunk + u * unit
        scaled = (wide * gain_ref[:, pl.ds(pl.multiple_of(start, 128), unit)]).astype(jnp.bfloat16)
        acc[halves, :] += jnp.dot(
            scaled,
            wall[pl.ds(pl.multiple_of(start, 16), unit), :],
            preferred_element_type=jnp.float32,
        )

    def project_due(slot):
        stage = slot // 2
        newest = jnp.minimum(stage + 1, last)
        catch_up = slot == 0
        for p in range(PARTS):
            catch_up = catch_up | (slot == part_slot[p])

        def one(i, carry):
            hop = i // (2 * UNITS)
            u = lax.rem(i // 2, UNITS)
            way = lax.rem(i, 2)
            g = ring_member(place + jnp.where(way == 0, -hop, hop), n_mp)
            start = g * chunk + u * unit
            owner = start // depth
            near = (owner // 2 == group) & ((start + unit - 1) // depth // 2 == group)
            if depth % unit == 0:
                needed = jnp.int32(0)
                for p in range(1, PARTS):
                    reached = lax.rem(start + unit - 1, depth) >= part_edges[p]
                    needed = needed + jnp.where(reached, 1, 0)
            else:
                needed = PARTS - 1
            when = part_slot[PARTS - 1]
            for p in range(PARTS - 2, -1, -1):
                when = jnp.where(needed == p, part_slot[p], when)
            here = jnp.where(hop == 0, 0, 2 * (hop - 1) + u)
            here = jnp.where(here == final - 1, final, here)
            due = jnp.where(near, here, jnp.maximum(here, when))

            @pl.when(due == slot)
            def _():
                project(way, g, u)

            return carry

        lowest = jnp.where(catch_up, 0, newest)
        lax.fori_loop(lowest * 2 * UNITS, (newest + 1) * 2 * UNITS, one, 0)

    def slot_of(slot, carry):
        for p in range(PARTS):
            pl.when(slot == part_slot[p])(functools.partial(pass_part, p))
        stage = jnp.minimum(slot // 2, last - 1)
        side = jnp.where(slot == final, 1, lax.rem(slot, 2))
        for i in range(SLICES // 2):
            sub = side * (SLICES // 2) + i
            for way in range(2):
                fresh = (slot != final - 1) & ((stage + sub >= SLICES - 1) | (stage == last - 1))

                @pl.when(fresh)
                def _():
                    x_arrival(stage, way, sub).wait_recv()

                    @pl.when(stage < last - 1)
                    def _():
                        x_copy(stage + 1, way, sub).start()

        for p in range(PARTS):
            pl.when(slot == part_slot[p])(functools.partial(rest_part, p))
        project_due(slot)

        if paired:

            @pl.when((slot == 2) & urgent)
            def _():
                send_away(base)

            @pl.when(slot == 3)
            def _():
                send_partner(base)

            @pl.when(slot == min(6, final))
            def _():
                for h in range(2):
                    pl.when(inner | urgent)(functools.partial(mate_arrived, h))
                    pl.when(urgent)(functools.partial(mate_away, h))

        else:

            @pl.when(slot == min(2, final))
            def _():
                for kind in range(base, kinds):
                    send_away(kind)
                    send_partner(kind)

        return carry

    lax.fori_loop(0, final + 1, slot_of, 0)
    def turn(u, cosine, sine):
        return (u * cosine + pltpu.roll(u, HEAD_SIZE // 2, 1) * sine).astype(jnp.bfloat16)

    def share(r, side):
        ref = attn.at[
            pl.ds(pl.multiple_of(r * ROW_TOKENS, ROW_TOKENS), ROW_TOKENS),
            pl.ds(pl.multiple_of(side * q_width, 128), q_width),
        ]
        return pltpu.make_async_remote_copy(
            src_ref=ref,
            dst_ref=ref,
            send_sem=a_send.at[r],
            recv_sem=a_recv.at[r],
            device_id={"mp": mate},
            device_id_type=MESH,
        )

    def mix(r):
        found = []
        rows = pl.ds(pl.multiple_of(r * ROW_TOKENS, ROW_TOKENS), ROW_TOKENS)
        power = jnp.sum(square[rows, :], axis=1, keepdims=True)
        scale = lax.rsqrt(power / (n_mp * chunk) + 1e-05)
        cosine = cos_ref[rows, :] * scale
        sine = sin_ref[rows, :] * scale
        seen = vis_ref[rows, :] > 0.5
        left = at_x * q_width if paired else 0
        for kv in range(k_width // HEAD_SIZE):
            at_k = q_width + kv * HEAD_SIZE
            key = turn(acc[rows, at_k:at_k + HEAD_SIZE], cosine, sine)
            at_v = at_k + k_width
            value = (acc[rows, at_v:at_v + HEAD_SIZE] * scale).astype(jnp.bfloat16)
            heads = range(kv * QUERY_PER_KV, (kv + 1) * QUERY_PER_KV)
            queries = jnp.concatenate(
                [turn(acc[rows, h * HEAD_SIZE:(h + 1) * HEAD_SIZE], cosine, sine) for h in heads],
                axis=0,
            )
            scores = lax.dot_general(
                queries, key, (((1,), (1,)), ((), ())), preferred_element_type=jnp.float32
            ) * HEAD_SIZE ** (-0.5)
            probs = []
            for i in range(QUERY_PER_KV):
                own = scores[i * ROW_TOKENS:(i + 1) * ROW_TOKENS, :]
                own = jnp.where(seen, own, -1e30)
                expo = jnp.exp(own - jnp.max(own, axis=-1, keepdims=True))
                probs.append(
                    (expo / jnp.sum(expo, axis=-1, keepdims=True)).astype(jnp.bfloat16)
                )
            mixed = jnp.dot(
                jnp.concatenate(probs, axis=0), value, preferred_element_type=jnp.float32
            ).astype(jnp.bfloat16)
            for i, h in enumerate(heads):
                found.append((left + h * HEAD_SIZE, mixed[i * ROW_TOKENS:(i + 1) * ROW_TOKENS, :]))
        return rows, found

    def attend(t, carry):
        both = [2 * t, 2 * t + 1]
        results = [mix(r) for r in both]
        for r, (rows, found) in zip(both, results):
            for start, value in found:
                attn[rows, pl.ds(pl.multiple_of(start, 128), HEAD_SIZE)] = value
            if paired:
                share(r, at_x).start()
        return carry

    lax.fori_loop(0, rows_dev // 2, attend, 0)
    owns[3].wait()

    def line_copy(way, z, r):
        h = r // rows_dev
        ref = sums.at[
            way,
            z,
            pl.ds(pl.multiple_of(lax.rem(r, rows_dev) * ROW_TOKENS, ROW_TOKENS), ROW_TOKENS),
            pl.ds(pl.multiple_of(h * line_width, 128), line_width),
        ]
        ahead = jnp.clip(me_mp + 2 - 4 * way, 0, n_mp - 1)
        return pltpu.make_async_remote_copy(
            src_ref=ref,
            dst_ref=ref,
            send_sem=s_send.at[way, z, r],
            recv_sem=s_recv.at[way, z, r],
            device_id={"mp": ahead},
            device_id_type=MESH,
        )

    def need(z, pieces):
        away = z // 2 != group

        @pl.when(z == partner)
        def _():
            for piece in pieces:
                ref = pair_part(piece, z)
                weight_copy(base + piece, z, ref, ref, 0, partner).wait_recv()

        @pl.when(away & (lax.rem(z, 2) == core))
        def _():
            for piece in pieces:
                ref = pair_part(piece, z)
                weight_copy(base + piece, z, ref, ref, 0, partner).wait_recv()
                weight_copy(base + piece, z, ref, ref, groups, partner).start()

        @pl.when(away & (lax.rem(z, 2) != core))
        def _():
            for piece in pieces:
                ref = pair_part(piece, z)
                weight_copy(base + piece, z, ref, ref, 0, partner).wait_recv()

    def along_line():
        outer = jnp.logical_not(inner)
        lazy = jnp.logical_not(urgent)
        for h in range(2):
            pl.when(outer & lazy)(mate_copy(h, at_x).start)
        pl.when(lazy)(functools.partial(send_away, base))
        entries = LINE_COLUMNS * rows_dev

        units = line - 1
        ways = [jnp.int32(0)] * units
        ends = [jnp.int32(0)] * units
        tie = jnp.int32(line)
        for plane in range(groups):
            for z in range(line):
                plan = line_plan(line, plane, z)
                here = (group == plane) & (at_z == z)
                for i in range(units):
                    ways[i] = jnp.where(here, plan[0][i], ways[i])
                    ends[i] = jnp.where(here, plan[1][i], ends[i])
                tie = jnp.where(here, plan[2], tie)

        def entry(i, carry):
            @pl.when((i == entries) & lazy)
            def _():
                for h in range(2):
                    pl.when(outer)(functools.partial(mate_arrived, h))
                    mate_away(h)

            within = i - tie * entries
            mixed = (within >= 0) & (within < 2 * entries)
            u = jnp.where(mixed, tie + lax.rem(within, 2), i // entries)
            e = jnp.where(mixed, within // 2, lax.rem(i, entries))
            h = e // rows_dev
            r = lax.rem(e, rows_dev)
            own = u == units
            way = jnp.int32(0)
            z = at_z
            for k in range(units):
                way = jnp.where(u == k, ways[k], way)
                z = jnp.where(u == k, ends[k], z)
            rows = pl.ds(pl.multiple_of(r * ROW_TOKENS, ROW_TOKENS), ROW_TOKENS)

            cols = pl.ds(pl.multiple_of(h * line_width, 128), line_width)
            pl.when(e == 0)(functools.partial(need, z, (0, 1) if LINE_COLUMNS > 1 else (0, 1, 2)))
            if LINE_COLUMNS > 1:
                second = rows_dev * LINE_COLUMNS // 2
                pl.when(e == second)(functools.partial(need, z, (2,)))

            @pl.when((u == 0) & (h == 0))
            def _():
                share(r, 1 - at_x).wait_recv()

            terms[...] = jnp.dot(
                attn[rows, :],
                wo[:, pl.ds(pl.multiple_of(z * chunk + h * line_width, 128), line_width)],
                preferred_element_type=jnp.float32,
            )
            for side in range(2):
                more = at_z > 0 if side == 0 else at_z < line - 1

                @pl.when(more & (own | (way == side)))
                def _():
                    line_copy(side, z, e).wait_recv()
                    terms[...] += sums[side, z, rows, cols].astype(jnp.float32)

            @pl.when(own)
            def _():
                out_ref[rows, cols] = terms[...].astype(jnp.bfloat16)

            for side in range(2):

                @pl.when(jnp.logical_not(own) & (way == side))
                def _():
                    sums[side, z, rows, cols] = terms[...].astype(jnp.bfloat16)
                    line_copy(side, z, e).start()

            return carry

        lax.fori_loop(0, line * entries, entry, 0)

        def sent(i, carry):
            z = i // entries
            e = lax.rem(i, entries)
            pl.when(z > at_z)(line_copy(0, z, e).wait_send)
            pl.when(z < at_z)(line_copy(1, z, e).wait_send)
            return carry

        lax.fori_loop(0, line * entries, sent, 0)
        for h in range(2):
            mate_copy(h, at_x).wait_send()
        for r in range(rows_dev):
            share(r, at_x).wait_send()

    def sum_copy(slot, way, c):
        cols = pl.ds(pl.multiple_of(c * column, 128), column)
        return pltpu.make_async_remote_copy(
            src_ref=sums.at[way, slot, :, cols],
            dst_ref=sums.at[way, slot + 1, :, cols],
            send_sem=s_send.at[way, c, slot],
            recv_sem=s_recv.at[way, c, slot],
            device_id={"mp": sides[way]},
            device_id_type=MESH,
        )

    def scatter(i, carry):
        hop = i // COLUMNS + 1
        c = lax.rem(i, COLUMNS)
        cols = pl.ds(pl.multiple_of(c * column, 128), column)
        for way in range(2):
            g = ring_member(place + (-hop if way == 0 else hop), n_mp)
            terms[way] = jnp.dot(
                attn[way * half:(way + 1) * half, :],
                wo[:, pl.ds(pl.multiple_of(g * chunk + c * column, 128), column)],
                preferred_element_type=jnp.float32,
            )
        for way in range(2):

            @pl.when(hop == 1)
            def _():
                sums[way, 0, :, cols] = terms[way].astype(jnp.bfloat16)

            @pl.when(hop > 1)
            def _():
                sum_copy(hop - 2, way, c).wait_recv()
                total = sums[way, hop - 1, :, cols].astype(jnp.float32) + terms[way]
                total = total.astype(jnp.bfloat16)

                @pl.when(hop < n_mp)
                def _():
                    sums[way, hop - 1, :, cols] = total

                @pl.when(hop == n_mp)
                def _():
                    out_ref[way * half:(way + 1) * half, cols] = total

            @pl.when(hop < n_mp)
            def _():
                sum_copy(hop - 1, way, c).start()

        return carry

    def around_ring():
        for kind in range(base, kinds):
            for j in range(1, groups):
                owner = lax.rem(me_dp + n_dp - 2 * j, n_dp)
                held_copy(kind, owner, 0).wait_recv()
                held_copy(kind, owner, groups + j - 1).start()
            for i in range(groups):
                held_copy(kind, lax.rem(partner + 2 * i, n_dp), 0).wait_recv()
        lax.fori_loop(0, n_mp * COLUMNS, scatter, 0)

        def sent(step, carry):
            for way in range(2):
                for c in range(COLUMNS):
                    sum_copy(step, way, c).wait_send()
            return carry

        lax.fori_loop(0, n_mp - 1, sent, 0)

    if paired:
        along_line()
    else:
        around_ring()

    def drain(step, carry):
        for way in range(2):
            for sub in range(SLICES):
                x_copy(step, way, sub).wait_send()
        return carry

    lax.fori_loop(0, n_mp - 1, drain, 0)
    for sub in range(SLICES):
        for j in range(1, n_dp):
            token_copy(j, sub, me_dp).wait_send()
    for kind in range(kinds):
        for i in range(2 * groups - 1):
            weight_copy(kind, me_dp, shard(kind), part(kind, me_dp), i, partner).wait_send()


def local(
    pair_tokens,
    norm_gain,
    q_weight,
    k_weight,
    value_weight,
    o_weight,
    pair_row,
    pair_span,
    block_ids,
):
    dp_count = lax.axis_size("dp")
    mp_count = lax.axis_size("mp")
    pairs_dev, pair_cap, width_local = pair_tokens.shape
    slots = dp_count * (-(-pairs_dev // dp_count))
    tok_dev = block_ids.shape[0]
    half = HEAD_SIZE // 2
    freq = 500000.0 ** (-(np.arange(half, dtype=np.float32) * 2.0 / HEAD_SIZE))
    freq = np.concatenate([freq, freq])[None, :].astype(np.float32)

    q_width = q_weight.shape[1]
    k_width = k_weight.shape[1]
    width = norm_gain.shape[0]
    out_rows = o_weight.shape[0]
    if pairs_up(dp_count, mp_count, o_weight.shape[1], width_local):
        kinds = 3 * PARTS + 3
        line = mp_count // 2
        attn_shape = (tok_dev, 2 * q_width)
        wo_shape = (2 * out_rows, width // 2)
        sums_shape = (2, line, tok_dev, width_local)
        terms_shape = (ROW_TOKENS, width_local // LINE_COLUMNS)
        sum_sems = (2, line, LINE_COLUMNS * (tok_dev // ROW_TOKENS))
    else:
        kinds = 3 * PARTS + COLUMNS
        attn_shape = (tok_dev, q_width)
        wo_shape = (out_rows, width)
        sums_shape = (2, mp_count, tok_dev // 2, width_local)
        terms_shape = (2, tok_dev // 2, width_local // COLUMNS)
        sum_sems = (2, COLUMNS, mp_count - 1)
    far = dp_count - 1
    vmem = pl.BlockSpec(memory_space=pltpu.VMEM)
    smem = pl.BlockSpec(memory_space=pltpu.SMEM)
    anyspace = pl.BlockSpec(memory_space=pl.ANY)
    bf16 = jnp.bfloat16
    return pl.pallas_call(
        functools.partial(kernel, dp_count, mp_count),
        out_shape=pltpu.VMEM((tok_dev, width_local), bf16),
        in_specs=[
            smem, smem, anyspace, vmem, anyspace, anyspace, anyspace, anyspace, vmem, vmem
        ],
        out_specs=vmem,
        scratch_shapes=[
            pltpu.VMEM((pairs_dev, pair_cap, width_local), bf16),
            pltpu.VMEM((slots * pair_cap, width_local), bf16),
            pltpu.VMEM((slots * pair_cap, width_local), bf16),
            pltpu.VMEM((mp_count, tok_dev, width_local), bf16),
            pltpu.VMEM((width, q_width + 2 * k_width), bf16),
            pltpu.VMEM(wo_shape, bf16),
            pltpu.VMEM((tok_dev, q_width + 2 * k_width), jnp.float32),
            pltpu.VMEM((tok_dev, 128), jnp.float32),
            pltpu.VMEM(attn_shape, bf16),
            pltpu.VMEM(sums_shape, bf16),
            pltpu.VMEM(terms_shape, jnp.float32),
            pltpu.VMEM((tok_dev, HEAD_SIZE), jnp.float32),
            pltpu.VMEM((tok_dev, HEAD_SIZE), jnp.float32),
            pltpu.VMEM((tok_dev, ROW_TOKENS), jnp.float32),
            pltpu.VMEM((tok_dev, slots * pair_cap), bf16),
            pltpu.SMEM((slots,), jnp.int32),
            pltpu.SMEM((slots,), jnp.int32),
            pltpu.SMEM((slots,), jnp.int32),
            pltpu.SemaphoreType.DMA((5,)),
            pltpu.SemaphoreType.DMA((SLICES, far)),
            pltpu.SemaphoreType.DMA((SLICES, dp_count)),
            pltpu.SemaphoreType.DMA((kinds, far)),
            pltpu.SemaphoreType.DMA((kinds, dp_count)),
            pltpu.SemaphoreType.DMA((2, SLICES, mp_count - 1)),
            pltpu.SemaphoreType.DMA((2, SLICES, mp_count - 1)),
            pltpu.SemaphoreType.DMA(sum_sems),
            pltpu.SemaphoreType.DMA(sum_sems),
            pltpu.SemaphoreType.DMA((2,)),
            pltpu.SemaphoreType.DMA((2,)),
            pltpu.SemaphoreType.DMA((tok_dev // ROW_TOKENS,)),
            pltpu.SemaphoreType.DMA((tok_dev // ROW_TOKENS,)),
        ],
        compiler_params=pltpu.CompilerParams(
            collective_id=0, has_side_effects=True, vmem_limit_bytes=60 * 1024 * 1024
        ),
    )(
        pair_row,
        jnp.transpose(pair_span),
        pair_tokens,
        norm_gain[None, :],
        q_weight,
        k_weight,
        value_weight,
        o_weight,
        block_ids.reshape(tok_dev // ROW_TOKENS, ROW_TOKENS),
        jnp.asarray(freq),
    )


def solution(mesh):
    placed = (
        P("dp", None, "mp"),
        P(),
        P("dp", "mp"),
        P("dp", "mp"),
        P("dp", "mp"),
        P("mp", "dp"),
        P(),
        P(),
        P("dp"),
    )
    return jax.shard_map(
        local, mesh=mesh, in_specs=placed, out_specs=P("dp", "mp"), check_vma=False
    )
```
